32 devices in a mesh: shard: 4 (over x, core), ctx: 2 (over y), tp: 4 (over z).
Axes of the slice: x: 2, y: 2, z: 4, core: 2. Of those that a mesh axis runs over, the one named last changes fastest.
Arguments:
- tokens: bfloat16 [1024, 16, 1024], P(('ctx', 'tp'), 'shard'), may hold values from -6 to 6
- segments: int32 [16, 1024], P('shard'), may hold values from 0 to 1, never falling along the last dimension, each value on 1 to 800 neighbouring positions
- encoder: bfloat16 [384, 16, 1024], P(None, 'shard'), may hold values from -6 to 6
- norm_self: float32 [1024], replicated, may hold values from 0.5 to 1.5
- norm_cross: float32 [1024], replicated, may hold values from 0.5 to 1.5
- norm_ffn: float32 [1024], replicated, may hold values from 0.5 to 1.5
- rel_table: float32 [32, 16], P(None, 'tp'), may hold values from -4 to 4
- self_query: bfloat16 [1024, 1024], P(('shard', 'ctx'), 'tp'), may hold values from -0.09375 to 0.09375
- self_key: bfloat16 [1024, 1024], P(('shard', 'ctx'), 'tp'), may hold values from -0.09375 to 0.09375
- self_value: bfloat16 [1024, 1024], P(('shard', 'ctx'), 'tp'), may hold values from -0.1875 to 0.1875
- self_out: bfloat16 [1024, 1024], P('tp', ('shard', 'ctx')), may hold values from -1 to 1
- cross_query: bfloat16 [1024, 1024], P(('shard', 'ctx'), 'tp'), may hold values from -0.09375 to 0.09375
- cross_key: bfloat16 [1024, 1024], P(('shard', 'ctx'), 'tp'), may hold values from -0.09375 to 0.09375
- cross_value: bfloat16 [1024, 1024], P(('shard', 'ctx'), 'tp'), may hold values from -0.1875 to 0.1875
- cross_out: bfloat16 [1024, 1024], P('tp', ('shard', 'ctx')), may hold values from -1 to 1
- ffn_gate: bfloat16 [1024, 2816], P(('shard', 'ctx'), 'tp'), may hold values from -0.1875 to 0.1875
- ffn_up: bfloat16 [1024, 2816], P(('shard', 'ctx'), 'tp'), may hold values from -0.1875 to 0.1875
- ffn_down: bfloat16 [2816, 1024], P('tp', ('shard', 'ctx')), may hold values from -0.109375 to 0.109375
- cotangent: bfloat16 [1024, 16, 1024], P(('ctx', 'tp'), 'shard'), may hold values from -6 to 6
Outputs:
- result: bfloat16 [1024, 16, 1024], P(('ctx', 'tp'), 'shard')
- tokens_grad: float32 [1024, 16, 1024], P(('ctx', 'tp'), 'shard')
- encoder_grad: float32 [384, 16, 1024], P('ctx', 'shard', 'tp')
- norm_self_grad: float32 [1024], replicated
- norm_cross_grad: float32 [1024], replicated
- norm_ffn_grad: float32 [1024], replicated
- rel_table_grad: float32 [32, 16], P(('shard', 'ctx'), 'tp')
- self_query_grad: float32 [1024, 1024], P(('shard', 'ctx'), 'tp')
- self_key_grad: float32 [1024, 1024], P(('shard', 'ctx'), 'tp')
- self_value_grad: float32 [1024, 1024], P(('shard', 'ctx'), 'tp')
- self_out_grad: float32 [1024, 1024], P('tp', ('shard', 'ctx'))
- cross_query_grad: float32 [1024, 1024], P(('shard', 'ctx'), 'tp')
- cross_key_grad: float32 [1024, 1024], P(('shard', 'ctx'), 'tp')
- cross_value_grad: float32 [1024, 1024], P(('shard', 'ctx'), 'tp')
- cross_out_grad: float32 [1024, 1024], P('tp', ('shard', 'ctx'))
- ffn_gate_grad: float32 [1024, 2816], P(('shard', 'ctx'), 'tp')
- ffn_up_grad: float32 [1024, 2816], P(('shard', 'ctx'), 'tp')
- feedforward_down_gradient: float32 [2816, 1024], P('tp', ('shard', 'ctx'))
The draws below stay inside these ranges and needn't reach their ends.
Inputs may be any that keep to these rules, and one draw needn't show every extreme that they name: `segments`: within each sequence the document numbers never fall; every document holds 1 to 800 tokens.
All inputs are finite; a program needn't handle non-finite values.
Results may differ from the reference program's by a relative error of at most 0.028.
The reference program's roundings to bfloat16 on the way count: a program that leaves them out, or rounds other values in their place, can miss the bound.
Values may be sent and summed in bfloat16 or wider, within the bound.
No kernel may reach another device: no remote copies, remote signals or barrier semaphores. Data moves between devices by JAX's collectives and lax.ppermute only.
A program may use at most 320 MiB of HBM per device.

```python
import math
from functools import reduce
import jax
import jax.numpy as jnp
import numpy as np
from jax import lax

D = 1024
H = 16
E = 64
FF = 2816
NB = 32
R = 384
MOST = 800
L = 1024
B = 16
DOCS = 2


def block_scale(key, dims, split, low, high):
    loudness, own = 1.0, jax.random.fold_in(key, 6)
    for axis_at, parts in split:
        draws = jnp.exp(jax.random.uniform(jax.random.fold_in(own, axis_at), (parts,), jnp.float32, low / len(split), high / len(split)))
        loudness = loudness * jnp.repeat(draws, dims[axis_at] // parts).reshape([-1 if axis == axis_at else 1 for axis in range(len(dims))])
    return loudness


def profile(amount, total, bound, lean):
    weights = [(1 << 20) // math.isqrt(grade ** lean) + 1 for grade in range(2, amount + 1)]
    surplus, given = total - bound - (amount - 1), [1] * (amount - 1)
    while surplus > 0:
        movable = [i for i in range(amount - 1) if given[i] < bound]
        whole, remaining = sum([weights[i] for i in movable]), surplus
        for i in movable:
            more = min(bound - given[i], max(1, remaining * weights[i] // whole), surplus)
            given[i] = given[i] + more
            surplus = surplus - more
    return np.array([bound] + given)


def ragged_sizes(own_key, count, total, most, skew):
    if count == 2:
        one = jax.random.randint(own_key, (), max(1, total - most), min(most, total - 1) + 1)
        return jnp.stack([one, total - one])
    tallies = jnp.asarray(profile(count, total, most, skew), jnp.int32)
    couples = (count - 1) // 2
    source_of, taker = tallies[1:1 + 2 * couples:2], tallies[2:2 + 2 * couples:2]
    room = jnp.minimum(source_of - 1, most - taker)
    shifted = jax.random.randint(jax.random.fold_in(own_key, 1), (couples,), 0, 1 << 20) % (room + 1)
    tallies = tallies.at[1:1 + 2 * couples:2].set(source_of - shifted).at[2:2 + 2 * couples:2].set(taker + shifted)
    return tallies[jax.random.permutation(jax.random.fold_in(own_key, 2), count)]


def normal_values(key, extent, spread, limit, shards=(), kind=jnp.bfloat16):
    drawn = spread * jax.random.normal(key, extent, jnp.float32)
    if shards:
        drawn = drawn * block_scale(key, extent, shards, -0.22, 0.18)
    return jnp.clip(drawn, -limit, limit).astype(kind)


def setup_inputs(seed: int = 0) -> dict:
    keys = jax.random.split(jax.random.key(seed), 20)
    tokens = normal_values(keys[0], (L, B, D), 1.0, 6.0, ((0, 8), (1, 4)))
    segments = jax.vmap(lambda own: jnp.searchsorted(jnp.cumsum(ragged_sizes(own, DOCS, L, MOST, 0)), jnp.arange(L), side="right"))(jax.random.split(keys[1], B)).reshape((B, L)).astype(jnp.int32)
    encoder = normal_values(keys[2], (R, B, D), 1.0, 6.0, ((1, 4),))
    norm_self = jnp.clip(1.0 + 0.1 * jax.random.normal(keys[3], (D,), jnp.float32), 0.5, 1.5)
    norm_cross = jnp.clip(1.0 + 0.1 * jax.random.normal(keys[4], (D,), jnp.float32), 0.5, 1.5)
    norm_ffn = jnp.clip(1.0 + 0.1 * jax.random.normal(keys[5], (D,), jnp.float32), 0.5, 1.5)
    rel_table = normal_values(keys[6], (NB, H), 1.0, 4.0, ((1, 4),), jnp.float32)
    self_query = normal_values(keys[7], (D, H * E), (4 * D) ** -0.5, 0.09375, ((0, 8), (1, 4)))
    self_key = normal_values(keys[8], (D, H * E), (4 * D) ** -0.5, 0.09375, ((0, 8), (1, 4)))
    self_value = normal_values(keys[9], (D, H * E), D ** -0.5, 0.1875, ((0, 8), (1, 4)))
    self_out = normal_values(keys[10], (H * E, D), (H * E // 32) ** -0.5, 1.0, ((0, 4), (1, 8)))
    cross_query = normal_values(keys[11], (D, H * E), (4 * D) ** -0.5, 0.09375, ((0, 8), (1, 4)))
    cross_key = normal_values(keys[12], (D, H * E), (4 * D) ** -0.5, 0.09375, ((0, 8), (1, 4)))
    cross_value = normal_values(keys[13], (D, H * E), D ** -0.5, 0.1875, ((0, 8), (1, 4)))
    cross_out = normal_values(keys[14], (H * E, D), (H * E // 32) ** -0.5, 1.0, ((0, 4), (1, 8)))
    ffn_gate = normal_values(keys[15], (D, FF), D ** -0.5, 0.1875, ((0, 8), (1, 4)))
    ffn_up = normal_values(keys[16], (D, FF), D ** -0.5, 0.1875, ((0, 8), (1, 4)))
    ffn_down = normal_values(keys[17], (FF, D), FF ** -0.5, 0.109375, ((0, 4), (1, 8)))
    cotangent = normal_values(keys[18], (L, B, D), 1.0, 6.0, ((0, 8), (1, 4)))
    return {"tokens": tokens, "segments": segments, "encoder": encoder, "norm_self": norm_self, "norm_cross": norm_cross, "norm_ffn": norm_ffn, "rel_table": rel_table, "self_query": self_query, "self_key": self_key, "self_value": self_value, "self_out": self_out, "cross_query": cross_query, "cross_key": cross_key, "cross_value": cross_value, "cross_out": cross_out, "ffn_gate": ffn_gate, "ffn_up": ffn_up, "ffn_down": ffn_down, "cotangent": cotangent}


epsilon = 1e-06
masked_score = -1000000000.0
bucket_edges = (19, 21, 24, 27, 31, 35, 40, 46, 52, 59, 67, 77, 87, 99, 113)

@jax.custom_vjp
def low(v):
    return lax.optimization_barrier(v.astype(jnp.bfloat16)).astype(jnp.float32)

@jax.custom_vjp
def low_back(v):
    return v

def low_keep(v):
    return (low(v), None)

def low_pass(kept, grad):
    return (grad,)

def back_keep(v):
    return (v, None)

def back_low(kept, grad):
    return (low(grad),)
low.defvjp(low_keep, low_pass)
low_back.defvjp(back_keep, back_low)

def bucket_index(distance):
    distance = jnp.maximum(distance, 0)
    far_bucket = reduce(lambda running, threshold: running + (distance >= threshold).astype(jnp.int32), bucket_edges, jnp.full(distance.shape, 16, jnp.int32))
    return jnp.where(distance < 16, distance, far_bucket)

def matmul(left, right):
    return jnp.dot(left, right, precision=lax.Precision.HIGHEST, preferred_element_type=jnp.float32)

def rms_norm(hidden_in, gain_vec):
    return hidden_in * lax.rsqrt(lax.optimization_barrier(jnp.mean(hidden_in * hidden_in, axis=-1, keepdims=True)) + epsilon) * gain_vec

def softmax_rows(scores):
    peak = lax.optimization_barrier(jnp.max(scores, axis=-1, keepdims=True))
    exp_scores = jnp.exp(scores - peak)
    return exp_scores / lax.optimization_barrier(jnp.sum(exp_scores, axis=-1, keepdims=True))

def decoder_layer(seq_tokens, seq_segments, seq_states, params):
    norm_self, norm_cross, norm_ffn, rel_table, self_query, self_key, self_value, self_out, cross_query, cross_key, cross_value, cross_out, ffn_gate, ffn_up, ffn_down = params
    block_rows = min(512, L)
    positions = jnp.arange(L, dtype=jnp.int32)
    starts = jnp.arange(0, L, block_rows, dtype=jnp.int32)
    normed_self = low(rms_norm(seq_tokens, norm_self))
    self_queries = low(low_back(matmul(normed_self, self_query))).reshape(L, H, E)
    self_keys = low(low_back(matmul(normed_self, self_key))).reshape(L, H, E)
    self_values = low(low_back(matmul(normed_self, self_value))).reshape(L, H, E)

    def self_block(start_row):
        query_block = lax.dynamic_slice_in_dim(self_queries, start_row, block_rows, 0)
        query_pos = start_row + jnp.arange(block_rows, dtype=jnp.int32)
        seg_block = lax.dynamic_slice_in_dim(seq_segments, start_row, block_rows, 0)
        raw_scores = low_back(jnp.einsum('qhe,khe->hqk', query_block, self_keys, precision=lax.Precision.HIGHEST))
        rel_bias = jnp.take(rel_table, bucket_index(query_pos[:, None] - positions[None, :]), axis=0)
        scores = raw_scores + jnp.transpose(rel_bias, (2, 0, 1))
        allowed = (seg_block[:, None] == seq_segments[None, :]) & (positions[None, :] <= query_pos[:, None])
        attn_probs = low(softmax_rows(jnp.where(allowed[None], scores, masked_score)))
        block_out = jnp.einsum('hqk,khe->qhe', attn_probs, self_values, precision=lax.Precision.HIGHEST)
        return low(low_back(block_out)).reshape(block_rows, H * E)
    attended_rows = lax.map(jax.checkpoint(self_block), starts).reshape(L, H * E)
    after_self = seq_tokens + low_back(matmul(attended_rows, self_out))
    normed_cross = low(rms_norm(after_self, norm_cross))
    cross_queries = low(low_back(matmul(normed_cross, cross_query))).reshape(L, H, E)
    cross_keys = low(low_back(matmul(seq_states, cross_key))).reshape(R, H, E)
    cross_values = low(low_back(matmul(seq_states, cross_value))).reshape(R, H, E)

    def cross_block(start_row):
        query_block = lax.dynamic_slice_in_dim(cross_queries, start_row, block_rows, 0)
        scores = low_back(jnp.einsum('qhe,khe->hqk', query_block, cross_keys, precision=lax.Precision.HIGHEST))
        attn_probs = low(softmax_rows(scores))
        block_out = jnp.einsum('hqk,khe->qhe', attn_probs, cross_values, precision=lax.Precision.HIGHEST)
        return low(low_back(block_out)).reshape(block_rows, H * E)
    cross_attended = lax.map(jax.checkpoint(cross_block), starts).reshape(L, H * E)
    after_cross = after_self + low_back(matmul(cross_attended, cross_out))
    normed_ffn = low(rms_norm(after_cross, norm_ffn))
    gate_pre = low_back(matmul(normed_ffn, ffn_gate))
    up_pre = low_back(matmul(normed_ffn, ffn_up))
    hidden_rows = low(jax.nn.gelu(gate_pre, approximate=True) * up_pre)
    return after_cross + low_back(matmul(hidden_rows, ffn_down))

def reference(tokens, segments, encoder, norm_self, norm_cross, norm_ffn, rel_table, self_query, self_key, self_value, self_out, cross_query, cross_key, cross_value, cross_out, ffn_gate, ffn_up, ffn_down, cotangent):
    params = (norm_self, norm_cross, norm_ffn, rel_table, self_query.astype(jnp.float32), self_key.astype(jnp.float32), self_value.astype(jnp.float32), self_out.astype(jnp.float32), cross_query.astype(jnp.float32), cross_key.astype(jnp.float32), cross_value.astype(jnp.float32), cross_out.astype(jnp.float32), ffn_gate.astype(jnp.float32), ffn_up.astype(jnp.float32), ffn_down.astype(jnp.float32))

    def forward(tokens_in, states_in, params_in):

        def one_sequence(items):
            seq_tokens, seq_segments, seq_states = items
            return decoder_layer(seq_tokens, seq_segments, seq_states, params_in)
        outputs = lax.map(jax.checkpoint(one_sequence), (jnp.transpose(tokens_in, (1, 0, 2)), segments, jnp.transpose(states_in, (1, 0, 2))))
        return jnp.transpose(outputs, (1, 0, 2))
    result, pull = jax.vjp(forward, tokens.astype(jnp.float32), encoder.astype(jnp.float32), params)
    tokens_grad, encoder_grad, grads = pull(cotangent.astype(jnp.float32))
    return (result.astype(jnp.bfloat16), tokens_grad, encoder_grad, grads[0], grads[1], grads[2], grads[3], grads[4], grads[5], grads[6], grads[7], grads[8], grads[9], grads[10], grads[11], grads[12], grads[13], grads[14])
```

```python
from functools import reduce

import jax
import jax.numpy as jnp
from jax import lax
from jax.experimental import pallas as pl
from jax.experimental.pallas import tpu as pltpu
from jax.sharding import PartitionSpec as P

MICRO = 4
SHARD, CTX, TP = AXES = ("shard", "ctx", "tp")

BF = jnp.bfloat16
F32 = jnp.float32


def nt(a, b):
    return lax.dot_general(a, b, (((1,), (1,)), ((), ())), preferred_element_type=F32)


def nn(a, b):
    return lax.dot_general(a, b, (((1,), (0,)), ((), ())), preferred_element_type=F32)


def tn(a, b):
    return lax.dot_general(a, b, (((0,), (0,)), ((), ())), preferred_element_type=F32)


def toeplitz(line, half):
    wide = jnp.broadcast_to(line, (half, 2 * half))
    return pltpu.roll(wide, 0, 1, stride=1, stride_axis=0)[:, :half]


def diagonals(tile, half):
    blank = jnp.zeros((8, half), F32)
    total = jnp.zeros((8, 2 * half), F32)
    for at in range(0, half, 8):
        wide = jnp.concatenate([tile[at : at + 8, :], blank], axis=1)
        total = total + (pltpu.roll(wide, 2 * half - at, 1) if at else wide)
    return total


def lane_pick(first, second, left):
    return jnp.where(left, first, second)


def row_softmax(tiles):
    peak = jnp.max(tiles[0], axis=1, keepdims=True)
    for tile in tiles[1:]:
        peak = jnp.maximum(peak, jnp.max(tile, axis=1, keepdims=True))
    exps = [jnp.exp(tile - peak) for tile in tiles]
    total = jnp.sum(reduce_add(exps), axis=1, keepdims=True)
    scale = 1.0 / total
    return [(e * scale).astype(BF) for e in exps], peak + jnp.log(total)


def reduce_add(parts):
    out = parts[0]
    for part in parts[1:]:
        out = out + part
    return out


def self_forward_kernel(core, q, k_own, v_own, k_far, v_far, lines, mask, out, logs):
    half = q.shape[0] // 2
    left = lax.broadcasted_iota(jnp.int32, (1, q.shape[1]), 1) < q.shape[1] // 2
    swapped = core[0] == 1
    a, b = slice(0, half), slice(half, 2 * half)
    outs, totals = [], []
    for head in range(2):
        keep = left if head == 0 else jnp.logical_not(left)
        qh = jnp.where(keep, q[...], jnp.zeros((), BF))
        near = toeplitz(lines[0, 2 * head : 2 * head + 1, :], half)
        next_tile = toeplitz(lines[0, 2 * head + 1 : 2 * head + 2, :], half)
        far = lines[0, 4 + head : 5 + head, :half]
        qa, qb = qh[a], qh[b]
        ka, kb, xa, xb = k_own[a, :], k_own[b, :], k_far[a, :], k_far[b, :]
        pa, la = row_softmax(
            [
                nt(qa, ka) + near + mask[a, 0:half],
                nt(qa, xa) + next_tile + mask[a, 2 * half : 3 * half],
            ]
        )
        oa = nn(pa[0], v_own[a, :]) + nn(pa[1], v_far[a, :])
        pb, lb = row_softmax(
            [
                nt(qb, ka) + jnp.where(swapped, next_tile, far) + mask[b, 0:half],
                nt(qb, kb) + near + mask[b, half : 2 * half],
                nt(qb, xa) + far + mask[b, 2 * half : 3 * half],
                nt(qb, xb) + next_tile + mask[b, 3 * half : 4 * half],
            ]
        )
        ob = (
            nn(pb[0], v_own[a, :])
            + nn(pb[1], v_own[b, :])
            + nn(pb[2], v_far[a, :])
            + nn(pb[3], v_far[b, :])
        )
        outs.append((oa, ob))
        totals.append((la, lb))
    out[a, :] = lane_pick(outs[0][0], outs[1][0], left).astype(BF)
    out[b, :] = lane_pick(outs[0][1], outs[1][1], left).astype(BF)
    for at, piece in ((0, a), (1, b)):
        turned = lane_pick(totals[0][at], totals[1][at], left).T
        logs[0, 0:1, piece] = turned[0:1, :]
        logs[0, 1:2, piece] = turned[q.shape[1] // 2 : q.shape[1] // 2 + 1, :]


def self_backward_kernel(
    core, q, k_own, v_own, k_far, v_far, grad, lines, mask, logs,
    dq, dk_own, dv_own, dk_far, dv_far, sums,
):
    half = q.shape[0] // 2
    left = lax.broadcasted_iota(jnp.int32, (1, q.shape[1]), 1) < q.shape[1] // 2
    swapped = core[0] == 1
    a, b = slice(0, half), slice(half, 2 * half)
    keys = {"oa": (k_own, v_own, a, 0), "ob": (k_own, v_own, b, 1), "xa": (k_far, v_far, a, 2), "xb": (k_far, v_far, b, 3)}
    dk, dv, dqs = {}, {}, [None, None]
    for head in range(2):
        keep = left if head == 0 else jnp.logical_not(left)
        zero = jnp.zeros((), BF)
        qh = jnp.where(keep, q[...], zero)
        gh = jnp.where(keep, grad[...], zero)
        near = toeplitz(lines[0, 2 * head : 2 * head + 1, :], half)
        next_tile = toeplitz(lines[0, 2 * head + 1 : 2 * head + 2, :], half)
        far = lines[0, 4 + head : 5 + head, :half]
        held = {}
        for at, piece, plan in (
            (0, a, (("oa", near), ("xa", next_tile))),
            (1, b, (("oa", jnp.where(swapped, next_tile, far)), ("ob", near), ("xa", far), ("xb", next_tile))),
        ):
            qp, gp = qh[piece], gh[piece]
            total = logs[0, head : head + 1, piece]
            probs, dots = [], []
            for name, bias in plan:
                k, v, rows, slot = keys[name]
                score = nt(k[rows, :], qp) + bias + mask[slot * half : (slot + 1) * half, piece]
                probs.append(jnp.exp(score - total))
                dots.append(nt(v[rows, :], gp))
            delta = jnp.sum(reduce_add([p * d for p, d in zip(probs, dots)]), axis=0, keepdims=True)
            for (name, _), p, d in zip(plan, probs, dots):
                k, v, rows, slot = keys[name]
                ds = p * (d - delta)
                held[at, name] = ds
                low = ds.astype(BF)
                dvp, dkp = nn(p.astype(BF), gp), nn(low, qp)
                dv[name] = dvp if name not in dv else dv[name] + dvp
                dk[name] = dkp if name not in dk else dk[name] + dkp
                dqp = tn(low, jnp.where(keep, k[rows, :], zero))
                dqs[at] = dqp if dqs[at] is None else dqs[at] + dqp
        base = 32 * head
        sums[0, base : base + 8, :] = diagonals(held[0, "oa"] + held[1, "ob"], half)
        sums[0, base + 8 : base + 16, :] = diagonals(held[0, "xa"] + held[1, "xb"], half)
        sums[0, base + 16 : base + 24, :] = diagonals(held[1, "oa"], half)
        rest = reduce_add([held[1, "xa"][at : at + 8, :] for at in range(0, half, 8)])
        sums[0, base + 24 : base + 32, :] = jnp.concatenate([rest, jnp.zeros_like(rest)], axis=1)
    dq[a, :] = dqs[0].astype(BF)
    dq[b, :] = dqs[1].astype(BF)
    for name, ref_k, ref_v, rows in (
        ("oa", dk_own, dv_own, a), ("ob", dk_own, dv_own, b),
        ("xa", dk_far, dv_far, a), ("xb", dk_far, dv_far, b),
    ):
        ref_k[rows, :] = dk[name].astype(ref_k.dtype)
        ref_v[rows, :] = dv[name].astype(ref_v.dtype)


def self_specs(rows):
    kv = lambda which: (lambda p, c: (0, (p // 2) * 4 + which * 2 + p % 2))
    q = pl.BlockSpec((rows, 128), lambda p, c: (0, p))
    k = pl.BlockSpec((rows, 128), kv(0))
    v = pl.BlockSpec((rows, 128), kv(1))
    small = pl.BlockSpec((1, 8, rows), lambda p, c: (p, 0, 0))
    return q, k, v, small


def self_forward(core, q, kv_own, kv_far, lines, mask):
    rows, width = q.shape
    pairs = width // 128
    qs, ks, vs, small = self_specs(rows)
    return pl.pallas_call(
        self_forward_kernel,
        grid_spec=pltpu.PrefetchScalarGridSpec(
            num_scalar_prefetch=1,
            grid=(pairs,),
            in_specs=[qs, ks, vs, ks, vs, small, pl.BlockSpec((rows, 2 * rows), lambda p, c: (0, 0))],
            out_specs=[qs, small],
        ),
        out_shape=(
            jax.ShapeDtypeStruct((rows, width), BF),
            jax.ShapeDtypeStruct((pairs, 8, rows), F32),
        ),
        cost_estimate=pl.CostEstimate(flops=pairs * 24 * 65536 * 128 * 2, bytes_accessed=10 << 20, transcendentals=0),
        name="self_fwd",
    )(core, q, kv_own, kv_own, kv_far, kv_far, lines, mask)


def self_backward(core, q, kv_own, kv_far, grad, lines, mask_t, logs):
    rows, width = q.shape
    pairs = width // 128
    qs, ks, vs, small = self_specs(rows)
    return pl.pallas_call(
        self_backward_kernel,
        grid_spec=pltpu.PrefetchScalarGridSpec(
            num_scalar_prefetch=1,
            grid=(pairs,),
            in_specs=[qs, ks, vs, ks, vs, qs, small, pl.BlockSpec((2 * rows, rows), lambda p, c: (0, 0)), small],
            out_specs=[qs, qs, qs, qs, qs, pl.BlockSpec((1, 64, rows), lambda p, c: (p, 0, 0))],
        ),
        out_shape=(
            jax.ShapeDtypeStruct((rows, width), BF),
            jax.ShapeDtypeStruct((rows, width), F32),
            jax.ShapeDtypeStruct((rows, width), F32),
            jax.ShapeDtypeStruct((rows, width), BF),
            jax.ShapeDtypeStruct((rows, width), BF),
            jax.ShapeDtypeStruct((pairs, 64, rows), F32),
        ),
        cost_estimate=pl.CostEstimate(flops=pairs * 60 * 65536 * 128 * 2, bytes_accessed=20 << 20, transcendentals=0),
        name="self_bwd",
    )(core, q, kv_own, kv_own, kv_far, kv_far, grad, lines, mask_t, logs)


def cross_forward_kernel(q, k, v, out, logs):
    left = lax.broadcasted_iota(jnp.int32, (1, q.shape[1]), 1) < q.shape[1] // 2
    outs, totals = [], []
    for head in range(2):
        keep = left if head == 0 else jnp.logical_not(left)
        qh = jnp.where(keep, q[...], jnp.zeros((), BF))
        p, total = row_softmax([nt(qh, k[...])])
        outs.append(nn(p[0], v[...]))
        totals.append(total)
    out[...] = lane_pick(outs[0], outs[1], left).astype(BF)
    turned = lane_pick(totals[0], totals[1], left).T
    logs[0, 0:1, :] = turned[0:1, :]
    logs[0, 1:2, :] = turned[q.shape[1] // 2 : q.shape[1] // 2 + 1, :]


def cross_backward_kernel(q, k, v, grad, logs, dq, dk, dv):
    left = lax.broadcasted_iota(jnp.int32, (1, q.shape[1]), 1) < q.shape[1] // 2
    dqs = dks = dvs = None
    zero = jnp.zeros((), BF)
    for head in range(2):
        keep = left if head == 0 else jnp.logical_not(left)
        qh = jnp.where(keep, q[...], zero)
        gh = jnp.where(keep, grad[...], zero)
        p = jnp.exp(nt(k[...], qh) - logs[0, head : head + 1, :])
        d = nt(v[...], gh)
        delta = jnp.sum(p * d, axis=0, keepdims=True)
        low = (p * (d - delta)).astype(BF)
        dvp, dkp, dqp = nn(p.astype(BF), gh), nn(low, qh), tn(low, jnp.where(keep, k[...], zero))
        dqs = dqp if dqs is None else dqs + dqp
        dks = dkp if dks is None else dks + dkp
        dvs = dvp if dvs is None else dvs + dvp
    dq[...] = dqs.astype(BF)
    dk[...] = dks.astype(dk.dtype)
    dv[...] = dvs.astype(dv.dtype)


def cross_specs(rows, states):
    kv = lambda which: (lambda p: (0, (p // 2) * 4 + which * 2 + p % 2))
    q = pl.BlockSpec((rows, 128), lambda p: (0, p))
    k = pl.BlockSpec((states, 128), kv(0))
    v = pl.BlockSpec((states, 128), kv(1))
    d = pl.BlockSpec((states, 128), lambda p: (0, p))
    small = pl.BlockSpec((1, 8, rows), lambda p: (p, 0, 0))
    return q, k, v, d, small


def cross_forward(q, kv):
    rows, width = q.shape
    states = kv.shape[0]
    pairs = width // 128
    qs, ks, vs, _, small = cross_specs(rows, states)
    return pl.pallas_call(
        cross_forward_kernel,
        grid=(pairs,),
        in_specs=[qs, ks, vs],
        out_specs=[qs, small],
        out_shape=(
            jax.ShapeDtypeStruct((rows, width), BF),
            jax.ShapeDtypeStruct((pairs, 8, rows), F32),
        ),
        cost_estimate=pl.CostEstimate(flops=pairs * 8 * rows * states * 128, bytes_accessed=4 << 20, transcendentals=0),
        name="cross_fwd",
    )(q, kv, kv)


def cross_backward(q, kv, grad, logs):
    rows, width = q.shape
    states = kv.shape[0]
    pairs = width // 128
    qs, ks, vs, ds, small = cross_specs(rows, states)
    return pl.pallas_call(
        cross_backward_kernel,
        grid=(pairs,),
        in_specs=[qs, ks, vs, qs, small],
        out_specs=[qs, ds, ds],
        out_shape=(
            jax.ShapeDtypeStruct((rows, width), BF),
            jax.ShapeDtypeStruct((states, width), F32),
            jax.ShapeDtypeStruct((states, width), F32),
        ),
        cost_estimate=pl.CostEstimate(flops=pairs * 20 * rows * states * 128, bytes_accessed=6 << 20, transcendentals=0),
        name="cross_bwd",
    )(q, kv, kv, grad, logs)


epsilon = 1e-06
masked_score = -1000000000.0
bucket_edges = (19, 21, 24, 27, 31, 35, 40, 46, 52, 59, 67, 77, 87, 99, 113)


def from_behind(x, axis, by):
    peers = lax.axis_size(axis)
    pairs = [(i, i + by) for i in range(peers) if 0 <= i + by < peers]
    return lax.ppermute(x, axis, pairs)


def bucket_index(distance):
    distance = jnp.maximum(distance, 0)
    far_bucket = reduce(
        lambda running, threshold: running + (distance >= threshold).astype(jnp.int32),
        bucket_edges,
        jnp.full(distance.shape, 16, jnp.int32),
    )
    return jnp.where(distance < 16, distance, far_bucket)


def rms_scale(hidden_in):
    return lax.rsqrt(jnp.mean(hidden_in * hidden_in, axis=-1, keepdims=True) + epsilon)


def norm_back(hidden_in, gain_vec, grad_in):
    inv_scale = rms_scale(hidden_in)
    scaled_grad = gain_vec * grad_in
    inner_mean = jnp.mean(scaled_grad * hidden_in, axis=-1, keepdims=True)
    grad_back = (
        inv_scale * scaled_grad - hidden_in * (inv_scale * inv_scale * inv_scale) * inner_mean
    )
    gain_part = jnp.sum(grad_in * hidden_in * inv_scale, axis=(0, 1))
    return (grad_back, gain_part)


def soft_rows(scores):
    peak = jnp.max(scores, axis=-1, keepdims=True)
    exp_scores = jnp.exp(scores - peak)
    row_total = jnp.sum(exp_scores, axis=-1, keepdims=True)
    return (exp_scores / row_total, peak + jnp.log(row_total))


def soft_back(attn_probs, grad_probs):
    return attn_probs * (grad_probs - jnp.sum(attn_probs * grad_probs, axis=-1, keepdims=True))


def spread_bias(bias_line, row_count, col_count):
    row_width = row_count + col_count
    head_total = bias_line.shape[0]
    tiled_line = jnp.tile(bias_line, (1, row_count))[:, : row_count * row_width]
    return tiled_line.reshape(head_total, row_count, row_width)[:, :, :col_count]


def fold_bias(score_grid, row_count, col_count):
    row_width = row_count + col_count
    head_total = score_grid.shape[0]
    padded = jnp.pad(score_grid, ((0, 0), (0, 0), (0, row_count))).reshape(
        head_total, row_count * row_width
    )
    padded = jnp.pad(padded, ((0, 0), (0, row_count))).reshape(head_total, row_count, row_width + 1)
    return jnp.sum(padded, axis=1)


def gather_rows(normed):
    return lax.all_gather(normed, TP, axis=0, tiled=True)


def gather_grads(grad_in):
    return lax.all_gather(grad_in, TP, axis=0, tiled=True)


def branch_sum(input_values, input_weight):
    return lax.psum_scatter(
        jnp.einsum("gci,iu->gcu", input_values, input_weight, preferred_element_type=jnp.float32),
        TP,
        scatter_dimension=0,
        tiled=True,
    )


def input_sum(incoming_gradients, input_weight):
    return lax.psum_scatter(
        jnp.einsum(
            "iyv,mv->iym", incoming_gradients, input_weight, preferred_element_type=jnp.float32
        ),
        TP,
        scatter_dimension=0,
        tiled=True,
    )


def cross_scores(queries_in, states_kv, head_count):
    local_len, seq_count, head_width = queries_in.shape
    state_len = states_kv.shape[0]
    queries_h = queries_in.reshape(local_len, seq_count, head_count, -1)
    keys_h = states_kv[..., :head_width].reshape(state_len, seq_count, head_count, -1)
    values_h = states_kv[..., head_width:].reshape(state_len, seq_count, head_count, -1)
    scores = jnp.einsum("qshe,kshe->shqk", queries_h, keys_h, preferred_element_type=jnp.float32)
    return (scores, queries_h, keys_h, values_h)


def micro_step(
    tokens, segments, encoder, cotangent, norm_self, norm_cross, norm_ffn, rel_table, shards
):
    gathered = (
        lax.all_gather(shards[0], (SHARD, CTX), axis=0, tiled=True),
        lax.all_gather(shards[1], (SHARD, CTX), axis=0, tiled=True),
        lax.all_gather(shards[2], (SHARD, CTX), axis=0, tiled=True),
        lax.all_gather(shards[3], (SHARD, CTX), axis=1, tiled=True),
        lax.all_gather(shards[4], (SHARD, CTX), axis=0, tiled=True),
        lax.all_gather(shards[5], (SHARD, CTX), axis=0, tiled=True),
        lax.all_gather(shards[6], (SHARD, CTX), axis=0, tiled=True),
        lax.all_gather(shards[7], (SHARD, CTX), axis=1, tiled=True),
        lax.all_gather(shards[8], (SHARD, CTX), axis=0, tiled=True),
        lax.all_gather(shards[9], (SHARD, CTX), axis=0, tiled=True),
        lax.all_gather(shards[10], (SHARD, CTX), axis=1, tiled=True),
    )
    (
        w_query,
        w_key,
        w_value,
        output_weight,
        cross_query_weight,
        c_key,
        c_value,
        cross_output_weight,
        w_gate,
        w_up,
        down_weight,
    ) = gathered
    own_rows = tokens.shape[0]
    seq_count = tokens.shape[1]
    local_len = own_rows * lax.axis_size(TP)
    window_len = 3 * local_len
    period = window_len + local_len + 1
    head_count = rel_table.shape[1]
    head_width = w_query.shape[1]
    feed_width = w_gate.shape[1]
    ctx_index = lax.axis_index(CTX)
    fill_ids = jnp.full((seq_count, 2 * local_len), -1, jnp.int32)
    seg_padded = jnp.concatenate([fill_ids, segments], axis=1)
    seg_window = lax.dynamic_slice_in_dim(seg_padded, ctx_index * local_len, window_len, 1)
    seg_query = lax.dynamic_slice_in_dim(segments, ctx_index * local_len, local_len, 1)
    offsets = jnp.arange(period, dtype=jnp.int32)
    distance = jnp.where(
        offsets < window_len, 2 * local_len - offsets, 2 * local_len - offsets + period
    )
    one_hot = (
        bucket_index(distance)[:, None] == jnp.arange(rel_table.shape[0], dtype=jnp.int32)[None, :]
    ).astype(jnp.float32)
    bias_line = jnp.dot(
        one_hot, rel_table, precision=lax.Precision.HIGHEST, preferred_element_type=jnp.float32
    ).T
    rel_bias = spread_bias(bias_line, local_len, window_len)
    causal_ok = (
        jnp.arange(window_len, dtype=jnp.int32)[None, :]
        <= jnp.arange(local_len, dtype=jnp.int32)[:, None] + 2 * local_len
    )

    def self_scores(one_query, one_window, query_ids, window_ids):
        queries_h = one_query.reshape(local_len, head_count, -1)
        keys_h = one_window[:, :head_width].reshape(window_len, head_count, -1)
        values_h = one_window[:, head_width:].reshape(window_len, head_count, -1)
        scores = (
            jnp.einsum("qhe,khe->hqk", queries_h, keys_h, preferred_element_type=jnp.float32)
            + rel_bias
        )
        allowed = (query_ids[:, None] == window_ids[None, :]) & causal_ok
        return (jnp.where(allowed[None], scores, masked_score), queries_h, keys_h, values_h)

    def self_forward(items):
        one_query, one_window, query_ids, window_ids = items
        scores, queries_h, keys_h, values_h = self_scores(
            one_query, one_window, query_ids, window_ids
        )
        attn_probs, log_total = soft_rows(scores)
        block_out = jnp.einsum(
            "hqk,khe->qhe",
            attn_probs.astype(jnp.bfloat16),
            values_h,
            preferred_element_type=jnp.float32,
        )
        return (block_out.reshape(local_len, head_width), log_total)

    def self_backward(items):
        one_query, one_window, query_ids, window_ids, log_total, grad_out = items
        scores, queries_h, keys_h, values_h = self_scores(
            one_query, one_window, query_ids, window_ids
        )
        attn_probs = jnp.exp(scores - log_total)
        grad_heads = grad_out.reshape(local_len, head_count, -1)
        grad_values = jnp.einsum(
            "hqk,qhe->khe",
            attn_probs.astype(jnp.bfloat16),
            grad_heads,
            preferred_element_type=jnp.float32,
        )
        grad_probs = jnp.einsum(
            "qhe,khe->hqk", grad_heads, values_h, preferred_element_type=jnp.float32
        )
        grad_scores = soft_back(attn_probs, grad_probs)
        grad_line = fold_bias(grad_scores, local_len, window_len)
        grad_low = grad_scores.astype(jnp.bfloat16)
        grad_queries = jnp.einsum(
            "hqk,khe->qhe", grad_low, keys_h, preferred_element_type=jnp.float32
        )
        grad_keys = jnp.einsum(
            "hqk,qhe->khe", grad_low, queries_h, preferred_element_type=jnp.float32
        )
        grad_pair = jnp.concatenate(
            [
                grad_keys.reshape(window_len, head_width),
                grad_values.reshape(window_len, head_width),
            ],
            axis=-1,
        )
        return (grad_queries.reshape(local_len, head_width), grad_pair, grad_line)

    resid_in = tokens.astype(jnp.float32)
    normed_one = (resid_in * rms_scale(resid_in) * norm_self).astype(jnp.bfloat16)
    first_rows = gather_rows(normed_one)
    self_attention_weight = jnp.concatenate([w_query, w_key, w_value], axis=1)
    projected = jnp.einsum(
        "rmh,ha->rma", first_rows, self_attention_weight, preferred_element_type=jnp.float32
    ).astype(jnp.bfloat16)
    queries = projected[..., :head_width]
    key_value = projected[..., head_width:]
    earlier = [from_behind(key_value, CTX, offset) for offset in (2, 1)]
    window = jnp.concatenate(earlier + [key_value], axis=0)
    seq_queries = jnp.moveaxis(queries, 1, 0)
    seq_window = jnp.moveaxis(window, 1, 0)
    self_mixed, self_logs = lax.map(self_forward, (seq_queries, seq_window, seg_query, seg_window))
    attended_rows = jnp.moveaxis(self_mixed, 0, 1).astype(jnp.bfloat16)
    after_self = resid_in + branch_sum(attended_rows, output_weight)
    normed_two = (after_self * rms_scale(after_self) * norm_cross).astype(jnp.bfloat16)
    second_rows = gather_rows(normed_two)
    cross_q = jnp.einsum(
        "rmh,ha->rma", second_rows, cross_query_weight, preferred_element_type=jnp.float32
    ).astype(jnp.bfloat16)
    state_weight = jnp.concatenate([c_key, c_value], axis=1)
    cross_kv = jnp.einsum(
        "rsd,df->rsf", encoder, state_weight, preferred_element_type=jnp.float32
    ).astype(jnp.bfloat16)
    scores, queries_h, keys_h, values_h = cross_scores(cross_q, cross_kv, head_count)
    attn_probs, cross_logs = soft_rows(scores)
    cross_mix = jnp.einsum(
        "shqk,kshe->qshe",
        attn_probs.astype(jnp.bfloat16),
        values_h,
        preferred_element_type=jnp.float32,
    )
    cross_attended = cross_mix.reshape(local_len, seq_count, head_width).astype(jnp.bfloat16)
    after_cross = after_self + branch_sum(cross_attended, cross_output_weight)
    normed_three = (after_cross * rms_scale(after_cross) * norm_ffn).astype(jnp.bfloat16)
    third_rows = gather_rows(normed_three)
    feedforward_weight = jnp.concatenate([w_gate, w_up], axis=1)
    gate_up_product = jnp.einsum(
        "rmh,ha->rma", third_rows, feedforward_weight, preferred_element_type=jnp.float32
    )
    gate_pre = gate_up_product[..., :feed_width]
    up_pre = gate_up_product[..., feed_width:]
    hidden_rows = (jax.nn.gelu(gate_pre, approximate=True) * up_pre).astype(jnp.bfloat16)
    result = after_cross + branch_sum(hidden_rows, down_weight)
    grad_result = cotangent.astype(jnp.float32)
    feedforward_gradient = gather_grads(grad_result.astype(jnp.bfloat16))
    feedforward_down_gradient = jnp.einsum(
        "euy,euh->yh", hidden_rows, feedforward_gradient, preferred_element_type=jnp.float32
    )
    hidden_gradient = jnp.einsum(
        "ezk,ck->ezc", feedforward_gradient, down_weight, preferred_element_type=jnp.float32
    )
    _, feed_pull = jax.vjp(
        lambda gate_in, up_in: jax.nn.gelu(gate_in, approximate=True) * up_in, gate_pre, up_pre
    )
    grad_gate, grad_up = feed_pull(hidden_gradient)
    gate_up_gradient = jnp.concatenate([grad_gate, grad_up], axis=-1).astype(jnp.bfloat16)
    feed_grads = jnp.einsum(
        "zvn,zvp->np", third_rows, gate_up_gradient, preferred_element_type=jnp.float32
    )
    ffn_gate_grad = feed_grads[:, :feed_width]
    ffn_up_grad = feed_grads[:, feed_width:]
    ffn_sums = None
    grad_back_three, gain_three = norm_back(
        after_cross, norm_ffn, input_sum(gate_up_gradient, feedforward_weight)
    )
    grad_mid = grad_result + grad_back_three
    cross_gradient = gather_grads(grad_mid.astype(jnp.bfloat16))
    cross_out_grad = jnp.einsum(
        "euy,euh->yh", cross_attended, cross_gradient, preferred_element_type=jnp.float32
    )
    grad_crossed = jnp.einsum(
        "ezk,ck->ezc", cross_gradient, cross_output_weight, preferred_element_type=jnp.float32
    ).astype(jnp.bfloat16)
    grad_heads = grad_crossed.reshape(local_len, seq_count, head_count, -1)
    cross_probs = jnp.exp(scores - cross_logs)
    grad_cvalues = jnp.einsum(
        "shqk,qshe->kshe",
        cross_probs.astype(jnp.bfloat16),
        grad_heads,
        preferred_element_type=jnp.float32,
    )
    grad_probs = jnp.einsum(
        "qshe,kshe->shqk", grad_heads, values_h, preferred_element_type=jnp.float32
    )
    grad_low = soft_back(cross_probs, grad_probs).astype(jnp.bfloat16)
    cross_query_weight_gradient = jnp.einsum(
        "shqk,kshe->qshe", grad_low, keys_h, preferred_element_type=jnp.float32
    )
    cross_query_weight_gradient = cross_query_weight_gradient.reshape(
        local_len, seq_count, head_width
    ).astype(jnp.bfloat16)
    grad_ckeys = jnp.einsum(
        "shqk,qshe->kshe", grad_low, queries_h, preferred_element_type=jnp.float32
    )
    state_len = encoder.shape[0]
    grad_ckv = jnp.concatenate(
        [
            grad_ckeys.reshape(state_len, seq_count, head_width),
            grad_cvalues.reshape(state_len, seq_count, head_width),
        ],
        axis=-1,
    )
    grad_ckv_own = lax.psum_scatter(
        grad_ckv.astype(jnp.bfloat16), CTX, scatter_dimension=0, tiled=True
    )
    state_rows = grad_ckv_own.shape[0]
    states_own = lax.dynamic_slice_in_dim(encoder, ctx_index * state_rows, state_rows, 0)
    state_grads = jnp.einsum(
        "rsd,rsf->df", states_own, grad_ckv_own, preferred_element_type=jnp.float32
    )
    cross_key_grad = state_grads[:, :head_width]
    cross_value_grad = state_grads[:, head_width:]
    state_term = jnp.einsum(
        "rsf,df->rsd", grad_ckv_own, state_weight, preferred_element_type=jnp.float32
    )
    encoder_grad = lax.psum_scatter(
        state_term.astype(jnp.bfloat16), TP, scatter_dimension=2, tiled=True
    ).astype(jnp.float32)
    cross_query_grad = jnp.einsum(
        "zvn,zvp->np", second_rows, cross_query_weight_gradient, preferred_element_type=jnp.float32
    )
    grad_back_two, gain_two = norm_back(
        after_self, norm_cross, input_sum(cross_query_weight_gradient, cross_query_weight)
    )
    grad_first = grad_mid + grad_back_two
    self_attention_gradient = gather_grads(grad_first.astype(jnp.bfloat16))
    self_out_grad = jnp.einsum(
        "euy,euh->yh", attended_rows, self_attention_gradient, preferred_element_type=jnp.float32
    )
    grad_attended = jnp.einsum(
        "ezk,ck->ezc", self_attention_gradient, output_weight, preferred_element_type=jnp.float32
    ).astype(jnp.bfloat16)
    grad_q, grad_window, grad_lines = lax.map(
        self_backward,
        (
            seq_queries,
            seq_window,
            seg_query,
            seg_window,
            self_logs,
            jnp.moveaxis(grad_attended, 1, 0),
        ),
    )
    table_grad = jnp.einsum(
        "tb,ht->bh",
        one_hot,
        jnp.sum(grad_lines, axis=0),
        precision=lax.Precision.HIGHEST,
        preferred_element_type=jnp.float32,
    )
    grad_window = jnp.moveaxis(grad_window, 0, 1)
    grad_kv = grad_window[2 * local_len :]
    for offset, grad_part in (
        (-2, grad_window[:local_len]),
        (-1, grad_window[local_len : 2 * local_len]),
    ):
        grad_kv = grad_kv + from_behind(grad_part.astype(jnp.bfloat16), CTX, offset).astype(
            grad_part.dtype
        )
    projection_gradient = jnp.concatenate([jnp.moveaxis(grad_q, 0, 1), grad_kv], axis=-1).astype(
        jnp.bfloat16
    )
    self_attention_gradients = jnp.einsum(
        "zvn,zvp->np", first_rows, projection_gradient, preferred_element_type=jnp.float32
    )
    self_query_grad = self_attention_gradients[:, :head_width]
    self_key_grad = self_attention_gradients[:, head_width : 2 * head_width]
    self_value_grad = self_attention_gradients[:, 2 * head_width :]
    grad_back_one, gain_one = norm_back(
        resid_in, norm_self, input_sum(projection_gradient, self_attention_weight)
    )
    tokens_grad = grad_first + grad_back_one
    local_grads = (
        self_query_grad,
        self_key_grad,
        self_value_grad,
        self_out_grad,
        cross_query_grad,
        cross_key_grad,
        cross_value_grad,
        cross_out_grad,
        ffn_gate_grad,
        ffn_up_grad,
        feedforward_down_gradient,
        table_grad,
    )
    return (
        result.astype(jnp.bfloat16),
        tokens_grad,
        encoder_grad,
        (gain_one, gain_two, gain_three),
        local_grads,
        ffn_sums,
    )


def body(
    tokens,
    segments,
    encoder,
    norm_self,
    norm_cross,
    norm_ffn,
    rel_table,
    self_query,
    self_key,
    self_value,
    self_out,
    cross_query,
    cross_key,
    cross_value,
    cross_out,
    ffn_gate,
    ffn_up,
    ffn_down,
    cotangent,
):
    shards = (
        self_query,
        self_key,
        self_value,
        self_out,
        cross_query,
        cross_key,
        cross_value,
        cross_out,
        ffn_gate,
        ffn_up,
        ffn_down,
    )
    per_micro = tokens.shape[1] // MICRO
    results = []
    token_grads = []
    state_grads = []
    gains = None
    totals = None
    for micro in range(MICRO):
        first = micro * per_micro
        out = micro_step(
            tokens[:, first : first + per_micro],
            segments[first : first + per_micro],
            encoder[:, first : first + per_micro],
            cotangent[:, first : first + per_micro],
            norm_self,
            norm_cross,
            norm_ffn,
            rel_table,
            shards,
        )
        results.append(out[0])
        token_grads.append(out[1])
        state_grads.append(out[2])
        gains = out[3] if gains is None else tuple((a + b for a, b in zip(gains, out[3])))
        totals = out[4] if totals is None else tuple((a + b for a, b in zip(totals, out[4])))
    gain_sums = lax.psum(gains, (SHARD, CTX, TP))
    summed = (
        lax.psum_scatter(
            totals[0].astype(jnp.bfloat16), (SHARD, CTX), scatter_dimension=0, tiled=True
        ).astype(jnp.float32),
        lax.psum_scatter(
            totals[1].astype(jnp.bfloat16), (SHARD, CTX), scatter_dimension=0, tiled=True
        ).astype(jnp.float32),
        lax.psum_scatter(
            totals[2].astype(jnp.bfloat16), (SHARD, CTX), scatter_dimension=0, tiled=True
        ).astype(jnp.float32),
        lax.psum_scatter(
            totals[3].astype(jnp.bfloat16), (SHARD, CTX), scatter_dimension=1, tiled=True
        ).astype(jnp.float32),
        lax.psum_scatter(
            totals[4].astype(jnp.bfloat16), (SHARD, CTX), scatter_dimension=0, tiled=True
        ).astype(jnp.float32),
        lax.psum_scatter(
            totals[5].astype(jnp.bfloat16), (SHARD, CTX), scatter_dimension=0, tiled=True
        ).astype(jnp.float32),
        lax.psum_scatter(
            totals[6].astype(jnp.bfloat16), (SHARD, CTX), scatter_dimension=0, tiled=True
        ).astype(jnp.float32),
        lax.psum_scatter(
            totals[7].astype(jnp.bfloat16), (SHARD, CTX), scatter_dimension=1, tiled=True
        ).astype(jnp.float32),
        lax.psum_scatter(
            totals[8].astype(jnp.bfloat16), (SHARD, CTX), scatter_dimension=0, tiled=True
        ).astype(jnp.float32),
        lax.psum_scatter(
            totals[9].astype(jnp.bfloat16), (SHARD, CTX), scatter_dimension=0, tiled=True
        ).astype(jnp.float32),
        lax.psum_scatter(
            totals[10].astype(jnp.bfloat16), (SHARD, CTX), scatter_dimension=1, tiled=True
        ).astype(jnp.float32),
        lax.psum_scatter(
            totals[11].astype(jnp.bfloat16), (SHARD, CTX), scatter_dimension=0, tiled=True
        ).astype(jnp.float32),
    )
    result = jnp.concatenate(results, axis=1)
    tokens_grad = jnp.concatenate(token_grads, axis=1)
    encoder_grad = jnp.concatenate(state_grads, axis=1)
    return (
        result,
        tokens_grad,
        encoder_grad,
        gain_sums[0],
        gain_sums[1],
        gain_sums[2],
        summed[11],
        summed[0],
        summed[1],
        summed[2],
        summed[3],
        summed[4],
        summed[5],
        summed[6],
        summed[7],
        summed[8],
        summed[9],
        summed[10],
    )


def chip_coords(index):
    return (index >> 4, (index >> 3) & 1, (index >> 2) & 1, index & 3)


def move(x, target):
    pairs = []
    for index in range(32):
        sx, core, y, z = target(*chip_coords(index))
        pairs.append((index, sx * 16 + core * 8 + y * 4 + z))
    return lax.ppermute(x, AXES, pairs)


def flip_x(v):
    return move(v, lambda sx, core, y, z: (1 - sx, core, y, z))


def flip_core(v):
    return move(v, lambda sx, core, y, z: (sx, 1 - core, y, z))


def flip_y(v):
    return move(v, lambda sx, core, y, z: (sx, core, 1 - y, z))


def from_z(v, step):
    return move(v, lambda sx, core, y, z: (sx, core, y, (z - step) % 4))


def my_coords():
    shard = lax.axis_index(SHARD)
    return (shard // 2, shard % 2, lax.axis_index(CTX), lax.axis_index(TP))


def swap_blocks(blocks, place):
    sx, core, y, _ = place
    for bit, mask in ((y, 1), (core, 2), (sx, 4)):
        taken = bit == 1
        blocks = [jnp.where(taken, blocks[at ^ mask], blocks[at]) for at in range(8)]
    return blocks


RELATIVE = (0, 1, 4, 5, 2, 3, 6, 7)


def lanes(v):
    width = v.shape[-1] // 8
    return [v[..., at * width : (at + 1) * width] for at in range(8)]


def to_relative(v, place):
    blocks = swap_blocks(lanes(v), place)
    return jnp.concatenate([blocks[at] for at in RELATIVE], axis=-1)


def from_relative(v, place):
    given = lanes(v)
    blocks = [given[RELATIVE.index(at)] for at in range(8)]
    return jnp.concatenate(swap_blocks(blocks, place), axis=-1)


def pick(stack, at):
    return lax.dynamic_index_in_dim(stack, at, 0, keepdims=False)


def bring_rows(block, place):
    sx, core, y, z = place
    by_seq = jnp.transpose(block, (1, 0, 2))
    got = []
    for step in range(4):
        got.append(
            move(
                pick(by_seq, (z + step) % 4),
                lambda sx, core, y, z, step=step: (sx, (z >> 1) ^ y, core, (z + step) % 4),
            )
        )
    stack = jnp.stack(got)
    return jnp.concatenate([pick(stack, (z - (at ^ (2 * core))) % 4) for at in range(4)], axis=0)


def return_rows(rows, place):
    sx, core, y, z = place
    slots = rows.reshape(4, rows.shape[0] // 4, rows.shape[1])
    got = []
    for step in range(4):
        got.append(
            move(
                pick(slots, ((z - step) % 4) ^ (2 * core)),
                lambda sx, core, y, z, step=step: (
                    sx,
                    y,
                    core ^ (((z - step) % 4) >> 1),
                    (z - step) % 4,
                ),
            )
        )
    stack = jnp.stack(got)
    return jnp.stack([pick(stack, (at - z) % 4) for at in range(4)], axis=1)


def gather_blocks(piece, first, second):
    held = jnp.stack([piece] + [from_z(piece, step) for step in (1, 2, 3)])
    near = first(held)
    blocks = {0: held, first_bit(first): near}
    blocks[first_bit(second)] = second(held)
    blocks[3] = second(near)
    for at in range(4):
        blocks[4 + at] = flip_core(blocks[at])
    return [blocks[at] for at in range(8)]


def first_bit(flip):
    return 1 if flip is flip_y else 2


def join(blocks, start, stop):
    whole = jnp.concatenate([block[:, start:stop] for block in blocks], axis=-1)
    return whole.reshape(-1, whole.shape[-1])


def weight_grads(rows_grad, rows_in, first, second):
    half = rows_in.shape[1] // 2
    away = jnp.einsum("mi,md->id", rows_grad, rows_in[:, half:], preferred_element_type=F32)
    came = flip_core(away.astype(BF))
    kept = jnp.einsum("mi,md->id", rows_grad, rows_in[:, :half], preferred_element_type=F32)
    return (kept + came.astype(F32)).astype(BF)


def finish_grads(part, first, second):
    width = part.shape[1] // 4
    blocks = [part[:, at * width : (at + 1) * width] for at in range(4)]
    bit, low = first_bit(first), first_bit(second)
    sent = jnp.stack([blocks[bit], blocks[3]])
    came = first(sent)
    held = jnp.stack([blocks[0], blocks[low]]) + came
    came = second(held[1])
    mine = (held[0].astype(F32) + came.astype(F32)).astype(BF)
    mine = mine.reshape(4, -1, width)
    total = mine[0].astype(F32)
    for step in (1, 2, 3):
        total = total + from_z(mine[step], -step).astype(F32)
    return total


def nt_rows(rows, weight):
    return jnp.einsum("md,id->mi", rows, weight, preferred_element_type=F32)


def nn_rows(rows, weight):
    return jnp.einsum("mi,id->md", rows, weight, preferred_element_type=F32)


def row_norm_back(hidden_in, gain_vec, grad_in):
    inv_scale = rms_scale(hidden_in)
    scaled_grad = gain_vec * grad_in
    inner_mean = jnp.mean(scaled_grad * hidden_in, axis=-1, keepdims=True)
    grad_back = (
        inv_scale * scaled_grad - hidden_in * (inv_scale * inv_scale * inv_scale) * inner_mean
    )
    return grad_back, jnp.sum(grad_in * hidden_in * inv_scale, axis=0)


def fast_body(
    tokens, segments, encoder, norm_self, norm_cross, norm_ffn, rel_table,
    self_query, self_key, self_value, self_out,
    cross_query, cross_key, cross_value, cross_out,
    ffn_gate, ffn_up, ffn_down, cotangent,
):
    place = my_coords()
    sx, core, y, z = place
    heads = rel_table.shape[1]
    inner = self_query.shape[1]
    feed = ffn_gate.shape[1]
    cut = feed // 2

    resid_in = to_relative(bring_rows(tokens, place), place).astype(F32)
    rows = resid_in.shape[0]
    half = rows // 2

    piece_kv = jnp.concatenate([self_key.T, self_value.T], axis=0)
    piece_qo = jnp.concatenate([self_query.T, self_out], axis=0)
    piece_ckv = jnp.concatenate([cross_key.T, cross_value.T], axis=0)
    piece_cqo = jnp.concatenate([cross_query.T, cross_out], axis=0)
    gate_t, up_t = ffn_gate.T, ffn_up.T
    piece_f = [
        jnp.concatenate([w[at : at + cut] for w in (gate_t, up_t, ffn_down)], axis=0)
        for at in (0, cut)
    ]
    ways = ((flip_y, flip_x), (flip_x, flip_y))
    blocks = gather_blocks(piece_kv, *ways[0])
    w_kv = join(blocks, 0, 2 * inner)
    blocks = gather_blocks(piece_qo, *ways[1])
    w_q, w_so = join(blocks, 0, inner), join(blocks, inner, 2 * inner)
    blocks = gather_blocks(piece_ckv, *ways[0])
    w_ckv = join(blocks, 0, 2 * inner)
    blocks = gather_blocks(piece_cqo, *ways[1])
    w_cq, w_co = join(blocks, 0, inner), join(blocks, inner, 2 * inner)
    w_f = []
    for piece, way in zip(piece_f, ways):
        blocks = gather_blocks(piece, *way)
        w_f.append([join(blocks, at * cut, (at + 1) * cut) for at in range(3)])

    mine = lax.dynamic_index_in_dim(encoder, z, 1, keepdims=False)
    mine_seg = lax.dynamic_index_in_dim(segments, z, 0, keepdims=True)
    pairs = []
    for index in range(32):
        ax, ac, ay, az = chip_coords(index)
        if ac == ay:
            pairs.append((index, ax * 16 + (1 - ac) * 8 + ay * 4 + az))
    own_seq = core == y
    states = jnp.where(own_seq, mine, lax.ppermute(mine, AXES, pairs))
    seg = jnp.where(own_seq, mine_seg, lax.ppermute(mine_seg, AXES, pairs))[0]
    states = to_relative(states, place)

    gains = to_relative(jnp.stack([norm_self, norm_cross, norm_ffn]), place)
    gain_self, gain_cross, gain_ffn = gains[0:1], gains[1:2], gains[2:3]

    table = jnp.concatenate([rel_table] + [from_z(rel_table, step) for step in (1, 2, 3)], axis=1)
    turn = jnp.arange(2 * half, dtype=jnp.int32)
    signed = jnp.where(turn < half, turn, turn - 2 * half)
    buckets = jnp.arange(table.shape[0], dtype=jnp.int32)

    def hot(distance):
        return (bucket_index(distance)[..., None] == buckets).astype(F32)

    def bias_lines(distance):
        return jnp.dot(
            hot(distance), table, precision=lax.Precision.HIGHEST, preferred_element_type=F32
        ).T

    def kernel_lines(sign):
        near = bias_lines(sign * signed).reshape(-1, 2, 2 * half)
        after = bias_lines(half + sign * signed).reshape(-1, 2, 2 * half)
        far = jnp.broadcast_to(table[-1].reshape(-1, 2, 1), near.shape)
        blank = jnp.zeros((near.shape[0], 2, 2 * half), F32)
        return jnp.concatenate(
            [near[:, 0:1], after[:, 0:1], near[:, 1:2], after[:, 1:2], far, blank], axis=1
        )

    lines_forward, lines_backward = kernel_lines(-1), kernel_lines(1)

    quarter = jnp.arange(half, dtype=jnp.int32)
    spots = jnp.concatenate([quarter + half * n for n in (core, 3 - core, 1 - core, 2 + core)])
    seg_spots = jnp.concatenate(
        [
            lax.dynamic_slice_in_dim(seg, half * n, half, 0)
            for n in (core, 3 - core, 1 - core, 2 + core)
        ]
    )

    def mask_of(query_at, key_at, query_seg, key_seg):
        return jnp.where((query_seg == key_seg) & (key_at <= query_at), 0.0, masked_score).astype(F32)

    mask = mask_of(spots[:rows, None], spots[None, :], seg_spots[:rows, None], seg_spots[None, :])
    mask_t = mask_of(spots[None, :rows], spots[:, None], seg_spots[None, :rows], seg_spots[:, None])
    core_id = core.reshape(1).astype(jnp.int32)

    normed_self = (resid_in * rms_scale(resid_in) * gain_self).astype(BF)
    kv_own = nt_rows(normed_self, w_kv).astype(BF)
    kv_far = flip_core(kv_own)
    queries = nt_rows(normed_self, w_q).astype(BF)
    mixed, self_logs = self_forward(core_id, queries, kv_own, kv_far, lines_forward, mask)
    after_self = resid_in + nn_rows(mixed, w_so)
    normed_cross = (after_self * rms_scale(after_self) * gain_cross).astype(BF)
    cross_q = nt_rows(normed_cross, w_cq).astype(BF)
    cross_kv = nt_rows(states, w_ckv).astype(BF)
    cross_mixed, cross_logs = cross_forward(cross_q, cross_kv)
    after_cross = after_self + nn_rows(cross_mixed, w_co)
    normed_ffn = (after_cross * rms_scale(after_cross) * gain_ffn).astype(BF)
    pres, hiddens = [], []
    outcome = after_cross
    for gate_w, up_w, down_w in w_f:
        gate_pre, up_pre = nt_rows(normed_ffn, gate_w), nt_rows(normed_ffn, up_w)
        hidden = (jax.nn.gelu(gate_pre, approximate=True) * up_pre).astype(BF)
        outcome = outcome + nn_rows(hidden, down_w)
        pres.append((gate_pre, up_pre))
        hiddens.append(hidden)
    result = return_rows(from_relative(outcome.astype(BF), place), place)

    grad_low = to_relative(bring_rows(cotangent, place), place)
    grad_result = grad_low.astype(F32)
    grad_normed = 0.0
    feed_parts = []
    for (gate_w, up_w, down_w), (gate_pre, up_pre), hidden, way in zip(w_f, pres, hiddens, ways):
        down_part = weight_grads(hidden, grad_low, *way)
        grad_hidden = nt_rows(grad_low, down_w)
        _, pull = jax.vjp(
            lambda gate_in, up_in: jax.nn.gelu(gate_in, approximate=True) * up_in, gate_pre, up_pre
        )
        grad_gate, grad_up = (v.astype(BF) for v in pull(grad_hidden))
        gate_part = weight_grads(grad_gate, normed_ffn, *way)
        up_part = weight_grads(grad_up, normed_ffn, *way)
        feed_parts.append((gate_part, up_part, down_part))
        grad_normed = grad_normed + nn_rows(grad_gate, gate_w) + nn_rows(grad_up, up_w)
    feed_done = [
        [finish_grads(part, *way) for part in parts] for parts, way in zip(feed_parts, ways)
    ]
    back, gain_three = row_norm_back(after_cross, gain_ffn, grad_normed)
    grad_mid = grad_result + back
    low_mid = grad_mid.astype(BF)
    co_done = finish_grads(weight_grads(cross_mixed, low_mid, *ways[1]), *ways[1])
    grad_cross_mixed = nt_rows(low_mid, w_co).astype(BF)
    grad_cq, grad_ck, grad_cv = cross_backward(cross_q, cross_kv, grad_cross_mixed, cross_logs)
    own_states = states.shape[0] // 2
    shared = jnp.concatenate(
        [v.reshape(v.shape[0], 4, 1, inner) for v in (grad_ck, grad_cv)], axis=2
    ).reshape(2 * own_states, -1)
    sent = lax.dynamic_slice_in_dim(shared, (1 - core) * own_states, own_states, 0).astype(BF)
    kept = lax.dynamic_slice_in_dim(shared, core * own_states, own_states, 0)
    grad_ckv = (kept + flip_core(sent).astype(F32)).astype(BF)
    states_own = lax.dynamic_slice_in_dim(states, core * own_states, own_states, 0)
    ckv_done = finish_grads(weight_grads(grad_ckv, states_own, *ways[0]), *ways[0])
    state_grad = from_relative(nn_rows(grad_ckv, w_ckv).astype(BF), place)
    state_cols = jnp.stack([state_grad[:, at * inner : (at + 1) * inner] for at in range(4)])
    got = []
    for step in range(4):
        got.append(
            move(
                pick(state_cols, (z + step) % 4),
                lambda sx, core, y, z, step=step: (sx, y, core, (z + step) % 4),
            )
        )
    got = jnp.stack(got)
    encoder_grad = jnp.stack([pick(got, (z - at) % 4) for at in range(4)], axis=1).astype(F32)

    cq_done = finish_grads(weight_grads(grad_cq, normed_cross, *ways[1]), *ways[1])
    back, gain_two = row_norm_back(after_self, gain_cross, nn_rows(grad_cq, w_cq))
    grad_first = grad_mid + back
    low_first = grad_first.astype(BF)
    so_done = finish_grads(weight_grads(mixed, low_first, *ways[1]), *ways[1])
    grad_mixed = nt_rows(low_first, w_so).astype(BF)
    grad_q, dk_own, dv_own, dk_far, dv_far, sums = self_backward(
        core_id, queries, kv_own, kv_far, grad_mixed, lines_backward, mask_t, self_logs
    )
    dk = (dk_own + flip_core(dk_far).astype(F32)).astype(BF)
    dv = (dv_own + flip_core(dv_far).astype(F32)).astype(BF)
    grad_kv = jnp.concatenate(
        [v.reshape(rows, 4, 1, inner) for v in (dk, dv)], axis=2
    ).reshape(rows, -1)
    q_done = finish_grads(weight_grads(grad_q, normed_self, *ways[1]), *ways[1])
    kv_done = finish_grads(weight_grads(grad_kv, normed_self, *ways[0]), *ways[0])
    back, gain_one = row_norm_back(
        resid_in, gain_self, nn_rows(grad_q, w_q) + nn_rows(grad_kv, w_kv)
    )
    tokens_grad = return_rows(
        from_relative((grad_first + back).astype(BF), place), place
    ).astype(F32)

    inside = (signed[None, :] - jnp.arange(8, dtype=jnp.int32)[:, None]) % (2 * half)
    inside = jnp.where(inside < half, inside, inside - 2 * half)
    kinds = jnp.stack(
        [inside, half + inside, (3 - 2 * core) * half + inside, jnp.full_like(inside, 2 * half)]
    )
    sums = sums.reshape(4 * heads, 4, 8, 2 * half)
    table_grad = jnp.einsum(
        "ndmb,hndm->bh",
        hot(kinds),
        sums,
        precision=lax.Precision.HIGHEST,
        preferred_element_type=F32,
    )
    by_z = table_grad.reshape(-1, 4, heads)
    by_z = jnp.concatenate(
        [lax.dynamic_index_in_dim(by_z, (at - z) % 4, 1, keepdims=True) for at in range(4)], axis=1
    )
    gain_parts = from_relative(jnp.stack([gain_one, gain_two, gain_three]), place)
    gain_sums, table_sum = lax.psum((gain_parts, by_z), AXES)
    block = lax.axis_index(SHARD) * 2 + y
    own_table = lax.dynamic_slice_in_dim(
        lax.dynamic_index_in_dim(table_sum, z, 1, keepdims=False), block * 4, 4, 0
    )
    gate_grad, up_grad, down_grad = (
        jnp.concatenate([done[at] for done in feed_done], axis=0) for at in range(3)
    )
    return (
        result,
        tokens_grad,
        encoder_grad,
        gain_sums[0],
        gain_sums[1],
        gain_sums[2],
        own_table,
        q_done.T,
        kv_done[:inner].T,
        kv_done[inner:].T,
        so_done,
        cq_done.T,
        ckv_done[:inner].T,
        ckv_done[inner:].T,
        co_done,
        gate_grad.T,
        up_grad.T,
        down_grad,
    )


def solution(mesh):
    placed = (
        P((CTX, TP), SHARD, None),
        P(SHARD, None),
        P(None, SHARD, None),
        P(),
        P(),
        P(),
        P(None, TP),
        P((SHARD, CTX), TP),
        P((SHARD, CTX), TP),
        P((SHARD, CTX), TP),
        P(TP, (SHARD, CTX)),
        P((SHARD, CTX), TP),
        P((SHARD, CTX), TP),
        P((SHARD, CTX), TP),
        P(TP, (SHARD, CTX)),
        P((SHARD, CTX), TP),
        P((SHARD, CTX), TP),
        P(TP, (SHARD, CTX)),
        P((CTX, TP), SHARD, None),
    )
    fits = tuple(mesh.shape[axis] for axis in AXES) == (4, 2, 4)
    return jax.shard_map(
        fast_body if fits else body,
        mesh=mesh,
        in_specs=placed,
        out_specs=(
            P((CTX, TP), SHARD, None),
            P((CTX, TP), SHARD, None),
            P(CTX, SHARD, TP),
            P(),
            P(),
            P(),
            P((SHARD, CTX), TP),
            P((SHARD, CTX), TP),
            P((SHARD, CTX), TP),
            P((SHARD, CTX), TP),
            P(TP, (SHARD, CTX)),
            P((SHARD, CTX), TP),
            P((SHARD, CTX), TP),
            P((SHARD, CTX), TP),
            P(TP, (SHARD, CTX)),
            P((SHARD, CTX), TP),
            P((SHARD, CTX), TP),
            P(TP, (SHARD, CTX)),
        ),
        check_vma=False,
    )
```

```python
from functools import partial, reduce

import jax
import jax.numpy as jnp
from jax import lax
from jax.experimental import pallas as pl
from jax.experimental.pallas import tpu as pltpu
from jax.sharding import PartitionSpec as P

MICRO = 4
SHARD, CTX, TP = AXES = ("shard", "ctx", "tp")

BF = jnp.bfloat16
F32 = jnp.float32


def nt(a, b):
    return lax.dot_general(a, b, (((1,), (1,)), ((), ())), preferred_element_type=F32)


def nn(a, b):
    return lax.dot_general(a, b, (((1,), (0,)), ((), ())), preferred_element_type=F32)


def tn(a, b):
    return lax.dot_general(a, b, (((0,), (0,)), ((), ())), preferred_element_type=F32)


def toeplitz(line, half):
    wide = jnp.broadcast_to(line, (half, 2 * half))
    return pltpu.roll(wide, 0, 1, stride=1, stride_axis=0)[:, :half]


def diagonals(tile, half):
    blank = jnp.zeros((8, half), F32)
    total = jnp.zeros((8, 2 * half), F32)
    for at in range(0, half, 8):
        wide = jnp.concatenate([tile[at : at + 8, :], blank], axis=1)
        total = total + (pltpu.roll(wide, 2 * half - at, 1) if at else wide)
    return total


def lane_pick(first, second, left):
    return jnp.where(left, first, second)


def row_softmax(tiles):
    peak = jnp.max(tiles[0], axis=1, keepdims=True)
    for tile in tiles[1:]:
        peak = jnp.maximum(peak, jnp.max(tile, axis=1, keepdims=True))
    exps = [jnp.exp(tile - peak) for tile in tiles]
    total = jnp.sum(reduce_add(exps), axis=1, keepdims=True)
    scale = 1.0 / total
    return [(e * scale).astype(BF) for e in exps], peak + jnp.log(total)


def reduce_add(parts):
    out = parts[0]
    for part in parts[1:]:
        out = out + part
    return out


def self_forward_kernel(core, q, k_own, v_own, k_far, v_far, lines, mask, out, logs):
    half = q.shape[0] // 2
    left = lax.broadcasted_iota(jnp.int32, (1, q.shape[1]), 1) < q.shape[1] // 2
    swapped = core[0] == 1
    a, b = slice(0, half), slice(half, 2 * half)
    outs, totals = [], []
    for head in range(2):
        keep = left if head == 0 else jnp.logical_not(left)
        qh = jnp.where(keep, q[...], jnp.zeros((), BF))
        near = toeplitz(lines[0, 2 * head : 2 * head + 1, :], half)
        next_tile = toeplitz(lines[0, 2 * head + 1 : 2 * head + 2, :], half)
        far = lines[0, 4 + head : 5 + head, :half]
        qa, qb = qh[a], qh[b]
        ka, kb, xa, xb = k_own[a, :], k_own[b, :], k_far[a, :], k_far[b, :]
        pa, la = row_softmax(
            [
                nt(qa, ka) + near + mask[a, 0:half],
                nt(qa, xa) + next_tile + mask[a, 2 * half : 3 * half],
            ]
        )
        oa = nn(pa[0], v_own[a, :]) + nn(pa[1], v_far[a, :])
        pb, lb = row_softmax(
            [
                nt(qb, ka) + jnp.where(swapped, next_tile, far) + mask[b, 0:half],
                nt(qb, kb) + near + mask[b, half : 2 * half],
                nt(qb, xa) + far + mask[b, 2 * half : 3 * half],
                nt(qb, xb) + next_tile + mask[b, 3 * half : 4 * half],
            ]
        )
        ob = (
            nn(pb[0], v_own[a, :])
            + nn(pb[1], v_own[b, :])
            + nn(pb[2], v_far[a, :])
            + nn(pb[3], v_far[b, :])
        )
        outs.append((oa, ob))
        totals.append((la, lb))
    out[a, :] = lane_pick(outs[0][0], outs[1][0], left).astype(BF)
    out[b, :] = lane_pick(outs[0][1], outs[1][1], left).astype(BF)
    for at, piece in ((0, a), (1, b)):
        turned = lane_pick(totals[0][at], totals[1][at], left).T
        logs[0, 0:1, piece] = turned[0:1, :]
        logs[0, 1:2, piece] = turned[q.shape[1] // 2 : q.shape[1] // 2 + 1, :]


def self_backward_kernel(
    core, q, k_own, v_own, k_far, v_far, grad, lines, mask, logs,
    dq, own_out, far_out, sums,
):
    half = q.shape[0] // 2
    left = lax.broadcasted_iota(jnp.int32, (1, q.shape[1]), 1) < q.shape[1] // 2
    swapped = core[0] == 1
    a, b = slice(0, half), slice(half, 2 * half)
    keys = {"oa": (k_own, v_own, a, 0), "ob": (k_own, v_own, b, 1), "xa": (k_far, v_far, a, 2), "xb": (k_far, v_far, b, 3)}
    dk, dv, dqs = {}, {}, [None, None]
    for head in range(2):
        keep = left if head == 0 else jnp.logical_not(left)
        zero = jnp.zeros((), BF)
        qh = jnp.where(keep, q[...], zero)
        gh = jnp.where(keep, grad[...], zero)
        near = toeplitz(lines[0, 2 * head : 2 * head + 1, :], half)
        next_tile = toeplitz(lines[0, 2 * head + 1 : 2 * head + 2, :], half)
        far = lines[0, 4 + head : 5 + head, :half]
        held = {}
        for at, piece, plan in (
            (0, a, (("oa", near), ("xa", next_tile))),
            (1, b, (("oa", jnp.where(swapped, next_tile, far)), ("ob", near), ("xa", far), ("xb", next_tile))),
        ):
            qp, gp = qh[piece], gh[piece]
            total = logs[0, head : head + 1, piece]
            probs, dots = [], []
            for name, bias in plan:
                k, v, rows, slot = keys[name]
                score = nt(k[rows, :], qp) + bias + mask[slot * half : (slot + 1) * half, piece]
                probs.append(jnp.exp(score - total))
                dots.append(nt(v[rows, :], gp))
            delta = jnp.sum(reduce_add([p * d for p, d in zip(probs, dots)]), axis=0, keepdims=True)
            for (name, _), p, d in zip(plan, probs, dots):
                k, v, rows, slot = keys[name]
                ds = p * (d - delta)
                held[at, name] = ds
                low = ds.astype(BF)
                dvp, dkp = nn(p.astype(BF), gp), nn(low, qp)
                dv[name] = dvp if name not in dv else dv[name] + dvp
                dk[name] = dkp if name not in dk else dk[name] + dkp
                dqp = tn(low, jnp.where(keep, k[rows, :], zero))
                dqs[at] = dqp if dqs[at] is None else dqs[at] + dqp
        base = 32 * head
        sums[0, base : base + 8, :] = diagonals(held[0, "oa"] + held[1, "ob"], half)
        sums[0, base + 8 : base + 16, :] = diagonals(held[0, "xa"] + held[1, "xb"], half)
        sums[0, base + 16 : base + 24, :] = diagonals(held[1, "oa"], half)
        rest = reduce_add([held[1, "xa"][at : at + 8, :] for at in range(0, half, 8)])
        sums[0, base + 24 : base + 32, :] = jnp.concatenate([rest, jnp.zeros_like(rest)], axis=1)
    dq[a, :] = dqs[0].astype(BF)
    dq[b, :] = dqs[1].astype(BF)
    sub = pl.multiple_of(lax.rem(pl.program_id(0), 2) * 128, 128)
    for name, ref, rows in (("oa", own_out, a), ("ob", own_out, b), ("xa", far_out, a), ("xb", far_out, b)):
        ref[rows, pl.ds(sub, 128)] = dk[name].astype(BF)
        ref[rows, pl.ds(sub + 256, 128)] = dv[name].astype(BF)


def self_specs(rows):
    kv = lambda which: (lambda p, c: (0, (p // 2) * 4 + which * 2 + p % 2))
    q = pl.BlockSpec((rows, 128), lambda p, c: (0, p))
    k = pl.BlockSpec((rows, 128), kv(0))
    v = pl.BlockSpec((rows, 128), kv(1))
    small = pl.BlockSpec((1, 8, rows), lambda p, c: (p, 0, 0))
    return q, k, v, small


def self_forward(core, q, kv_own, kv_far, lines, mask):
    rows, width = q.shape
    pairs = width // 128
    qs, ks, vs, small = self_specs(rows)
    return pl.pallas_call(
        self_forward_kernel,
        grid_spec=pltpu.PrefetchScalarGridSpec(
            num_scalar_prefetch=1,
            grid=(pairs,),
            in_specs=[qs, ks, vs, ks, vs, small, pl.BlockSpec((rows, 2 * rows), lambda p, c: (0, 0))],
            out_specs=[qs, small],
        ),
        out_shape=(
            jax.ShapeDtypeStruct((rows, width), BF),
            jax.ShapeDtypeStruct((pairs, 8, rows), F32),
        ),
        cost_estimate=pl.CostEstimate(flops=pairs * 24 * 65536 * 128 * 2, bytes_accessed=10 << 20, transcendentals=0),
        name="self_fwd",
    )(core, q, kv_own, kv_own, kv_far, kv_far, lines, mask)


def self_backward(core, q, kv_own, kv_far, grad, lines, mask_t, logs):
    rows, width = q.shape
    pairs = width // 128
    qs, ks, vs, small = self_specs(rows)
    wide = pl.BlockSpec((rows, 512), lambda p, c: (0, p // 2))
    return pl.pallas_call(
        self_backward_kernel,
        grid_spec=pltpu.PrefetchScalarGridSpec(
            num_scalar_prefetch=1,
            grid=(pairs,),
            in_specs=[qs, ks, vs, ks, vs, qs, small, pl.BlockSpec((2 * rows, rows), lambda p, c: (0, 0)), small],
            out_specs=[qs, wide, wide, pl.BlockSpec((1, 64, rows), lambda p, c: (p, 0, 0))],
        ),
        out_shape=(
            jax.ShapeDtypeStruct((rows, width), BF),
            jax.ShapeDtypeStruct((rows, 2 * width), BF),
            jax.ShapeDtypeStruct((rows, 2 * width), BF),
            jax.ShapeDtypeStruct((pairs, 64, rows), F32),
        ),
        cost_estimate=pl.CostEstimate(flops=pairs * 60 * 65536 * 128 * 2, bytes_accessed=20 << 20, transcendentals=0),
        name="self_bwd",
    )(core, q, kv_own, kv_own, kv_far, kv_far, grad, lines, mask_t, logs)


def cross_forward_kernel(q, k, v, out, logs):
    left = lax.broadcasted_iota(jnp.int32, (1, q.shape[1]), 1) < q.shape[1] // 2
    outs, totals = [], []
    for head in range(2):
        keep = left if head == 0 else jnp.logical_not(left)
        qh = jnp.where(keep, q[...], jnp.zeros((), BF))
        p, total = row_softmax([nt(qh, k[...])])
        outs.append(nn(p[0], v[...]))
        totals.append(total)
    out[...] = lane_pick(outs[0], outs[1], left).astype(BF)
    turned = lane_pick(totals[0], totals[1], left).T
    logs[0, 0:1, :] = turned[0:1, :]
    logs[0, 1:2, :] = turned[q.shape[1] // 2 : q.shape[1] // 2 + 1, :]


def cross_backward_kernel(q, k, v, grad, logs, dq, out):
    left = lax.broadcasted_iota(jnp.int32, (1, q.shape[1]), 1) < q.shape[1] // 2
    dqs = dks = dvs = None
    zero = jnp.zeros((), BF)
    for head in range(2):
        keep = left if head == 0 else jnp.logical_not(left)
        qh = jnp.where(keep, q[...], zero)
        gh = jnp.where(keep, grad[...], zero)
        p = jnp.exp(nt(k[...], qh) - logs[0, head : head + 1, :])
        d = nt(v[...], gh)
        delta = jnp.sum(p * d, axis=0, keepdims=True)
        low = (p * (d - delta)).astype(BF)
        dvp, dkp, dqp = nn(p.astype(BF), gh), nn(low, qh), tn(low, jnp.where(keep, k[...], zero))
        dqs = dqp if dqs is None else dqs + dqp
        dks = dkp if dks is None else dks + dkp
        dvs = dvp if dvs is None else dvs + dvp
    dq[...] = dqs.astype(BF)
    sub = pl.multiple_of(lax.rem(pl.program_id(0), 2) * 128, 128)
    out[:, pl.ds(sub, 128)] = dks.astype(BF)
    out[:, pl.ds(sub + 256, 128)] = dvs.astype(BF)


def cross_specs(rows, states):
    kv = lambda which: (lambda p: (0, (p // 2) * 4 + which * 2 + p % 2))
    q = pl.BlockSpec((rows, 128), lambda p: (0, p))
    k = pl.BlockSpec((states, 128), kv(0))
    v = pl.BlockSpec((states, 128), kv(1))
    small = pl.BlockSpec((1, 8, rows), lambda p: (p, 0, 0))
    return q, k, v, small


def cross_forward(q, kv):
    rows, width = q.shape
    states = kv.shape[0]
    pairs = width // 128
    qs, ks, vs, small = cross_specs(rows, states)
    return pl.pallas_call(
        cross_forward_kernel,
        grid=(pairs,),
        in_specs=[qs, ks, vs],
        out_specs=[qs, small],
        out_shape=(
            jax.ShapeDtypeStruct((rows, width), BF),
            jax.ShapeDtypeStruct((pairs, 8, rows), F32),
        ),
        cost_estimate=pl.CostEstimate(flops=pairs * 8 * rows * states * 128, bytes_accessed=4 << 20, transcendentals=0),
        name="cross_fwd",
    )(q, kv, kv)


def cross_backward(q, kv, grad, logs):
    rows, width = q.shape
    states = kv.shape[0]
    pairs = width // 128
    qs, ks, vs, small = cross_specs(rows, states)
    return pl.pallas_call(
        cross_backward_kernel,
        grid=(pairs,),
        in_specs=[qs, ks, vs, qs, small],
        out_specs=[qs, pl.BlockSpec((states, 512), lambda p: (0, p // 2))],
        out_shape=(
            jax.ShapeDtypeStruct((rows, width), BF),
            jax.ShapeDtypeStruct((states, 2 * width), BF),
        ),
        cost_estimate=pl.CostEstimate(flops=pairs * 20 * rows * states * 128, bytes_accessed=6 << 20, transcendentals=0),
        name="cross_bwd",
    )(q, kv, kv, grad, logs)


def staged_kernel(body, weights, n_blocks, n_tiled, n_whole, n_out, *refs):
    core_refs = refs[:n_blocks]
    at = n_blocks
    tiled, at = refs[at : at + n_tiled], at + n_tiled
    whole, at = refs[at : at + n_whole], at + n_whole
    outs, at = refs[at : at + n_out], at + n_out
    held, sems = refs[at : at + len(weights)], refs[at + len(weights) :]
    first = pl.program_id(0) == 0
    copies = []
    for (colors, start, size), store, sem in zip(weights, held, sems):
        own = []
        for color, blocks in enumerate(colors):
            for slot, block in enumerate(blocks):
                own.append(
                    pltpu.make_async_copy(
                        core_refs[block].at[:, start : start + size, :],
                        store.at[:, color * size : (color + 1) * size, slot * 128 : (slot + 1) * 128],
                        sem.at[color * 8 + slot],
                    )
                )
        copies.append(own)

    @pl.when(first)
    def _():
        for own in copies:
            for copy in own:
                copy.start()

    ready = set()

    def weight(which):
        if which not in ready:
            ready.add(which)

            @pl.when(first)
            def _():
                for copy in copies[which]:
                    copy.wait()

        value = held[which][...]
        return value.reshape(-1, value.shape[-1])

    body(first, weight, tiled, whole, outs)


def staged(body, weights, tiled, whole, out_types, tile, flops):
    flat, index = [], {}
    plan = []
    for colors, start, size in weights:
        for blocks in colors:
            for block in blocks:
                if id(block) not in index:
                    index[id(block)] = len(flat)
                    flat.append(block)
        plan.append(([[index[id(b)] for b in blocks] for blocks in colors], start, size))
    rows = tiled[0].shape[0]

    def tile_spec(shape):
        return pl.BlockSpec((tile, shape[1]), lambda m: (m, 0))

    def whole_spec(shape):
        return pl.BlockSpec(shape, lambda m: (0,) * len(shape))

    out_specs, out_shapes = [], []
    for shape, dtype in out_types:
        out_shapes.append(jax.ShapeDtypeStruct(shape, dtype))
        if len(shape) == 3:
            out_specs.append(pl.BlockSpec((shape[0], tile, shape[2]), lambda m: (0, m, 0)))
        else:
            out_specs.append(tile_spec(shape) if shape[0] == rows else whole_spec(shape))
    nbytes = sum(v.size * v.dtype.itemsize for v in (*flat, *tiled, *whole))
    return pl.pallas_call(
        partial(staged_kernel, body, plan, len(flat), len(tiled), len(whole), len(out_types)),
        grid=(rows // tile,),
        in_specs=[pl.BlockSpec(memory_space=pl.ANY)] * len(flat)
        + [tile_spec(v.shape) for v in tiled]
        + [whole_spec(v.shape) for v in whole],
        out_specs=out_specs,
        out_shape=out_shapes,
        scratch_shapes=[
            pltpu.VMEM((4, len(colors) * size, 1024), BF) for colors, start, size in plan
        ]
        + [pltpu.SemaphoreType.DMA((8 * len(colors),)) for colors, start, size in plan],
        cost_estimate=pl.CostEstimate(flops=flops, bytes_accessed=nbytes, transcendentals=0),
    )(*flat, *tiled, *whole)


def unit(h):
    return lax.rsqrt(jnp.mean(h * h, axis=-1, keepdims=True) + epsilon)


def normed(h, gain):
    return (h * unit(h) * gain).astype(BF)


def norm_pull(h, gain, grad):
    scale = unit(h)
    inner = gain * grad
    mean = jnp.mean(inner * h, axis=-1, keepdims=True)
    back = scale * inner - h * (scale * scale * scale) * mean
    return back, jnp.sum(grad * h * scale, axis=0, keepdims=True)


def add_up(first, out, value):
    @pl.when(first)
    def _():
        out[...] = value

    @pl.when(jnp.logical_not(first))
    def _():
        out[...] = out[...] + value


def kv_body(first, weight, tiled, whole, outs):
    n = normed(tiled[0][...].astype(F32), whole[0][...])
    outs[0][...] = n
    outs[1][...] = nt(n, weight(0)).astype(BF)


def nt_body(first, weight, tiled, whole, outs):
    outs[0][...] = nt(tiled[0][...], weight(0)).astype(BF)


def nn_body(first, weight, tiled, whole, outs):
    outs[0][...] = nn(tiled[0][...], weight(0)).astype(BF)


def mid_body(first, weight, tiled, whole, outs):
    mixed, resid = tiled
    after = resid[...].astype(F32) + nn(mixed[...], weight(0))
    outs[0][...] = after
    n = normed(after, whole[0][...])
    outs[1][...] = n
    if len(outs) > 2:
        outs[2][...] = nt(n, weight(1)).astype(BF)


GELU_SCALE = (2.0 / 3.141592653589793) ** 0.5


def feed_body(first, weight, tiled, whole, outs):
    n, g, before, grad_before = tiled
    sides_out, after_out, normed_out = outs
    gate = nt(n[...], weight(0))
    up = nt(n[...], weight(1))
    square = gate * gate
    wave = jnp.tanh(GELU_SCALE * gate * (1.0 + 0.044715 * square))
    soft = 0.5 * (1.0 + wave)
    act = gate * soft
    hidden = (act * up).astype(BF)
    sides_out[2] = hidden
    after_out[...] = (before[...].astype(F32) + nn(hidden, weight(2))).astype(after_out.dtype)
    grad = nt(g[...], weight(2))
    slope = soft + 0.5 * gate * (1.0 - wave * wave) * (GELU_SCALE * (1.0 + 3 * 0.044715 * square))
    grad_gate = (grad * up * slope).astype(BF)
    grad_up = (grad * act).astype(BF)
    sides_out[0] = grad_gate
    sides_out[1] = grad_up
    normed_out[...] = grad_before[...] + nn(grad_gate, weight(0)) + nn(grad_up, weight(1))


def turn_body(first, weight, tiled, whole, outs):
    h, grad_normed, grad_out = tiled
    back, gain_part = norm_pull(h[...], whole[0][...], grad_normed[...])
    total = grad_out[...].astype(F32) + back
    low = total.astype(BF)
    outs[0][...] = total
    outs[1][...] = low
    outs[2][...] = nt(low, weight(0)).astype(BF)
    add_up(first, outs[3], gain_part)


def second_turn_body(first, weight, tiled, whole, outs):
    grad_query, h, grad_out = tiled
    back, gain_part = norm_pull(h[...], whole[0][...], nn(grad_query[...], weight(0)))
    total = grad_out[...].astype(F32) + back
    low = total.astype(BF)
    outs[0][...] = total
    outs[1][...] = low
    outs[2][...] = nt(low, weight(1)).astype(BF)
    add_up(first, outs[3], gain_part)


def last_body(first, weight, tiled, whole, outs):
    grad_query, grad_kv, h, grad_out = tiled
    grad_normed = nn(grad_query[...], weight(0)) + nn(grad_kv[...], weight(1))
    back, gain_part = norm_pull(h[...].astype(F32), whole[0][...], grad_normed)
    outs[0][...] = (grad_out[...] + back).astype(BF)
    add_up(first, outs[1], gain_part)


def grads_kernel(size, ways, kept, two, *refs):
    n_colors = len(ways)
    last = pl.program_id(0) == pl.num_programs(0) - 1
    if two:
        rows_grad = jnp.where(last, refs[1][...], refs[0][...])
    else:
        rows_grad = refs[0][0]
    refs = refs[1 + two :]
    came = refs[2 : 2 + n_colors] if kept else ()
    outs = refs[2 + len(came) :]
    value = tn(rows_grad, jnp.where(last, refs[1][...], refs[0][...]))
    for color, bit in enumerate(ways):
        for z in range(4):
            row = (z * n_colors + color) * size
            piece = value[row : row + size]
            for at in range(4):
                part = piece[:, at * 128 : (at + 1) * 128]
                if not kept:
                    outs[color][at, z] = part.astype(BF)
                    continue
                part = (part + came[color][at, z].astype(F32)).astype(BF)
                if at & bit:
                    outs[2 * color][at // 3, z] = part
                else:
                    outs[2 * color + 1][min(at, 1), z] = part


def weight_grads(rows_grad, first_in, second_in, size, ways, came=None):
    two = isinstance(rows_grad, tuple)
    if two:
        (rows, inner), count = rows_grad[0].shape, 2
        sources = list(rows_grad)
        source_specs = [pl.BlockSpec((rows, inner), lambda w: (0, 0))] * 2
    else:
        count, rows, inner = rows_grad.shape
        sources = [rows_grad]
        source_specs = [pl.BlockSpec((1, rows, inner), lambda w: (w, 0, 0))]
    kept = came is not None
    slab = pl.BlockSpec((4, 4, size, 128), lambda w: (0, 0, w, 0))
    pair = pl.BlockSpec((2, 4, size, 128), lambda w: (0, 0, w, 0))
    side = pl.BlockSpec((rows, 512), lambda w: (0, 0 if kept else 1))
    if kept:
        out_specs = [pair] * (2 * len(ways))
        out_shape = [jax.ShapeDtypeStruct((2, 4, count * size, 128), BF)] * (2 * len(ways))
    else:
        out_specs = [slab] * len(ways)
        out_shape = [jax.ShapeDtypeStruct((4, 4, count * size, 128), BF)] * len(ways)
    extra = list(came) if kept else []
    return pl.pallas_call(
        partial(grads_kernel, size, ways, kept, two),
        grid=(count,),
        in_specs=source_specs + [side, side] + [slab] * len(extra),
        out_specs=out_specs,
        out_shape=out_shape,
        cost_estimate=pl.CostEstimate(
            flops=2 * count * rows * inner * 512,
            bytes_accessed=2 * count * inner * (rows + 1024),
            transcendentals=0,
        ),
    )(*sources, first_in, second_in, *extra)


def near_sum_kernel(*refs):
    count = len(refs) // 3
    for at in range(count):
        refs[2 * count + at][...] = refs[2 * at][0] + refs[2 * at + 1][0]


def near_sums(kept, came):
    shape = kept[0].shape
    second = pl.BlockSpec((1, *shape[1:]), lambda m: (1, 0, 0, 0))
    out = pl.BlockSpec(shape[1:], lambda m: (0, 0, 0))
    operands = [v for both in zip(kept, came) for v in both]
    return pl.pallas_call(
        near_sum_kernel,
        grid=(1,),
        in_specs=[second] * len(operands),
        out_specs=[out] * len(kept),
        out_shape=[jax.ShapeDtypeStruct(shape[1:], BF)] * len(kept),
        cost_estimate=pl.CostEstimate(flops=0, bytes_accessed=6 * kept[0].size, transcendentals=0),
        name="s1",
    )(*operands)


def far_sum_kernel(*refs):
    out = refs[-1]
    count = len(refs) // 3
    size = out.shape[1] // count
    for at in range(count):
        total = refs[3 * at][0].astype(F32) + refs[3 * at + 1][0].astype(F32)
        total = total + refs[3 * at + 2][...].astype(F32)
        out[:, at * size : (at + 1) * size, :] = total.astype(BF)


def far_sums(kept, came, last):
    shape = kept[0].shape
    first = pl.BlockSpec((1, *shape[1:]), lambda m: (0, 0, 0, 0))
    whole = pl.BlockSpec(shape[1:], lambda m: (0, 0, 0))
    operands = [v for both in zip(kept, came, last) for v in both]
    total = (shape[1], shape[2] * len(kept), shape[3])
    return pl.pallas_call(
        far_sum_kernel,
        grid=(1,),
        in_specs=[first, first, whole] * len(kept),
        out_specs=pl.BlockSpec(total, lambda m: (0, 0, 0)),
        out_shape=jax.ShapeDtypeStruct(total, BF),
        cost_estimate=pl.CostEstimate(flops=0, bytes_accessed=8 * kept[0].size, transcendentals=0),
        name="s2",
    )(*operands)


def gather_rows_kernel(place, *refs):
    got, out, sem = refs[:4], refs[4], refs[5]
    sx, core, y, z = place[0], place[1], place[2], place[3]
    copies = []
    for step in range(4):
        row = pl.multiple_of(lax.rem(z + 4 - step, 4) ^ (2 * core), 1) * 128
        for at in range(8):
            lane = 128 * ((((at >> 1) & 1) ^ sx) * 4 + ((at >> 2) ^ core) * 2 + ((at & 1) ^ y))
            copies.append(
                pltpu.make_async_copy(
                    got[step].at[:, pl.ds(pl.multiple_of(lane, 128), 128)],
                    out.at[pl.ds(pl.multiple_of(row, 128), 128), at * 128 : (at + 1) * 128],
                    sem.at[step * 8 + at],
                )
            )
    for copy in copies:
        copy.start()
    for copy in copies:
        copy.wait()


def gather_rows_call(place, got):
    rows, width = got[0].shape
    return pl.pallas_call(
        gather_rows_kernel,
        grid_spec=pltpu.PrefetchScalarGridSpec(
            num_scalar_prefetch=1,
            grid=(1,),
            in_specs=[pl.BlockSpec(memory_space=pl.ANY)] * 4,
            out_specs=pl.BlockSpec((4 * rows, width), lambda m, p: (0, 0)),
            scratch_shapes=[pltpu.SemaphoreType.DMA((32,))],
        ),
        out_shape=jax.ShapeDtypeStruct((4 * rows, width), got[0].dtype),
        cost_estimate=pl.CostEstimate(flops=0, bytes_accessed=16 * rows * width, transcendentals=0),
        name="rows_in",
    )(place, *got)


def scatter_rows_kernel(place, rows_ref, *refs):
    outs, sem = refs[:4], refs[4]
    sx, core, y, z = place[0], place[1], place[2], place[3]
    copies = []
    for step in range(4):
        row = (lax.rem(z + 4 - step, 4) ^ (2 * core)) * 128
        for at in range(8):
            lane = 128 * ((((at >> 1) & 1) ^ sx) * 4 + ((at >> 2) ^ core) * 2 + ((at & 1) ^ y))
            copies.append(
                pltpu.make_async_copy(
                    rows_ref.at[pl.ds(pl.multiple_of(row, 128), 128), at * 128 : (at + 1) * 128],
                    outs[step].at[:, pl.ds(pl.multiple_of(lane, 128), 128)],
                    sem.at[step * 8 + at],
                )
            )
    for copy in copies:
        copy.start()
    for copy in copies:
        copy.wait()


def scatter_rows_call(place, rows_in):
    rows, width = rows_in.shape
    part = jax.ShapeDtypeStruct((rows // 4, width), rows_in.dtype)
    return pl.pallas_call(
        scatter_rows_kernel,
        grid_spec=pltpu.PrefetchScalarGridSpec(
            num_scalar_prefetch=1,
            grid=(1,),
            in_specs=[pl.BlockSpec(memory_space=pl.ANY)],
            out_specs=[pl.BlockSpec((rows // 4, width), lambda m, p: (0, 0))] * 4,
            scratch_shapes=[pltpu.SemaphoreType.DMA((32,))],
        ),
        out_shape=[part] * 4,
        cost_estimate=pl.CostEstimate(flops=0, bytes_accessed=4 * rows * width, transcendentals=0),
        name="rows_out",
    )(place, rows_in)


epsilon = 1e-06
masked_score = -1000000000.0
bucket_edges = (19, 21, 24, 27, 31, 35, 40, 46, 52, 59, 67, 77, 87, 99, 113)


def from_behind(x, axis, by):
    peers = lax.axis_size(axis)
    pairs = [(i, i + by) for i in range(peers) if 0 <= i + by < peers]
    return lax.ppermute(x, axis, pairs)


def bucket_index(distance):
    distance = jnp.maximum(distance, 0)
    far_bucket = reduce(
        lambda running, threshold: running + (distance >= threshold).astype(jnp.int32),
        bucket_edges,
        jnp.full(distance.shape, 16, jnp.int32),
    )
    return jnp.where(distance < 16, distance, far_bucket)


def rms_scale(hidden_in):
    return lax.rsqrt(jnp.mean(hidden_in * hidden_in, axis=-1, keepdims=True) + epsilon)


def norm_back(hidden_in, gain_vec, grad_in):
    inv_scale = rms_scale(hidden_in)
    scaled_grad = gain_vec * grad_in
    inner_mean = jnp.mean(scaled_grad * hidden_in, axis=-1, keepdims=True)
    grad_back = (
        inv_scale * scaled_grad - hidden_in * (inv_scale * inv_scale * inv_scale) * inner_mean
    )
    gain_part = jnp.sum(grad_in * hidden_in * inv_scale, axis=(0, 1))
    return (grad_back, gain_part)


def soft_rows(scores):
    peak = jnp.max(scores, axis=-1, keepdims=True)
    exp_scores = jnp.exp(scores - peak)
    row_total = jnp.sum(exp_scores, axis=-1, keepdims=True)
    return (exp_scores / row_total, peak + jnp.log(row_total))


def soft_back(attn_probs, grad_probs):
    return attn_probs * (grad_probs - jnp.sum(attn_probs * grad_probs, axis=-1, keepdims=True))


def spread_bias(bias_line, row_count, col_count):
    row_width = row_count + col_count
    head_total = bias_line.shape[0]
    tiled_line = jnp.tile(bias_line, (1, row_count))[:, : row_count * row_width]
    return tiled_line.reshape(head_total, row_count, row_width)[:, :, :col_count]


def fold_bias(score_grid, row_count, col_count):
    row_width = row_count + col_count
    head_total = score_grid.shape[0]
    padded = jnp.pad(score_grid, ((0, 0), (0, 0), (0, row_count))).reshape(
        head_total, row_count * row_width
    )
    padded = jnp.pad(padded, ((0, 0), (0, row_count))).reshape(head_total, row_count, row_width + 1)
    return jnp.sum(padded, axis=1)


def gather_rows(normed):
    return lax.all_gather(normed, TP, axis=0, tiled=True)


def gather_grads(grad_in):
    return lax.all_gather(grad_in, TP, axis=0, tiled=True)


def branch_sum(input_values, input_weight):
    return lax.psum_scatter(
        jnp.einsum("gci,iu->gcu", input_values, input_weight, preferred_element_type=jnp.float32),
        TP,
        scatter_dimension=0,
        tiled=True,
    )


def input_sum(incoming_gradients, input_weight):
    return lax.psum_scatter(
        jnp.einsum(
            "iyv,mv->iym", incoming_gradients, input_weight, preferred_element_type=jnp.float32
        ),
        TP,
        scatter_dimension=0,
        tiled=True,
    )


def cross_scores(queries_in, states_kv, head_count):
    local_len, seq_count, head_width = queries_in.shape
    state_len = states_kv.shape[0]
    queries_h = queries_in.reshape(local_len, seq_count, head_count, -1)
    keys_h = states_kv[..., :head_width].reshape(state_len, seq_count, head_count, -1)
    values_h = states_kv[..., head_width:].reshape(state_len, seq_count, head_count, -1)
    scores = jnp.einsum("qshe,kshe->shqk", queries_h, keys_h, preferred_element_type=jnp.float32)
    return (scores, queries_h, keys_h, values_h)


def micro_step(
    tokens, segments, encoder, cotangent, norm_self, norm_cross, norm_ffn, rel_table, shards
):
    gathered = (
        lax.all_gather(shards[0], (SHARD, CTX), axis=0, tiled=True),
        lax.all_gather(shards[1], (SHARD, CTX), axis=0, tiled=True),
        lax.all_gather(shards[2], (SHARD, CTX), axis=0, tiled=True),
        lax.all_gather(shards[3], (SHARD, CTX), axis=1, tiled=True),
        lax.all_gather(shards[4], (SHARD, CTX), axis=0, tiled=True),
        lax.all_gather(shards[5], (SHARD, CTX), axis=0, tiled=True),
        lax.all_gather(shards[6], (SHARD, CTX), axis=0, tiled=True),
        lax.all_gather(shards[7], (SHARD, CTX), axis=1, tiled=True),
        lax.all_gather(shards[8], (SHARD, CTX), axis=0, tiled=True),
        lax.all_gather(shards[9], (SHARD, CTX), axis=0, tiled=True),
        lax.all_gather(shards[10], (SHARD, CTX), axis=1, tiled=True),
    )
    (
        w_query,
        w_key,
        w_value,
        output_weight,
        cross_query_weight,
        c_key,
        c_value,
        cross_output_weight,
        w_gate,
        w_up,
        down_weight,
    ) = gathered
    own_rows = tokens.shape[0]
    seq_count = tokens.shape[1]
    local_len = own_rows * lax.axis_size(TP)
    window_len = 3 * local_len
    period = window_len + local_len + 1
    head_count = rel_table.shape[1]
    head_width = w_query.shape[1]
    feed_width = w_gate.shape[1]
    ctx_index = lax.axis_index(CTX)
    fill_ids = jnp.full((seq_count, 2 * local_len), -1, jnp.int32)
    seg_padded = jnp.concatenate([fill_ids, segments], axis=1)
    seg_window = lax.dynamic_slice_in_dim(seg_padded, ctx_index * local_len, window_len, 1)
    seg_query = lax.dynamic_slice_in_dim(segments, ctx_index * local_len, local_len, 1)
    offsets = jnp.arange(period, dtype=jnp.int32)
    distance = jnp.where(
        offsets < window_len, 2 * local_len - offsets, 2 * local_len - offsets + period
    )
    one_hot = (
        bucket_index(distance)[:, None] == jnp.arange(rel_table.shape[0], dtype=jnp.int32)[None, :]
    ).astype(jnp.float32)
    bias_line = jnp.dot(
        one_hot, rel_table, precision=lax.Precision.HIGHEST, preferred_element_type=jnp.float32
    ).T
    rel_bias = spread_bias(bias_line, local_len, window_len)
    causal_ok = (
        jnp.arange(window_len, dtype=jnp.int32)[None, :]
        <= jnp.arange(local_len, dtype=jnp.int32)[:, None] + 2 * local_len
    )

    def self_scores(one_query, one_window, query_ids, window_ids):
        queries_h = one_query.reshape(local_len, head_count, -1)
        keys_h = one_window[:, :head_width].reshape(window_len, head_count, -1)
        values_h = one_window[:, head_width:].reshape(window_len, head_count, -1)
        scores = (
            jnp.einsum("qhe,khe->hqk", queries_h, keys_h, preferred_element_type=jnp.float32)
            + rel_bias
        )
        allowed = (query_ids[:, None] == window_ids[None, :]) & causal_ok
        return (jnp.where(allowed[None], scores, masked_score), queries_h, keys_h, values_h)

    def self_forward(items):
        one_query, one_window, query_ids, window_ids = items
        scores, _, _, values_h = self_scores(one_query, one_window, query_ids, window_ids)
        attn_probs, log_total = soft_rows(scores)
        block_out = jnp.einsum(
            "hqk,khe->qhe",
            attn_probs.astype(jnp.bfloat16),
            values_h,
            preferred_element_type=jnp.float32,
        )
        return (block_out.reshape(local_len, head_width), log_total)

    def self_backward(items):
        one_query, one_window, query_ids, window_ids, log_total, grad_out = items
        scores, queries_h, keys_h, values_h = self_scores(
            one_query, one_window, query_ids, window_ids
        )
        attn_probs = jnp.exp(scores - log_total)
        grad_heads = grad_out.reshape(local_len, head_count, -1)
        grad_values = jnp.einsum(
            "hqk,qhe->khe",
            attn_probs.astype(jnp.bfloat16),
            grad_heads,
            preferred_element_type=jnp.float32,
        )
        grad_probs = jnp.einsum(
            "qhe,khe->hqk", grad_heads, values_h, preferred_element_type=jnp.float32
        )
        grad_scores = soft_back(attn_probs, grad_probs)
        grad_line = fold_bias(grad_scores, local_len, window_len)
        grad_low = grad_scores.astype(jnp.bfloat16)
        grad_queries = jnp.einsum(
            "hqk,khe->qhe", grad_low, keys_h, preferred_element_type=jnp.float32
        )
        grad_keys = jnp.einsum(
            "hqk,qhe->khe", grad_low, queries_h, preferred_element_type=jnp.float32
        )
        grad_pair = jnp.concatenate(
            [
                grad_keys.reshape(window_len, head_width),
                grad_values.reshape(window_len, head_width),
            ],
            axis=-1,
        )
        return (grad_queries.reshape(local_len, head_width), grad_pair, grad_line)

    resid_in = tokens.astype(jnp.float32)
    normed_one = (resid_in * rms_scale(resid_in) * norm_self).astype(jnp.bfloat16)
    first_rows = gather_rows(normed_one)
    self_attention_weight = jnp.concatenate([w_query, w_key, w_value], axis=1)
    projected = jnp.einsum(
        "rmh,ha->rma", first_rows, self_attention_weight, preferred_element_type=jnp.float32
    ).astype(jnp.bfloat16)
    queries = projected[..., :head_width]
    key_value = projected[..., head_width:]
    earlier = [from_behind(key_value, CTX, offset) for offset in (2, 1)]
    window = jnp.concatenate(earlier + [key_value], axis=0)
    seq_queries = jnp.moveaxis(queries, 1, 0)
    seq_window = jnp.moveaxis(window, 1, 0)
    self_mixed, self_logs = lax.map(self_forward, (seq_queries, seq_window, seg_query, seg_window))
    attended_rows = jnp.moveaxis(self_mixed, 0, 1).astype(jnp.bfloat16)
    after_self = resid_in + branch_sum(attended_rows, output_weight)
    normed_two = (after_self * rms_scale(after_self) * norm_cross).astype(jnp.bfloat16)
    second_rows = gather_rows(normed_two)
    cross_q = jnp.einsum(
        "rmh,ha->rma", second_rows, cross_query_weight, preferred_element_type=jnp.float32
    ).astype(jnp.bfloat16)
    state_weight = jnp.concatenate([c_key, c_value], axis=1)
    cross_kv = jnp.einsum(
        "rsd,df->rsf", encoder, state_weight, preferred_element_type=jnp.float32
    ).astype(jnp.bfloat16)
    scores, queries_h, keys_h, values_h = cross_scores(cross_q, cross_kv, head_count)
    attn_probs, cross_logs = soft_rows(scores)
    cross_mix = jnp.einsum(
        "shqk,kshe->qshe",
        attn_probs.astype(jnp.bfloat16),
        values_h,
        preferred_element_type=jnp.float32,
    )
    cross_attended = cross_mix.reshape(local_len, seq_count, head_width).astype(jnp.bfloat16)
    after_cross = after_self + branch_sum(cross_attended, cross_output_weight)
    normed_three = (after_cross * rms_scale(after_cross) * norm_ffn).astype(jnp.bfloat16)
    third_rows = gather_rows(normed_three)
    feedforward_weight = jnp.concatenate([w_gate, w_up], axis=1)
    gate_up_product = jnp.einsum(
        "rmh,ha->rma", third_rows, feedforward_weight, preferred_element_type=jnp.float32
    )
    gate_pre = gate_up_product[..., :feed_width]
    up_pre = gate_up_product[..., feed_width:]
    hidden_rows = (jax.nn.gelu(gate_pre, approximate=True) * up_pre).astype(jnp.bfloat16)
    result = after_cross + branch_sum(hidden_rows, down_weight)
    grad_result = cotangent.astype(jnp.float32)
    feedforward_gradient = gather_grads(grad_result.astype(jnp.bfloat16))
    feedforward_down_gradient = jnp.einsum(
        "euy,euh->yh", hidden_rows, feedforward_gradient, preferred_element_type=jnp.float32
    )
    hidden_gradient = jnp.einsum(
        "ezk,ck->ezc", feedforward_gradient, down_weight, preferred_element_type=jnp.float32
    )
    _, feed_pull = jax.vjp(
        lambda gate_in, up_in: jax.nn.gelu(gate_in, approximate=True) * up_in, gate_pre, up_pre
    )
    grad_gate, grad_up = feed_pull(hidden_gradient)
    gate_up_gradient = jnp.concatenate([grad_gate, grad_up], axis=-1).astype(jnp.bfloat16)
    feed_grads = jnp.einsum(
        "zvn,zvp->np", third_rows, gate_up_gradient, preferred_element_type=jnp.float32
    )
    ffn_gate_grad = feed_grads[:, :feed_width]
    ffn_up_grad = feed_grads[:, feed_width:]
    ffn_sums = None
    grad_back_three, gain_three = norm_back(
        after_cross, norm_ffn, input_sum(gate_up_gradient, feedforward_weight)
    )
    grad_mid = grad_result + grad_back_three
    cross_gradient = gather_grads(grad_mid.astype(jnp.bfloat16))
    cross_out_grad = jnp.einsum(
        "euy,euh->yh", cross_attended, cross_gradient, preferred_element_type=jnp.float32
    )
    grad_crossed = jnp.einsum(
        "ezk,ck->ezc", cross_gradient, cross_output_weight, preferred_element_type=jnp.float32
    ).astype(jnp.bfloat16)
    grad_heads = grad_crossed.reshape(local_len, seq_count, head_count, -1)
    cross_probs = jnp.exp(scores - cross_logs)
    grad_cvalues = jnp.einsum(
        "shqk,qshe->kshe",
        cross_probs.astype(jnp.bfloat16),
        grad_heads,
        preferred_element_type=jnp.float32,
    )
    grad_probs = jnp.einsum(
        "qshe,kshe->shqk", grad_heads, values_h, preferred_element_type=jnp.float32
    )
    grad_low = soft_back(cross_probs, grad_probs).astype(jnp.bfloat16)
    cross_query_weight_gradient = jnp.einsum(
        "shqk,kshe->qshe", grad_low, keys_h, preferred_element_type=jnp.float32
    )
    cross_query_weight_gradient = cross_query_weight_gradient.reshape(
        local_len, seq_count, head_width
    ).astype(jnp.bfloat16)
    grad_ckeys = jnp.einsum(
        "shqk,qshe->kshe", grad_low, queries_h, preferred_element_type=jnp.float32
    )
    state_len = encoder.shape[0]
    grad_ckv = jnp.concatenate(
        [
            grad_ckeys.reshape(state_len, seq_count, head_width),
            grad_cvalues.reshape(state_len, seq_count, head_width),
        ],
        axis=-1,
    )
    grad_ckv_own = lax.psum_scatter(
        grad_ckv.astype(jnp.bfloat16), CTX, scatter_dimension=0, tiled=True
    )
    state_rows = grad_ckv_own.shape[0]
    states_own = lax.dynamic_slice_in_dim(encoder, ctx_index * state_rows, state_rows, 0)
    state_grads = jnp.einsum(
        "rsd,rsf->df", states_own, grad_ckv_own, preferred_element_type=jnp.float32
    )
    cross_key_grad = state_grads[:, :head_width]
    cross_value_grad = state_grads[:, head_width:]
    state_term = jnp.einsum(
        "rsf,df->rsd", grad_ckv_own, state_weight, preferred_element_type=jnp.float32
    )
    encoder_grad = lax.psum_scatter(
        state_term.astype(jnp.bfloat16), TP, scatter_dimension=2, tiled=True
    ).astype(jnp.float32)
    cross_query_grad = jnp.einsum(
        "zvn,zvp->np", second_rows, cross_query_weight_gradient, preferred_element_type=jnp.float32
    )
    grad_back_two, gain_two = norm_back(
        after_self, norm_cross, input_sum(cross_query_weight_gradient, cross_query_weight)
    )
    grad_first = grad_mid + grad_back_two
    self_attention_gradient = gather_grads(grad_first.astype(jnp.bfloat16))
    self_out_grad = jnp.einsum(
        "euy,euh->yh", attended_rows, self_attention_gradient, preferred_element_type=jnp.float32
    )
    grad_attended = jnp.einsum(
        "ezk,ck->ezc", self_attention_gradient, output_weight, preferred_element_type=jnp.float32
    ).astype(jnp.bfloat16)
    grad_q, grad_window, grad_lines = lax.map(
        self_backward,
        (
            seq_queries,
            seq_window,
            seg_query,
            seg_window,
            self_logs,
            jnp.moveaxis(grad_attended, 1, 0),
        ),
    )
    table_grad = jnp.einsum(
        "tb,ht->bh",
        one_hot,
        jnp.sum(grad_lines, axis=0),
        precision=lax.Precision.HIGHEST,
        preferred_element_type=jnp.float32,
    )
    grad_window = jnp.moveaxis(grad_window, 0, 1)
    grad_kv = grad_window[2 * local_len :]
    for offset, grad_part in (
        (-2, grad_window[:local_len]),
        (-1, grad_window[local_len : 2 * local_len]),
    ):
        grad_kv = grad_kv + from_behind(grad_part.astype(jnp.bfloat16), CTX, offset).astype(
            grad_part.dtype
        )
    projection_gradient = jnp.concatenate([jnp.moveaxis(grad_q, 0, 1), grad_kv], axis=-1).astype(
        jnp.bfloat16
    )
    self_attention_gradients = jnp.einsum(
        "zvn,zvp->np", first_rows, projection_gradient, preferred_element_type=jnp.float32
    )
    self_query_grad = self_attention_gradients[:, :head_width]
    self_key_grad = self_attention_gradients[:, head_width : 2 * head_width]
    self_value_grad = self_attention_gradients[:, 2 * head_width :]
    grad_back_one, gain_one = norm_back(
        resid_in, norm_self, input_sum(projection_gradient, self_attention_weight)
    )
    tokens_grad = grad_first + grad_back_one
    local_grads = (
        self_query_grad,
        self_key_grad,
        self_value_grad,
        self_out_grad,
        cross_query_grad,
        cross_key_grad,
        cross_value_grad,
        cross_out_grad,
        ffn_gate_grad,
        ffn_up_grad,
        feedforward_down_gradient,
        table_grad,
    )
    return (
        result.astype(jnp.bfloat16),
        tokens_grad,
        encoder_grad,
        (gain_one, gain_two, gain_three),
        local_grads,
        ffn_sums,
    )


def body(
    tokens,
    segments,
    encoder,
    norm_self,
    norm_cross,
    norm_ffn,
    rel_table,
    self_query,
    self_key,
    self_value,
    self_out,
    cross_query,
    cross_key,
    cross_value,
    cross_out,
    ffn_gate,
    ffn_up,
    ffn_down,
    cotangent,
):
    shards = (
        self_query,
        self_key,
        self_value,
        self_out,
        cross_query,
        cross_key,
        cross_value,
        cross_out,
        ffn_gate,
        ffn_up,
        ffn_down,
    )
    per_micro = tokens.shape[1] // MICRO
    results = []
    token_grads = []
    state_grads = []
    gains = None
    totals = None
    for micro in range(MICRO):
        first = micro * per_micro
        out = micro_step(
            tokens[:, first : first + per_micro],
            segments[first : first + per_micro],
            encoder[:, first : first + per_micro],
            cotangent[:, first : first + per_micro],
            norm_self,
            norm_cross,
            norm_ffn,
            rel_table,
            shards,
        )
        results.append(out[0])
        token_grads.append(out[1])
        state_grads.append(out[2])
        gains = out[3] if gains is None else tuple((a + b for a, b in zip(gains, out[3])))
        totals = out[4] if totals is None else tuple((a + b for a, b in zip(totals, out[4])))
    gain_sums = lax.psum(gains, (SHARD, CTX, TP))
    summed = (
        lax.psum_scatter(
            totals[0].astype(jnp.bfloat16), (SHARD, CTX), scatter_dimension=0, tiled=True
        ).astype(jnp.float32),
        lax.psum_scatter(
            totals[1].astype(jnp.bfloat16), (SHARD, CTX), scatter_dimension=0, tiled=True
        ).astype(jnp.float32),
        lax.psum_scatter(
            totals[2].astype(jnp.bfloat16), (SHARD, CTX), scatter_dimension=0, tiled=True
        ).astype(jnp.float32),
        lax.psum_scatter(
            totals[3].astype(jnp.bfloat16), (SHARD, CTX), scatter_dimension=1, tiled=True
        ).astype(jnp.float32),
        lax.psum_scatter(
            totals[4].astype(jnp.bfloat16), (SHARD, CTX), scatter_dimension=0, tiled=True
        ).astype(jnp.float32),
        lax.psum_scatter(
            totals[5].astype(jnp.bfloat16), (SHARD, CTX), scatter_dimension=0, tiled=True
        ).astype(jnp.float32),
        lax.psum_scatter(
            totals[6].astype(jnp.bfloat16), (SHARD, CTX), scatter_dimension=0, tiled=True
        ).astype(jnp.float32),
        lax.psum_scatter(
            totals[7].astype(jnp.bfloat16), (SHARD, CTX), scatter_dimension=1, tiled=True
        ).astype(jnp.float32),
        lax.psum_scatter(
            totals[8].astype(jnp.bfloat16), (SHARD, CTX), scatter_dimension=0, tiled=True
        ).astype(jnp.float32),
        lax.psum_scatter(
            totals[9].astype(jnp.bfloat16), (SHARD, CTX), scatter_dimension=0, tiled=True
        ).astype(jnp.float32),
        lax.psum_scatter(
            totals[10].astype(jnp.bfloat16), (SHARD, CTX), scatter_dimension=1, tiled=True
        ).astype(jnp.float32),
        lax.psum_scatter(
            totals[11].astype(jnp.bfloat16), (SHARD, CTX), scatter_dimension=0, tiled=True
        ).astype(jnp.float32),
    )
    result = jnp.concatenate(results, axis=1)
    tokens_grad = jnp.concatenate(token_grads, axis=1)
    encoder_grad = jnp.concatenate(state_grads, axis=1)
    return (
        result,
        tokens_grad,
        encoder_grad,
        gain_sums[0],
        gain_sums[1],
        gain_sums[2],
        summed[11],
        summed[0],
        summed[1],
        summed[2],
        summed[3],
        summed[4],
        summed[5],
        summed[6],
        summed[7],
        summed[8],
        summed[9],
        summed[10],
    )


def chip_coords(index):
    return (index >> 4, (index >> 3) & 1, (index >> 2) & 1, index & 3)


def move(x, target):
    pairs = []
    for index in range(32):
        sx, core, y, z = target(*chip_coords(index))
        pairs.append((index, sx * 16 + core * 8 + y * 4 + z))
    return lax.ppermute(x, AXES, pairs)


def flip_x(v):
    return move(v, lambda sx, core, y, z: (1 - sx, core, y, z))


def flip_core(v):
    return move(v, lambda sx, core, y, z: (sx, 1 - core, y, z))


def flip_y(v):
    return move(v, lambda sx, core, y, z: (sx, core, 1 - y, z))


def from_z(v, step):
    return move(v, lambda sx, core, y, z: (sx, core, y, (z - step) % 4))


def my_coords():
    shard = lax.axis_index(SHARD)
    return (shard // 2, shard % 2, lax.axis_index(CTX), lax.axis_index(TP))


def swap_blocks(blocks, place):
    sx, core, y, _ = place
    for bit, mask in ((y, 1), (core, 2), (sx, 4)):
        taken = bit == 1
        blocks = [jnp.where(taken, blocks[at ^ mask], blocks[at]) for at in range(8)]
    return blocks


RELATIVE = (0, 1, 4, 5, 2, 3, 6, 7)


def lanes(v):
    width = v.shape[-1] // 8
    return [v[..., at * width : (at + 1) * width] for at in range(8)]


def to_relative(v, place):
    blocks = swap_blocks(lanes(v), place)
    return jnp.concatenate([blocks[at] for at in RELATIVE], axis=-1)


def from_relative(v, place):
    given = lanes(v)
    blocks = [given[RELATIVE.index(at)] for at in range(8)]
    return jnp.concatenate(swap_blocks(blocks, place), axis=-1)


def pick(stack, at):
    return lax.dynamic_index_in_dim(stack, at, 0, keepdims=False)


def send_rows(block, place):
    _, _, _, z = place
    by_seq = jnp.transpose(block, (1, 0, 2))
    return [
        move(
            pick(by_seq, (z + step) % 4),
            lambda sx, core, y, z, step=step: (sx, (z >> 1) ^ y, core, (z + step) % 4),
        )
        for step in range(4)
    ]


def send_back(slots):
    return [
        move(
            slots[step],
            lambda sx, core, y, z, step=step: (
                sx,
                y,
                core ^ (((z - step) % 4) >> 1),
                (z - step) % 4,
            ),
        )
        for step in range(4)
    ]


def place_back(got, place):
    z = place[3]
    stack = jnp.stack(got)
    return jnp.stack([pick(stack, (at - z) % 4) for at in range(4)], axis=1)


def settle(*values):
    return lax.optimization_barrier(values)


WAYS = ((flip_y, flip_x), (flip_x, flip_y))
BITS = (1, 2)


def spread(pieces):
    both = lax.all_gather(jnp.stack(pieces), TP, axis=1)
    return [both[0], both[1]]


def ordered(way, held, near, far, cores):
    if way[0] is flip_y:
        return [held, near, far[0], far[1]] + cores
    return [held, far[0], near, far[1], cores[0], cores[2], cores[1], cores[3]]


def collect(both):
    rows = both.shape[1] // 2
    both = lax.psum_scatter(both, TP, scatter_dimension=0)
    return [both[:rows], both[rows:]]


def fast_layer(
    tokens, segments, encoder, norm_self, norm_cross, norm_ffn, rel_table,
    self_query, self_key, self_value, self_out,
    cross_query, cross_key, cross_value, cross_out,
    ffn_gate, ffn_up, ffn_down, cotangent,
):
    place = my_coords()
    _, core, y, z = place
    spot = jnp.stack(place).astype(jnp.int32)
    core_id = spot[1:2]
    heads = rel_table.shape[1]
    inner = self_query.shape[1]
    feed = ffn_gate.shape[1]
    cut = feed // 4
    rows = tokens.shape[0] * 4
    half = rows // 2
    width = tokens.shape[2]

    def near_of(held):
        return [way[0](h) for way, h in zip(WAYS, held)]

    def far_of(held, near):
        return [[way[1](h), way[1](n)] for way, h, n in zip(WAYS, held, near)]

    def cores_of(values):
        return [flip_core(v) for v in values]

    def far_cores(far):
        return [cores_of(f) for f in far]

    def arrange(held, near, far, core_0, core_1, core_23):
        return [
            ordered(way, h, n, f, [a, b] + c)
            for way, h, n, f, a, b, c in zip(WAYS, held, near, far, core_0, core_1, core_23)
        ]

    pieces_s = [
        jnp.concatenate([self_key.T, self_value.T], axis=0),
        jnp.concatenate([self_query.T, self_out], axis=0),
    ]
    pieces_c = [
        jnp.concatenate([cross_key.T, cross_value.T], axis=0),
        jnp.concatenate([cross_query.T, cross_out], axis=0),
    ]
    gate_t, up_t = ffn_gate.T, ffn_up.T
    pieces_f = [
        [
            jnp.concatenate([w[at : at + cut] for w in (gate_t, up_t, ffn_down)], axis=0)
            for at in (2 * chunk * cut, (2 * chunk + 1) * cut)
        ]
        for chunk in (0, 1)
    ]
    mine = lax.dynamic_index_in_dim(encoder, z, 1, keepdims=False)
    mine_seg = lax.dynamic_index_in_dim(segments, z, 0, keepdims=True)
    pairs = []
    for index in range(32):
        ax, ac, ay, az = chip_coords(index)
        if ac == ay:
            pairs.append((index, ax * 16 + (1 - ac) * 8 + ay * 4 + az))

    held_s = spread(pieces_s)
    held_c = spread(pieces_c)
    held_f1 = spread(pieces_f[0])
    held_f2 = spread(pieces_f[1])
    held_s, rows_out, mine, mine_seg, rel_table = settle(held_s, tokens, mine, mine_seg, rel_table)
    near_s, core_s0 = near_of(held_s), cores_of(held_s)
    came_rows = send_rows(rows_out, place)
    came_enc = lax.ppermute(mine, AXES, pairs)
    came_seg = lax.ppermute(mine_seg, AXES, pairs)
    came_table = [from_z(rel_table, step) for step in (1, 2, 3)]
    near_s, core_s0 = settle(near_s, core_s0)
    far_s, core_s1 = far_of(held_s, near_s), cores_of(near_s)
    far_s, core_s1, held_c = settle(far_s, core_s1, held_c)
    core_s2 = far_cores(far_s)
    near_c, core_c0 = near_of(held_c), cores_of(held_c)
    near_c, core_c0, held_f1 = settle(near_c, core_c0, held_f1)
    far_c, core_c1 = far_of(held_c, near_c), cores_of(near_c)
    near_f1, core_f10 = near_of(held_f1), cores_of(held_f1)
    far_c, core_c1, near_f1, core_f10, held_f2, low_cotangent = settle(
        far_c, core_c1, near_f1, core_f10, held_f2, cotangent
    )
    core_c2 = far_cores(far_c)
    far_f1, core_f11 = far_of(held_f1, near_f1), cores_of(near_f1)
    near_f2, core_f20 = near_of(held_f2), cores_of(held_f2)
    came_grad = send_rows(low_cotangent, place)
    far_f1, core_f11, near_f2, core_f20, came_grad = settle(
        far_f1, core_f11, near_f2, core_f20, came_grad
    )
    core_f12 = far_cores(far_f1)
    far_f2, core_f21 = far_of(held_f2, near_f2), cores_of(near_f2)
    far_f2, core_f21 = settle(far_f2, core_f21)
    core_f22 = far_cores(far_f2)

    s_kv, s_qo = arrange(held_s, near_s, far_s, core_s0, core_s1, core_s2)
    c_kv, c_qo = arrange(held_c, near_c, far_c, core_c0, core_c1, core_c2)
    f_one = arrange(held_f1, near_f1, far_f1, core_f10, core_f11, core_f12)
    f_two = arrange(held_f2, near_f2, far_f2, core_f20, core_f21, core_f22)
    w_kv, w_ckv = ([s_kv], 0, 2 * inner), ([c_kv], 0, 2 * inner)
    w_q, w_so = ([s_qo], 0, inner), ([s_qo], inner, inner)
    w_cq, w_co = ([c_qo], 0, inner), ([c_qo], inner, inner)
    w_feed = [[(blocks, at * cut, cut) for at in range(3)] for blocks in (f_one, f_two)]

    resid = gather_rows_call(spot, came_rows)
    own_seq = core == y
    states = to_relative(jnp.where(own_seq, mine, came_enc), place)
    seg = jnp.where(own_seq, mine_seg, came_seg)[0]
    tables = jnp.stack([rel_table] + came_table)
    table = jnp.concatenate([pick(tables, (at - z) % 4) for at in range(4)], axis=1)
    gains = to_relative(jnp.stack([norm_self, norm_cross, norm_ffn]), place)
    gain_self, gain_cross, gain_ffn = gains[0:1], gains[1:2], gains[2:3]

    turn = jnp.arange(2 * half, dtype=jnp.int32)
    signed = jnp.where(turn < half, turn, turn - 2 * half)
    buckets = jnp.arange(table.shape[0], dtype=jnp.int32)

    def hot(distance):
        return (bucket_index(distance)[..., None] == buckets).astype(F32)

    def bias_lines(distance):
        return jnp.dot(
            hot(distance), table, precision=lax.Precision.HIGHEST, preferred_element_type=F32
        ).T

    def kernel_lines(sign):
        near = bias_lines(sign * signed).reshape(-1, 2, 2 * half)
        after = bias_lines(half + sign * signed).reshape(-1, 2, 2 * half)
        far = jnp.broadcast_to(table[-1].reshape(-1, 2, 1), near.shape)
        blank = jnp.zeros((near.shape[0], 2, 2 * half), F32)
        return jnp.concatenate(
            [near[:, 0:1], after[:, 0:1], near[:, 1:2], after[:, 1:2], far, blank], axis=1
        )

    lines_forward, lines_backward = kernel_lines(-1), kernel_lines(1)

    quarter = jnp.arange(half, dtype=jnp.int32)
    spots = jnp.concatenate([quarter + half * n for n in (core, 3 - core, 1 - core, 2 + core)])
    seg_spots = jnp.concatenate(
        [
            lax.dynamic_slice_in_dim(seg, half * n, half, 0)
            for n in (core, 3 - core, 1 - core, 2 + core)
        ]
    )

    def mask_of(query_at, key_at, query_seg, key_seg):
        return jnp.where((query_seg == key_seg) & (key_at <= query_at), 0.0, masked_score).astype(F32)

    mask = mask_of(spots[:rows, None], spots[None, :], seg_spots[:rows, None], seg_spots[None, :])
    mask_t = mask_of(spots[None, :rows], spots[:, None], seg_spots[None, :rows], seg_spots[:, None])

    tall = min(256, rows)
    dot = 2 * rows * width

    def full(count, dtype=BF):
        return ((rows, count), dtype)

    gain_out = ((1, width), F32)

    normed_self, kv_own = staged(
        kv_body, [w_kv], [resid], [gain_self],
        [full(width), full(2 * width)], tall, dot * 2 * width,
    )
    kv_far = flip_core(kv_own)
    (queries,) = staged(nt_body, [w_q], [normed_self], [], [full(width)], tall, dot * width)
    mixed, self_logs = self_forward(core_id, queries, kv_own, kv_far, lines_forward, mask)
    (cross_kv,) = staged(
        nt_body, [w_ckv], [states], [],
        [((states.shape[0], 2 * width), BF)], states.shape[0], dot * width,
    )
    after_self, normed_cross, cross_q = staged(
        mid_body, [w_so, w_cq], [mixed, resid], [gain_cross],
        [full(width, F32), full(width), full(width)], tall, dot * 2 * width,
    )
    cross_mixed, cross_logs = cross_forward(cross_q, cross_kv)
    after_cross, normed_ffn = staged(
        mid_body, [w_co], [cross_mixed, after_self], [gain_ffn],
        [full(width, F32), full(width)], tall, dot * width,
    )
    grad_low = gather_rows_call(spot, came_grad)
    total, grad_normed = after_cross, jnp.zeros((rows, width), F32)
    feed_sides, feed_over = [], []
    for chunk in (0, 1):
        sides, total, grad_normed = staged(
            feed_body, w_feed[chunk], [normed_ffn, grad_low, total, grad_normed], [],
            [((3, rows, 8 * cut), BF), full(width, BF if chunk else F32), full(width, F32)],
            tall, dot * 6 * 8 * cut,
        )
        away = weight_grads(sides, normed_ffn, grad_low, cut, BITS)
        feed_sides.append(sides)
        feed_over.append(cores_of(away))
    result_slots = scatter_rows_call(spot, total)

    def feed_jobs(chunk):
        return weight_grads(feed_sides[chunk], normed_ffn, grad_low, cut, BITS, feed_over[chunk])

    def first_stage(jobs):
        return [way[0](sent) for way, sent in zip(WAYS, jobs[0::2])]

    def second_stage(jobs, came):
        return [way[1](h) for way, h in zip(WAYS, near_sums(jobs[1::2], came))]

    def finish(jobs, came, last):
        return collect(far_sums(jobs[1::2], came, last))

    grad_mid, low_mid, grad_cross_mixed, gain_three = staged(
        turn_body, [w_co], [after_cross, grad_normed, grad_low], [gain_ffn],
        [full(width, F32), full(width), full(width), gain_out], tall, dot * width,
    )
    grad_cq, shared = cross_backward(cross_q, cross_kv, grad_cross_mixed, cross_logs)
    own_states = states.shape[0] // 2
    sent = lax.dynamic_slice_in_dim(shared, (1 - core) * own_states, own_states, 0)
    kept = lax.dynamic_slice_in_dim(shared, core * own_states, own_states, 0)
    grad_ckv = kept + flip_core(sent)
    states_own = lax.dynamic_slice_in_dim(states, core * own_states, own_states, 0)
    grad_first, low_first, grad_mixed, gain_two = staged(
        second_turn_body, [w_cq, w_so], [grad_cq, after_self, grad_mid], [gain_cross],
        [full(width, F32), full(width), full(width), gain_out], tall, dot * 2 * width,
    )
    pair_c = (grad_cq, cross_mixed)
    away_c = weight_grads(grad_ckv[None], states_own, states_own, 2 * inner, BITS[:1])
    away_c += weight_grads(pair_c, normed_cross, low_mid, inner, BITS[1:])
    over_c = cores_of(away_c)
    (state_grad,) = staged(
        nn_body, [w_ckv], [grad_ckv], [],
        [((own_states, width), BF)], own_states, dot * width,
    )
    grad_q, kv_kept, kv_sent, sums = self_backward(
        core_id, queries, kv_own, kv_far, grad_mixed, lines_backward, mask_t, self_logs
    )
    grad_kv = kv_kept + flip_core(kv_sent)
    pair_s = (grad_q, mixed)
    away_s = weight_grads(pair_s, normed_self, low_first, inner, BITS[1:])
    away_s = weight_grads(grad_kv[None], normed_self, normed_self, 2 * inner, BITS[:1]) + away_s
    over_s = cores_of(away_s)
    tokens_rows, gain_one = staged(
        last_body, [w_q, w_kv], [grad_q, grad_kv, resid, grad_first], [gain_self],
        [full(width), gain_out], tall, dot * 3 * width,
    )
    token_slots = scatter_rows_call(spot, tokens_rows)

    def cross_jobs():
        first = weight_grads(
            grad_ckv[None], states_own, states_own, 2 * inner, BITS[:1], over_c[:1]
        )
        return first + weight_grads(pair_c, normed_cross, low_mid, inner, BITS[1:], over_c[1:])

    def self_jobs():
        first = weight_grads(
            grad_kv[None], normed_self, normed_self, 2 * inner, BITS[:1], over_s[:1]
        )
        return first + weight_grads(pair_s, normed_self, low_first, inner, BITS[1:], over_s[1:])

    jobs_f1 = feed_jobs(0)
    n1 = first_stage(jobs_f1)
    n1, jobs_f2 = settle(n1, feed_jobs(1))
    n2 = second_stage(jobs_f1, n1)
    done_f1 = finish(jobs_f1, n1, n2)
    n1 = first_stage(jobs_f2)
    n1, result_slots, jobs_c = settle(n1, result_slots, cross_jobs())
    n2 = second_stage(jobs_f2, n1)
    back_result = send_back(result_slots)
    done_f2 = finish(jobs_f2, n1, n2)
    n1 = first_stage(jobs_c)
    n1, done_f1 = settle(n1, done_f1)
    jobs_s = self_jobs()
    n2 = second_stage(jobs_c, n1)
    done_c = finish(jobs_c, n1, n2)
    state_abs = from_relative(state_grad, place)
    state_cols = jnp.stack([state_abs[:, at * inner : (at + 1) * inner] for at in range(4)])
    got = [
        move(
            pick(state_cols, (z + step) % 4),
            lambda sx, core, y, z, step=step: (sx, y, core, (z + step) % 4),
        )
        for step in range(4)
    ]
    n1 = first_stage(jobs_s)
    n1, done_f2 = settle(n1, done_f2)
    back_tokens = send_back(token_slots)
    n2 = second_stage(jobs_s, n1)
    n2, done_c = settle(n2, done_c)
    sum_s = far_sums(jobs_s[1::2], n1, n2)

    inside = (signed[None, :] - jnp.arange(8, dtype=jnp.int32)[:, None]) % (2 * half)
    inside = jnp.where(inside < half, inside, inside - 2 * half)
    kinds = jnp.stack(
        [inside, half + inside, (3 - 2 * core) * half + inside, jnp.full_like(inside, 2 * half)]
    )
    sums = sums.reshape(4 * heads, 4, 8, 2 * half)
    table_grad = jnp.einsum(
        "ndmb,hndm->bh",
        hot(kinds),
        sums,
        precision=lax.Precision.HIGHEST,
        preferred_element_type=F32,
    )
    by_z = table_grad.reshape(-1, 4, heads)
    gain_parts = from_relative(jnp.concatenate([gain_one, gain_two, gain_three]), place)
    small = jnp.concatenate([gain_parts.reshape(-1), by_z.reshape(-1)]).reshape(-1, 128)
    sum_s, small = settle(sum_s, small)
    done_s = collect(sum_s)
    for flip in (
        flip_core,
        flip_x,
        flip_y,
        lambda v: move(v, lambda sx, core, y, z: (sx, core, y, z ^ 1)),
        lambda v: move(v, lambda sx, core, y, z: (sx, core, y, z ^ 2)),
    ):
        small = small + flip(small)
    small = small.reshape(-1)
    gain_sums = small[: gain_parts.size].reshape(gain_parts.shape)
    table_sum = small[gain_parts.size :].reshape(by_z.shape)
    block = lax.axis_index(SHARD) * 2 + y
    own_table = lax.dynamic_slice_in_dim(
        lax.dynamic_index_in_dim(table_sum, z, 1, keepdims=False), block * 4, 4, 0
    )
    result = place_back(back_result, place)
    tokens_grad = place_back(back_tokens, place).astype(F32)
    got = jnp.stack(got)
    encoder_grad = jnp.stack([pick(got, (z - at) % 4) for at in range(4)], axis=1).astype(F32)
    done_f1, done_f2, done_c, done_s = (
        [v.astype(F32) for v in done] for done in (done_f1, done_f2, done_c, done_s)
    )
    feed_done = [*done_f1, *done_f2]
    gate_grad, up_grad, down_grad = (
        jnp.concatenate([done[at * cut : (at + 1) * cut] for done in feed_done], axis=0)
        for at in range(3)
    )
    (kv_done, qo_done), (ckv_done, cqo_done) = done_s, done_c
    return (
        result,
        tokens_grad,
        encoder_grad,
        gain_sums[0],
        gain_sums[1],
        gain_sums[2],
        own_table,
        qo_done[:inner].T,
        kv_done[:inner].T,
        kv_done[inner:].T,
        qo_done[inner:],
        cqo_done[:inner].T,
        ckv_done[:inner].T,
        ckv_done[inner:].T,
        cqo_done[inner:],
        gate_grad.T,
        up_grad.T,
        down_grad,
    )


def fast_body(*args):
    return fast_layer(*args)


def solution(mesh):
    placed = (
        P((CTX, TP), SHARD, None),
        P(SHARD, None),
        P(None, SHARD, None),
        P(),
        P(),
        P(),
        P(None, TP),
        P((SHARD, CTX), TP),
        P((SHARD, CTX), TP),
        P((SHARD, CTX), TP),
        P(TP, (SHARD, CTX)),
        P((SHARD, CTX), TP),
        P((SHARD, CTX), TP),
        P((SHARD, CTX), TP),
        P(TP, (SHARD, CTX)),
        P((SHARD, CTX), TP),
        P((SHARD, CTX), TP),
        P(TP, (SHARD, CTX)),
        P((CTX, TP), SHARD, None),
    )
    fits = tuple(mesh.shape[axis] for axis in AXES) == (4, 2, 4)
    return jax.shard_map(
        fast_body if fits else body,
        mesh=mesh,
        in_specs=placed,
        out_specs=(
            P((CTX, TP), SHARD, None),
            P((CTX, TP), SHARD, None),
            P(CTX, SHARD, TP),
            P(),
            P(),
            P(),
            P((SHARD, CTX), TP),
            P((SHARD, CTX), TP),
            P((SHARD, CTX), TP),
            P((SHARD, CTX), TP),
            P(TP, (SHARD, CTX)),
            P((SHARD, CTX), TP),
            P((SHARD, CTX), TP),
            P((SHARD, CTX), TP),
            P(TP, (SHARD, CTX)),
            P((SHARD, CTX), TP),
            P((SHARD, CTX), TP),
            P(TP, (SHARD, CTX)),
        ),
        check_vma=False,
    )
```

```python
from functools import partial, reduce

import jax
import jax.numpy as jnp
from jax import lax
from jax.experimental import pallas as pl
from jax.experimental.pallas import tpu as pltpu
from jax.sharding import PartitionSpec as P

MICRO = 4
SHARD, CTX, TP = AXES = ("shard", "ctx", "tp")

BF = jnp.bfloat16
F32 = jnp.float32


def nt(a, b):
    return lax.dot_general(a, b, (((1,), (1,)), ((), ())), preferred_element_type=F32)


def nn(a, b):
    return lax.dot_general(a, b, (((1,), (0,)), ((), ())), preferred_element_type=F32)


def tn(a, b):
    return lax.dot_general(a, b, (((0,), (0,)), ((), ())), preferred_element_type=F32)


def toeplitz(line, half):
    wide = jnp.broadcast_to(line, (half, 2 * half))
    return pltpu.roll(wide, 0, 1, stride=1, stride_axis=0)[:, :half]


def diagonals(tile, half):
    blank = jnp.zeros((8, half), F32)
    total = jnp.zeros((8, 2 * half), F32)
    for at in range(0, half, 8):
        wide = jnp.concatenate([tile[at : at + 8, :], blank], axis=1)
        total = total + (pltpu.roll(wide, 2 * half - at, 1) if at else wide)
    return total


def lane_pick(first, second, left):
    return jnp.where(left, first, second)


def col_softmax(tiles):
    peak = tiles[0]
    for tile in tiles[1:]:
        peak = jnp.maximum(peak, tile)
    peak = jnp.max(peak, axis=0, keepdims=True)
    exps = [jnp.exp(tile - peak) for tile in tiles]
    total = jnp.sum(reduce_add(exps), axis=0, keepdims=True)
    scale = 1.0 / total
    return [(e * scale).astype(BF) for e in exps], peak + jnp.log(total)


def reduce_add(parts):
    out = parts[0]
    for part in parts[1:]:
        out = out + part
    return out


def pick_late(swapped, first, second):
    return jnp.where(swapped, first, second)


def self_forward_kernel(core, q, k_own, v_own, k_far, v_far, lines, mask, out, logs):
    half = q.shape[0] // 2
    left = lax.broadcasted_iota(jnp.int32, (1, q.shape[1]), 1) < q.shape[1] // 2
    swapped = core[0] == 1
    a, b = slice(0, half), slice(half, 2 * half)
    low = -3.0e38
    k_late = pick_late(swapped, k_far[a, :], k_far[b, :])
    v_late = pick_late(swapped, v_far[a, :], v_far[b, :])
    mask_late = pick_late(
        swapped, mask[2 * half : 3 * half, a], mask[3 * half : 4 * half, b]
    )
    outs = []
    for head in range(2):
        keep = left if head == 0 else jnp.logical_not(left)
        qh = jnp.where(keep, q[...], jnp.zeros((), BF))
        near = toeplitz(lines[0, 2 * head : 2 * head + 1, :], half)
        next_tile = toeplitz(lines[0, 2 * head + 1 : 2 * head + 2, :], half)
        far = lines[0, 4 + head : 5 + head, :half]
        qa, qb = qh[a], qh[b]
        ka, kb, xa = k_own[a, :], k_own[b, :], k_far[a, :]
        tiles_a = [nt(ka, qa) + near + mask[0:half, a]]
        tiles_b = [
            nt(ka, qb) + jnp.where(swapped, next_tile, far) + mask[0:half, b],
            nt(kb, qb) + near + mask[half : 2 * half, b],
            nt(xa, qb) + far + mask[2 * half : 3 * half, b],
        ]
        late = nt(k_late, pick_late(swapped, qa, qb)) + next_tile + mask_late
        late_peak = jnp.max(late, axis=0, keepdims=True)
        peak_a = jnp.max(tiles_a[0], axis=0, keepdims=True)
        peak_b = jnp.max(
            jnp.maximum(jnp.maximum(tiles_b[0], tiles_b[1]), tiles_b[2]), axis=0, keepdims=True
        )
        peak_a = jnp.maximum(peak_a, pick_late(swapped, late_peak, low))
        peak_b = jnp.maximum(peak_b, pick_late(swapped, low, late_peak))
        exps_a = [jnp.exp(tile - peak_a) for tile in tiles_a]
        exps_b = [jnp.exp(tile - peak_b) for tile in tiles_b]
        exp_late = jnp.exp(late - pick_late(swapped, peak_a, peak_b))
        sum_late = jnp.sum(exp_late, axis=0, keepdims=True)
        total_a = jnp.sum(exps_a[0], axis=0, keepdims=True) + pick_late(swapped, sum_late, 0.0)
        total_b = jnp.sum(reduce_add(exps_b), axis=0, keepdims=True) + pick_late(
            swapped, 0.0, sum_late
        )
        scale_a, scale_b = 1.0 / total_a, 1.0 / total_b
        out_late = tn((exp_late * pick_late(swapped, scale_a, scale_b)).astype(BF), v_late)
        oa = tn((exps_a[0] * scale_a).astype(BF), v_own[a, :])
        pb = [(e * scale_b).astype(BF) for e in exps_b]
        ob = tn(pb[0], v_own[a, :]) + tn(pb[1], v_own[b, :]) + tn(pb[2], v_far[a, :])
        oa = oa + pick_late(swapped, out_late, 0.0)
        ob = ob + pick_late(swapped, 0.0, out_late)
        outs.append((oa, ob))
        logs[0, head : head + 1, a] = peak_a + jnp.log(total_a)
        logs[0, head : head + 1, b] = peak_b + jnp.log(total_b)
    out[a, :] = lane_pick(outs[0][0], outs[1][0], left).astype(BF)
    out[b, :] = lane_pick(outs[0][1], outs[1][1], left).astype(BF)


def self_backward_kernel(
    core, q, k_own, v_own, k_far, v_far, grad, lines, mask, logs,
    dq, own_out, far_out, sums,
):
    half = q.shape[0] // 2
    left = lax.broadcasted_iota(jnp.int32, (1, q.shape[1]), 1) < q.shape[1] // 2
    swapped = core[0] == 1
    a, b = slice(0, half), slice(half, 2 * half)
    zero = jnp.zeros((), BF)
    mask_late = pick_late(
        swapped, mask[2 * half : 3 * half, a], mask[3 * half : 4 * half, b]
    )
    keys = {
        "oa": (k_own[a, :], v_own[a, :]),
        "ob": (k_own[b, :], v_own[b, :]),
        "xa": (k_far[a, :], v_far[a, :]),
        "x": (
            pick_late(swapped, k_far[a, :], k_far[b, :]),
            pick_late(swapped, v_far[a, :], v_far[b, :]),
        ),
    }
    dk, dv, dqs = {}, {}, {}

    def grow(store, name, value):
        store[name] = value if name not in store else store[name] + value

    for head in range(2):
        keep = left if head == 0 else jnp.logical_not(left)
        qh = jnp.where(keep, q[...], zero)
        gh = jnp.where(keep, grad[...], zero)
        near = toeplitz(lines[0, 2 * head : 2 * head + 1, :], half)
        next_tile = toeplitz(lines[0, 2 * head + 1 : 2 * head + 2, :], half)
        far = lines[0, 4 + head : 5 + head, :half]
        log_a, log_b = logs[0, head : head + 1, a], logs[0, head : head + 1, b]
        queries = {"a": (qh[a], gh[a], log_a), "b": (qh[b], gh[b], log_b)}
        queries["x"] = tuple(pick_late(swapped, u, v) for u, v in zip(queries["a"], queries["b"]))
        plan = (
            ("a", "oa", near, mask[0:half, a]),
            ("b", "oa", jnp.where(swapped, next_tile, far), mask[0:half, b]),
            ("b", "ob", near, mask[half : 2 * half, b]),
            ("b", "xa", far, mask[2 * half : 3 * half, b]),
            ("x", "x", next_tile, mask_late),
        )
        probs, dots, sums_of = [], [], {}
        for side, name, bias, hide in plan:
            qp, gp, total = queries[side]
            k, v = keys[name]
            p = jnp.exp(nt(k, qp) + bias + hide - total)
            d = nt(v, gp)
            probs.append(p)
            dots.append(d)
            grow(sums_of, side, p * d)
        delta = {side: jnp.sum(v, axis=0, keepdims=True) for side, v in sums_of.items()}
        delta_a = delta["a"] + pick_late(swapped, delta["x"], 0.0)
        delta_b = delta["b"] + pick_late(swapped, 0.0, delta["x"])
        delta = {"a": delta_a, "b": delta_b, "x": pick_late(swapped, delta_a, delta_b)}
        held = {}
        for (side, name, _, _), p, d in zip(plan, probs, dots):
            qp, gp, _ = queries[side]
            k, _ = keys[name]
            ds = p * (d - delta[side])
            held[side, name] = ds
            low = ds.astype(BF)
            grow(dv, name, nn(p.astype(BF), gp))
            grow(dk, name, nn(low, qp))
            grow(dqs, side, tn(low, jnp.where(keep, k, zero)))
        base = 32 * head
        sums[0, base : base + 8, :] = diagonals(held["a", "oa"] + held["b", "ob"], half)
        sums[0, base + 8 : base + 16, :] = diagonals(held["x", "x"], half)
        sums[0, base + 16 : base + 24, :] = diagonals(held["b", "oa"], half)
        rest = reduce_add([held["b", "xa"][at : at + 8, :] for at in range(0, half, 8)])
        sums[0, base + 24 : base + 32, :] = jnp.concatenate([rest, jnp.zeros_like(rest)], axis=1)
    dq[a, :] = (dqs["a"] + pick_late(swapped, dqs["x"], 0.0)).astype(BF)
    dq[b, :] = (dqs["b"] + pick_late(swapped, 0.0, dqs["x"])).astype(BF)
    sub = pl.multiple_of(lax.rem(pl.program_id(0), 2) * 128, 128)
    for at, grads in ((0, dk), (256, dv)):
        own_out[a, pl.ds(sub + at, 128)] = grads["oa"].astype(BF)
        own_out[b, pl.ds(sub + at, 128)] = grads["ob"].astype(BF)
        far_out[a, pl.ds(sub + at, 128)] = (
            grads["xa"] + pick_late(swapped, grads["x"], 0.0)
        ).astype(BF)
        far_out[b, pl.ds(sub + at, 128)] = pick_late(swapped, 0.0, grads["x"]).astype(BF)


def self_specs(rows):
    kv = lambda which: (lambda p, c: (0, (p // 2) * 4 + which * 2 + p % 2))
    q = pl.BlockSpec((rows, 128), lambda p, c: (0, p))
    k = pl.BlockSpec((rows, 128), kv(0))
    v = pl.BlockSpec((rows, 128), kv(1))
    small = pl.BlockSpec((1, 8, rows), lambda p, c: (p, 0, 0))
    return q, k, v, small


def self_forward(core, q, kv_own, kv_far, lines, mask):
    rows, width = q.shape
    pairs = width // 128
    qs, ks, vs, small = self_specs(rows)
    return pl.pallas_call(
        self_forward_kernel,
        grid_spec=pltpu.PrefetchScalarGridSpec(
            num_scalar_prefetch=1,
            grid=(pairs,),
            in_specs=[qs, ks, vs, ks, vs, small, pl.BlockSpec((2 * rows, rows), lambda p, c: (0, 0))],
            out_specs=[qs, small],
        ),
        out_shape=(
            jax.ShapeDtypeStruct((rows, width), BF),
            jax.ShapeDtypeStruct((pairs, 8, rows), F32),
        ),
        cost_estimate=pl.CostEstimate(flops=pairs * 24 * 65536 * 128 * 2, bytes_accessed=10 << 20, transcendentals=0),
        name="self_fwd",
    )(core, q, kv_own, kv_own, kv_far, kv_far, lines, mask)


def self_backward(core, q, kv_own, kv_far, grad, lines, mask_t, logs):
    rows, width = q.shape
    pairs = width // 128
    qs, ks, vs, small = self_specs(rows)
    wide = pl.BlockSpec((rows, 512), lambda p, c: (0, p // 2))
    return pl.pallas_call(
        self_backward_kernel,
        grid_spec=pltpu.PrefetchScalarGridSpec(
            num_scalar_prefetch=1,
            grid=(pairs,),
            in_specs=[qs, ks, vs, ks, vs, qs, small, pl.BlockSpec((2 * rows, rows), lambda p, c: (0, 0)), small],
            out_specs=[qs, wide, wide, pl.BlockSpec((1, 64, rows), lambda p, c: (p, 0, 0))],
        ),
        out_shape=(
            jax.ShapeDtypeStruct((rows, width), BF),
            jax.ShapeDtypeStruct((rows, 2 * width), BF),
            jax.ShapeDtypeStruct((rows, 2 * width), BF),
            jax.ShapeDtypeStruct((pairs, 64, rows), F32),
        ),
        cost_estimate=pl.CostEstimate(flops=pairs * 60 * 65536 * 128 * 2, bytes_accessed=20 << 20, transcendentals=0),
        name="self_bwd",
    )(core, q, kv_own, kv_own, kv_far, kv_far, grad, lines, mask_t, logs)


def cross_forward_kernel(q, k, v, out, logs):
    left = lax.broadcasted_iota(jnp.int32, (1, q.shape[1]), 1) < q.shape[1] // 2
    for at in range(0, q.shape[0], 128):
        piece = slice(at, at + 128)
        outs = []
        for head in range(2):
            keep = left if head == 0 else jnp.logical_not(left)
            qh = jnp.where(keep, q[piece, :], jnp.zeros((), BF))
            p, total = col_softmax([nt(k[...], qh)])
            outs.append(tn(p[0], v[...]))
            logs[0, head : head + 1, piece] = total
        out[piece, :] = lane_pick(outs[0], outs[1], left).astype(BF)


def cross_backward_kernel(q, k, v, grad, logs, dq, out):
    left = lax.broadcasted_iota(jnp.int32, (1, q.shape[1]), 1) < q.shape[1] // 2
    dqs = dks = dvs = None
    zero = jnp.zeros((), BF)
    for head in range(2):
        keep = left if head == 0 else jnp.logical_not(left)
        qh = jnp.where(keep, q[...], zero)
        gh = jnp.where(keep, grad[...], zero)
        p = jnp.exp(nt(k[...], qh) - logs[0, head : head + 1, :])
        d = nt(v[...], gh)
        delta = jnp.sum(p * d, axis=0, keepdims=True)
        low = (p * (d - delta)).astype(BF)
        dvp, dkp, dqp = nn(p.astype(BF), gh), nn(low, qh), tn(low, jnp.where(keep, k[...], zero))
        dqs = dqp if dqs is None else dqs + dqp
        dks = dkp if dks is None else dks + dkp
        dvs = dvp if dvs is None else dvs + dvp
    dq[...] = dqs.astype(BF)
    sub = pl.multiple_of(lax.rem(pl.program_id(0), 2) * 128, 128)
    out[:, pl.ds(sub, 128)] = dks.astype(BF)
    out[:, pl.ds(sub + 256, 128)] = dvs.astype(BF)


def cross_specs(rows, states):
    kv = lambda which: (lambda p: (0, (p // 2) * 4 + which * 2 + p % 2))
    q = pl.BlockSpec((rows, 128), lambda p: (0, p))
    k = pl.BlockSpec((states, 128), kv(0))
    v = pl.BlockSpec((states, 128), kv(1))
    small = pl.BlockSpec((1, 8, rows), lambda p: (p, 0, 0))
    return q, k, v, small


def cross_forward(q, kv):
    rows, width = q.shape
    states = kv.shape[0]
    pairs = width // 128
    qs, ks, vs, small = cross_specs(rows, states)
    return pl.pallas_call(
        cross_forward_kernel,
        grid=(pairs,),
        in_specs=[qs, ks, vs],
        out_specs=[qs, small],
        out_shape=(
            jax.ShapeDtypeStruct((rows, width), BF),
            jax.ShapeDtypeStruct((pairs, 8, rows), F32),
        ),
        cost_estimate=pl.CostEstimate(flops=pairs * 8 * rows * states * 128, bytes_accessed=4 << 20, transcendentals=0),
        name="cross_fwd",
    )(q, kv, kv)


def cross_backward(q, kv, grad, logs):
    rows, width = q.shape
    states = kv.shape[0]
    pairs = width // 128
    qs, ks, vs, small = cross_specs(rows, states)
    return pl.pallas_call(
        cross_backward_kernel,
        grid=(pairs,),
        in_specs=[qs, ks, vs, qs, small],
        out_specs=[qs, pl.BlockSpec((states, 512), lambda p: (0, p // 2))],
        out_shape=(
            jax.ShapeDtypeStruct((rows, width), BF),
            jax.ShapeDtypeStruct((states, 2 * width), BF),
        ),
        cost_estimate=pl.CostEstimate(flops=pairs * 20 * rows * states * 128, bytes_accessed=6 << 20, transcendentals=0),
        name="cross_bwd",
    )(q, kv, kv, grad, logs)


def staged_kernel(body, weights, n_blocks, n_tiled, n_whole, n_out, *refs):
    core_refs = refs[:n_blocks]
    at = n_blocks
    tiled, at = refs[at : at + n_tiled], at + n_tiled
    whole, at = refs[at : at + n_whole], at + n_whole
    outs, at = refs[at : at + n_out], at + n_out
    held, sems = refs[at : at + len(weights)], refs[at + len(weights) :]
    first = pl.program_id(0) == 0
    copies = []
    for (colors, start, size), store, sem in zip(weights, held, sems):
        own = []
        for color, blocks in enumerate(colors):
            for slot, block in enumerate(blocks):
                own.append(
                    pltpu.make_async_copy(
                        core_refs[block].at[:, start : start + size, :],
                        store.at[:, color * size : (color + 1) * size, slot * 128 : (slot + 1) * 128],
                        sem.at[color * 8 + slot],
                    )
                )
        copies.append(own)

    @pl.when(first)
    def _():
        for own in copies:
            for copy in own:
                copy.start()

    ready = set()

    def weight(which):
        if which not in ready:
            ready.add(which)

            @pl.when(first)
            def _():
                for copy in copies[which]:
                    copy.wait()

        value = held[which][...]
        return value.reshape(-1, value.shape[-1])

    body(first, weight, tiled, whole, outs)


def staged(body, weights, tiled, whole, out_types, tile, flops):
    flat, index = [], {}
    plan = []
    for colors, start, size in weights:
        for blocks in colors:
            for block in blocks:
                if id(block) not in index:
                    index[id(block)] = len(flat)
                    flat.append(block)
        plan.append(([[index[id(b)] for b in blocks] for blocks in colors], start, size))
    rows = tiled[0].shape[0]

    def tile_spec(shape):
        return pl.BlockSpec((tile, shape[1]), lambda m: (m, 0))

    def whole_spec(shape):
        return pl.BlockSpec(shape, lambda m: (0,) * len(shape))

    out_specs, out_shapes = [], []
    for shape, dtype in out_types:
        out_shapes.append(jax.ShapeDtypeStruct(shape, dtype))
        if len(shape) == 3:
            out_specs.append(pl.BlockSpec((shape[0], tile, shape[2]), lambda m: (0, m, 0)))
        else:
            out_specs.append(tile_spec(shape) if shape[0] == rows else whole_spec(shape))
    nbytes = sum(v.size * v.dtype.itemsize for v in (*flat, *tiled, *whole))
    return pl.pallas_call(
        partial(staged_kernel, body, plan, len(flat), len(tiled), len(whole), len(out_types)),
        grid=(rows // tile,),
        in_specs=[pl.BlockSpec(memory_space=pl.ANY)] * len(flat)
        + [tile_spec(v.shape) for v in tiled]
        + [whole_spec(v.shape) for v in whole],
        out_specs=out_specs,
        out_shape=out_shapes,
        scratch_shapes=[
            pltpu.VMEM((4, len(colors) * size, 1024), BF) for colors, start, size in plan
        ]
        + [pltpu.SemaphoreType.DMA((8 * len(colors),)) for colors, start, size in plan],
        cost_estimate=pl.CostEstimate(flops=flops, bytes_accessed=nbytes, transcendentals=0),
    )(*flat, *tiled, *whole)


def unit(h):
    return lax.rsqrt(jnp.mean(h * h, axis=-1, keepdims=True) + epsilon)


def normed(h, gain):
    return (h * unit(h) * gain).astype(BF)


def norm_pull(h, gain, grad):
    scale = unit(h)
    inner = gain * grad
    mean = jnp.mean(inner * h, axis=-1, keepdims=True)
    back = scale * inner - h * (scale * scale * scale) * mean
    return back, jnp.sum(grad * h * scale, axis=0, keepdims=True)


def add_up(first, out, value):
    @pl.when(first)
    def _():
        out[...] = value

    @pl.when(jnp.logical_not(first))
    def _():
        out[...] = out[...] + value


def kv_body(first, weight, tiled, whole, outs):
    n = normed(tiled[0][...].astype(F32), whole[0][...])
    outs[0][...] = n
    outs[1][...] = nt(n, weight(0)).astype(BF)


def nt_body(first, weight, tiled, whole, outs):
    outs[0][...] = nt(tiled[0][...], weight(0)).astype(BF)


def nn_body(first, weight, tiled, whole, outs):
    outs[0][...] = nn(tiled[0][...], weight(0)).astype(BF)


def mid_body(first, weight, tiled, whole, outs):
    mixed, resid = tiled
    after = resid[...].astype(F32) + nn(mixed[...], weight(0))
    outs[0][...] = after
    n = normed(after, whole[0][...])
    outs[1][...] = n
    if len(outs) > 2:
        outs[2][...] = nt(n, weight(1)).astype(BF)


GELU_SCALE = (2.0 / 3.141592653589793) ** 0.5


def feed_body(first, weight, tiled, whole, outs):
    n, g, before, *grad_before = tiled
    sides_out, after_out, normed_out = outs
    gate = nt(n[...], weight(0))
    up = nt(n[...], weight(1))
    square = gate * gate
    wave = jnp.tanh(GELU_SCALE * gate * (1.0 + 0.044715 * square))
    soft = 0.5 * (1.0 + wave)
    act = gate * soft
    hidden = (act * up).astype(BF)
    sides_out[2] = hidden
    after_out[...] = (before[...].astype(F32) + nn(hidden, weight(2))).astype(after_out.dtype)
    grad = nt(g[...], weight(2))
    slope = soft + 0.5 * gate * (1.0 - wave * wave) * (GELU_SCALE * (1.0 + 3 * 0.044715 * square))
    grad_gate = (grad * up * slope).astype(BF)
    grad_up = (grad * act).astype(BF)
    sides_out[0] = grad_gate
    sides_out[1] = grad_up
    grad_normed = nn(grad_gate, weight(0)) + nn(grad_up, weight(1))
    for part in grad_before:
        grad_normed = grad_normed + part[...]
    normed_out[...] = grad_normed


def turn_body(first, weight, tiled, whole, outs):
    h, grad_normed, grad_out = tiled
    back, gain_part = norm_pull(h[...], whole[0][...], grad_normed[...])
    total = grad_out[...].astype(F32) + back
    low = total.astype(BF)
    outs[0][...] = total
    outs[1][...] = low
    outs[2][...] = nt(low, weight(0)).astype(BF)
    add_up(first, outs[3], gain_part)


def second_turn_body(first, weight, tiled, whole, outs):
    grad_query, h, grad_out = tiled
    back, gain_part = norm_pull(h[...], whole[0][...], nn(grad_query[...], weight(0)))
    total = grad_out[...].astype(F32) + back
    low = total.astype(BF)
    outs[0][...] = total
    outs[1][...] = low
    outs[2][...] = nt(low, weight(1)).astype(BF)
    add_up(first, outs[3], gain_part)


def last_body(first, weight, tiled, whole, outs):
    grad_query, grad_kv, h, grad_out = tiled
    grad_normed = nn(grad_query[...], weight(0)) + nn(grad_kv[...], weight(1))
    back, gain_part = norm_pull(h[...].astype(F32), whole[0][...], grad_normed)
    outs[0][...] = (grad_out[...] + back).astype(BF)
    add_up(first, outs[1], gain_part)


def grads_kernel(size, ways, kept, two, *refs):
    n_colors = len(ways)
    last = pl.program_id(0) == pl.num_programs(0) - 1
    if two:
        rows_grad = jnp.where(last, refs[1][...], refs[0][...])
    else:
        rows_grad = refs[0][0]
    refs = refs[1 + two :]
    came = refs[2 : 2 + n_colors] if kept else ()
    outs = refs[2 + len(came) :]
    value = tn(rows_grad, jnp.where(last, refs[1][...], refs[0][...]))
    for color, bit in enumerate(ways):
        for z in range(4):
            row = (z * n_colors + color) * size
            piece = value[row : row + size]
            for at in range(4):
                part = piece[:, at * 128 : (at + 1) * 128]
                if not kept:
                    outs[color][at, z] = part.astype(BF)
                    continue
                part = (part + came[color][at, z].astype(F32)).astype(BF)
                if at & bit:
                    outs[2 * color][at // 3, z] = part
                else:
                    outs[2 * color + 1][min(at, 1), z] = part


def weight_grads(rows_grad, first_in, second_in, size, ways, came=None):
    two = isinstance(rows_grad, tuple)
    if two:
        (rows, inner), count = rows_grad[0].shape, 2
        sources = list(rows_grad)
        source_specs = [pl.BlockSpec((rows, inner), lambda w: (0, 0))] * 2
    else:
        count, rows, inner = rows_grad.shape
        sources = [rows_grad]
        source_specs = [pl.BlockSpec((1, rows, inner), lambda w: (w, 0, 0))]
    kept = came is not None
    slab = pl.BlockSpec((4, 4, size, 128), lambda w: (0, 0, w, 0))
    pair = pl.BlockSpec((2, 4, size, 128), lambda w: (0, 0, w, 0))
    side = pl.BlockSpec((rows, 512), lambda w: (0, 0 if kept else 1))
    if kept:
        out_specs = [pair] * (2 * len(ways))
        out_shape = [jax.ShapeDtypeStruct((2, 4, count * size, 128), BF)] * (2 * len(ways))
    else:
        out_specs = [slab] * len(ways)
        out_shape = [jax.ShapeDtypeStruct((4, 4, count * size, 128), BF)] * len(ways)
    extra = list(came) if kept else []
    return pl.pallas_call(
        partial(grads_kernel, size, ways, kept, two),
        grid=(count,),
        in_specs=source_specs + [side, side] + [slab] * len(extra),
        out_specs=out_specs,
        out_shape=out_shape,
        cost_estimate=pl.CostEstimate(
            flops=2 * count * rows * inner * 512,
            bytes_accessed=2 * count * inner * (rows + 1024),
            transcendentals=0,
        ),
    )(*sources, first_in, second_in, *extra)


def near_sum_kernel(*refs):
    count = len(refs) // 3
    for at in range(count):
        refs[2 * count + at][...] = refs[2 * at][0] + refs[2 * at + 1][0]


def near_sums(kept, came):
    shape = kept[0].shape
    second = pl.BlockSpec((1, *shape[1:]), lambda m: (1, 0, 0, 0))
    out = pl.BlockSpec(shape[1:], lambda m: (0, 0, 0))
    operands = [v for both in zip(kept, came) for v in both]
    return pl.pallas_call(
        near_sum_kernel,
        grid=(1,),
        in_specs=[second] * len(operands),
        out_specs=[out] * len(kept),
        out_shape=[jax.ShapeDtypeStruct(shape[1:], BF)] * len(kept),
        cost_estimate=pl.CostEstimate(flops=0, bytes_accessed=6 * kept[0].size, transcendentals=0),
        name="s1",
    )(*operands)


def far_sum_kernel(*refs):
    out = refs[-1]
    count = len(refs) // 3
    size = out.shape[1] // count
    for at in range(count):
        total = refs[3 * at][0].astype(F32) + refs[3 * at + 1][0].astype(F32)
        total = total + refs[3 * at + 2][...].astype(F32)
        out[:, at * size : (at + 1) * size, :] = total.astype(BF)


def far_sums(kept, came, last):
    shape = kept[0].shape
    first = pl.BlockSpec((1, *shape[1:]), lambda m: (0, 0, 0, 0))
    whole = pl.BlockSpec(shape[1:], lambda m: (0, 0, 0))
    operands = [v for both in zip(kept, came, last) for v in both]
    total = (shape[1], shape[2] * len(kept), shape[3])
    return pl.pallas_call(
        far_sum_kernel,
        grid=(1,),
        in_specs=[first, first, whole] * len(kept),
        out_specs=pl.BlockSpec(total, lambda m: (0, 0, 0)),
        out_shape=jax.ShapeDtypeStruct(total, BF),
        cost_estimate=pl.CostEstimate(flops=0, bytes_accessed=8 * kept[0].size, transcendentals=0),
        name="s2",
    )(*operands)


def gather_rows_kernel(place, *refs):
    got, out, sem = refs[:4], refs[4], refs[5]
    sx, core, y, z = place[0], place[1], place[2], place[3]
    copies = []
    for step in range(4):
        row = pl.multiple_of(lax.rem(z + 4 - step, 4) ^ (2 * core), 1) * 128
        for at in range(8):
            lane = 128 * ((((at >> 1) & 1) ^ sx) * 4 + ((at >> 2) ^ core) * 2 + ((at & 1) ^ y))
            copies.append(
                pltpu.make_async_copy(
                    got[step].at[:, pl.ds(pl.multiple_of(lane, 128), 128)],
                    out.at[pl.ds(pl.multiple_of(row, 128), 128), at * 128 : (at + 1) * 128],
                    sem.at[step * 8 + at],
                )
            )
    for copy in copies:
        copy.start()
    for copy in copies:
        copy.wait()


def gather_rows_call(place, got):
    rows, width = got[0].shape
    return pl.pallas_call(
        gather_rows_kernel,
        grid_spec=pltpu.PrefetchScalarGridSpec(
            num_scalar_prefetch=1,
            grid=(1,),
            in_specs=[pl.BlockSpec(memory_space=pl.ANY)] * 4,
            out_specs=pl.BlockSpec((4 * rows, width), lambda m, p: (0, 0)),
            scratch_shapes=[pltpu.SemaphoreType.DMA((32,))],
        ),
        out_shape=jax.ShapeDtypeStruct((4 * rows, width), got[0].dtype),
        cost_estimate=pl.CostEstimate(flops=0, bytes_accessed=16 * rows * width, transcendentals=0),
        name="rows_in",
    )(place, *got)


def scatter_rows_kernel(place, rows_ref, *refs):
    outs, sem = refs[:4], refs[4]
    sx, core, y, z = place[0], place[1], place[2], place[3]
    copies = []
    for step in range(4):
        row = (lax.rem(z + 4 - step, 4) ^ (2 * core)) * 128
        for at in range(8):
            lane = 128 * ((((at >> 1) & 1) ^ sx) * 4 + ((at >> 2) ^ core) * 2 + ((at & 1) ^ y))
            copies.append(
                pltpu.make_async_copy(
                    rows_ref.at[pl.ds(pl.multiple_of(row, 128), 128), at * 128 : (at + 1) * 128],
                    outs[step].at[:, pl.ds(pl.multiple_of(lane, 128), 128)],
                    sem.at[step * 8 + at],
                )
            )
    for copy in copies:
        copy.start()
    for copy in copies:
        copy.wait()


def scatter_rows_call(place, rows_in):
    rows, width = rows_in.shape
    part = jax.ShapeDtypeStruct((rows // 4, width), rows_in.dtype)
    return pl.pallas_call(
        scatter_rows_kernel,
        grid_spec=pltpu.PrefetchScalarGridSpec(
            num_scalar_prefetch=1,
            grid=(1,),
            in_specs=[pl.BlockSpec(memory_space=pl.ANY)],
            out_specs=[pl.BlockSpec((rows // 4, width), lambda m, p: (0, 0))] * 4,
            scratch_shapes=[pltpu.SemaphoreType.DMA((32,))],
        ),
        out_shape=[part] * 4,
        cost_estimate=pl.CostEstimate(flops=0, bytes_accessed=4 * rows * width, transcendentals=0),
        name="rows_out",
    )(place, rows_in)


epsilon = 1e-06
masked_score = -1000000000.0
bucket_edges = (19, 21, 24, 27, 31, 35, 40, 46, 52, 59, 67, 77, 87, 99, 113)


def from_behind(x, axis, by):
    peers = lax.axis_size(axis)
    pairs = [(i, i + by) for i in range(peers) if 0 <= i + by < peers]
    return lax.ppermute(x, axis, pairs)


def bucket_index(distance):
    distance = jnp.maximum(distance, 0)
    far_bucket = reduce(
        lambda running, threshold: running + (distance >= threshold).astype(jnp.int32),
        bucket_edges,
        jnp.full(distance.shape, 16, jnp.int32),
    )
    return jnp.where(distance < 16, distance, far_bucket)


def rms_scale(hidden_in):
    return lax.rsqrt(jnp.mean(hidden_in * hidden_in, axis=-1, keepdims=True) + epsilon)


def norm_back(hidden_in, gain_vec, grad_in):
    inv_scale = rms_scale(hidden_in)
    scaled_grad = gain_vec * grad_in
    inner_mean = jnp.mean(scaled_grad * hidden_in, axis=-1, keepdims=True)
    grad_back = (
        inv_scale * scaled_grad - hidden_in * (inv_scale * inv_scale * inv_scale) * inner_mean
    )
    gain_part = jnp.sum(grad_in * hidden_in * inv_scale, axis=(0, 1))
    return (grad_back, gain_part)


def soft_rows(scores):
    peak = jnp.max(scores, axis=-1, keepdims=True)
    exp_scores = jnp.exp(scores - peak)
    row_total = jnp.sum(exp_scores, axis=-1, keepdims=True)
    return (exp_scores / row_total, peak + jnp.log(row_total))


def soft_back(attn_probs, grad_probs):
    return attn_probs * (grad_probs - jnp.sum(attn_probs * grad_probs, axis=-1, keepdims=True))


def spread_bias(bias_line, row_count, col_count):
    row_width = row_count + col_count
    head_total = bias_line.shape[0]
    tiled_line = jnp.tile(bias_line, (1, row_count))[:, : row_count * row_width]
    return tiled_line.reshape(head_total, row_count, row_width)[:, :, :col_count]


def fold_bias(score_grid, row_count, col_count):
    row_width = row_count + col_count
    head_total = score_grid.shape[0]
    padded = jnp.pad(score_grid, ((0, 0), (0, 0), (0, row_count))).reshape(
        head_total, row_count * row_width
    )
    padded = jnp.pad(padded, ((0, 0), (0, row_count))).reshape(head_total, row_count, row_width + 1)
    return jnp.sum(padded, axis=1)


def gather_rows(normed):
    return lax.all_gather(normed, TP, axis=0, tiled=True)


def gather_grads(grad_in):
    return lax.all_gather(grad_in, TP, axis=0, tiled=True)


def branch_sum(input_values, input_weight):
    return lax.psum_scatter(
        jnp.einsum("gci,iu->gcu", input_values, input_weight, preferred_element_type=jnp.float32),
        TP,
        scatter_dimension=0,
        tiled=True,
    )


def input_sum(incoming_gradients, input_weight):
    return lax.psum_scatter(
        jnp.einsum(
            "iyv,mv->iym", incoming_gradients, input_weight, preferred_element_type=jnp.float32
        ),
        TP,
        scatter_dimension=0,
        tiled=True,
    )


def cross_scores(queries_in, states_kv, head_count):
    local_len, seq_count, head_width = queries_in.shape
    state_len = states_kv.shape[0]
    queries_h = queries_in.reshape(local_len, seq_count, head_count, -1)
    keys_h = states_kv[..., :head_width].reshape(state_len, seq_count, head_count, -1)
    values_h = states_kv[..., head_width:].reshape(state_len, seq_count, head_count, -1)
    scores = jnp.einsum("qshe,kshe->shqk", queries_h, keys_h, preferred_element_type=jnp.float32)
    return (scores, queries_h, keys_h, values_h)


def micro_step(
    tokens, segments, encoder, cotangent, norm_self, norm_cross, norm_ffn, rel_table, shards
):
    gathered = (
        lax.all_gather(shards[0], (SHARD, CTX), axis=0, tiled=True),
        lax.all_gather(shards[1], (SHARD, CTX), axis=0, tiled=True),
        lax.all_gather(shards[2], (SHARD, CTX), axis=0, tiled=True),
        lax.all_gather(shards[3], (SHARD, CTX), axis=1, tiled=True),
        lax.all_gather(shards[4], (SHARD, CTX), axis=0, tiled=True),
        lax.all_gather(shards[5], (SHARD, CTX), axis=0, tiled=True),
        lax.all_gather(shards[6], (SHARD, CTX), axis=0, tiled=True),
        lax.all_gather(shards[7], (SHARD, CTX), axis=1, tiled=True),
        lax.all_gather(shards[8], (SHARD, CTX), axis=0, tiled=True),
        lax.all_gather(shards[9], (SHARD, CTX), axis=0, tiled=True),
        lax.all_gather(shards[10], (SHARD, CTX), axis=1, tiled=True),
    )
    (
        w_query,
        w_key,
        w_value,
        output_weight,
        cross_query_weight,
        c_key,
        c_value,
        cross_output_weight,
        w_gate,
        w_up,
        down_weight,
    ) = gathered
    own_rows = tokens.shape[0]
    seq_count = tokens.shape[1]
    local_len = own_rows * lax.axis_size(TP)
    window_len = 3 * local_len
    period = window_len + local_len + 1
    head_count = rel_table.shape[1]
    head_width = w_query.shape[1]
    feed_width = w_gate.shape[1]
    ctx_index = lax.axis_index(CTX)
    fill_ids = jnp.full((seq_count, 2 * local_len), -1, jnp.int32)
    seg_padded = jnp.concatenate([fill_ids, segments], axis=1)
    seg_window = lax.dynamic_slice_in_dim(seg_padded, ctx_index * local_len, window_len, 1)
    seg_query = lax.dynamic_slice_in_dim(segments, ctx_index * local_len, local_len, 1)
    offsets = jnp.arange(period, dtype=jnp.int32)
    distance = jnp.where(
        offsets < window_len, 2 * local_len - offsets, 2 * local_len - offsets + period
    )
    one_hot = (
        bucket_index(distance)[:, None] == jnp.arange(rel_table.shape[0], dtype=jnp.int32)[None, :]
    ).astype(jnp.float32)
    bias_line = jnp.dot(
        one_hot, rel_table, precision=lax.Precision.HIGHEST, preferred_element_type=jnp.float32
    ).T
    rel_bias = spread_bias(bias_line, local_len, window_len)
    causal_ok = (
        jnp.arange(window_len, dtype=jnp.int32)[None, :]
        <= jnp.arange(local_len, dtype=jnp.int32)[:, None] + 2 * local_len
    )

    def self_scores(one_query, one_window, query_ids, window_ids):
        queries_h = one_query.reshape(local_len, head_count, -1)
        keys_h = one_window[:, :head_width].reshape(window_len, head_count, -1)
        values_h = one_window[:, head_width:].reshape(window_len, head_count, -1)
        scores = (
            jnp.einsum("qhe,khe->hqk", queries_h, keys_h, preferred_element_type=jnp.float32)
            + rel_bias
        )
        allowed = (query_ids[:, None] == window_ids[None, :]) & causal_ok
        return (jnp.where(allowed[None], scores, masked_score), queries_h, keys_h, values_h)

    def self_forward(items):
        one_query, one_window, query_ids, window_ids = items
        scores, _, _, values_h = self_scores(one_query, one_window, query_ids, window_ids)
        attn_probs, log_total = soft_rows(scores)
        block_out = jnp.einsum(
            "hqk,khe->qhe",
            attn_probs.astype(jnp.bfloat16),
            values_h,
            preferred_element_type=jnp.float32,
        )
        return (block_out.reshape(local_len, head_width), log_total)

    def self_backward(items):
        one_query, one_window, query_ids, window_ids, log_total, grad_out = items
        scores, queries_h, keys_h, values_h = self_scores(
            one_query, one_window, query_ids, window_ids
        )
        attn_probs = jnp.exp(scores - log_total)
        grad_heads = grad_out.reshape(local_len, head_count, -1)
        grad_values = jnp.einsum(
            "hqk,qhe->khe",
            attn_probs.astype(jnp.bfloat16),
            grad_heads,
            preferred_element_type=jnp.float32,
        )
        grad_probs = jnp.einsum(
            "qhe,khe->hqk", grad_heads, values_h, preferred_element_type=jnp.float32
        )
        grad_scores = soft_back(attn_probs, grad_probs)
        grad_line = fold_bias(grad_scores, local_len, window_len)
        grad_low = grad_scores.astype(jnp.bfloat16)
        grad_queries = jnp.einsum(
            "hqk,khe->qhe", grad_low, keys_h, preferred_element_type=jnp.float32
        )
        grad_keys = jnp.einsum(
            "hqk,qhe->khe", grad_low, queries_h, preferred_element_type=jnp.float32
        )
        grad_pair = jnp.concatenate(
            [
                grad_keys.reshape(window_len, head_width),
                grad_values.reshape(window_len, head_width),
            ],
            axis=-1,
        )
        return (grad_queries.reshape(local_len, head_width), grad_pair, grad_line)

    resid_in = tokens.astype(jnp.float32)
    normed_one = (resid_in * rms_scale(resid_in) * norm_self).astype(jnp.bfloat16)
    first_rows = gather_rows(normed_one)
    self_attention_weight = jnp.concatenate([w_query, w_key, w_value], axis=1)
    projected = jnp.einsum(
        "rmh,ha->rma", first_rows, self_attention_weight, preferred_element_type=jnp.float32
    ).astype(jnp.bfloat16)
    queries = projected[..., :head_width]
    key_value = projected[..., head_width:]
    earlier = [from_behind(key_value, CTX, offset) for offset in (2, 1)]
    window = jnp.concatenate(earlier + [key_value], axis=0)
    seq_queries = jnp.moveaxis(queries, 1, 0)
    seq_window = jnp.moveaxis(window, 1, 0)
    self_mixed, self_logs = lax.map(self_forward, (seq_queries, seq_window, seg_query, seg_window))
    attended_rows = jnp.moveaxis(self_mixed, 0, 1).astype(jnp.bfloat16)
    after_self = resid_in + branch_sum(attended_rows, output_weight)
    normed_two = (after_self * rms_scale(after_self) * norm_cross).astype(jnp.bfloat16)
    second_rows = gather_rows(normed_two)
    cross_q = jnp.einsum(
        "rmh,ha->rma", second_rows, cross_query_weight, preferred_element_type=jnp.float32
    ).astype(jnp.bfloat16)
    state_weight = jnp.concatenate([c_key, c_value], axis=1)
    cross_kv = jnp.einsum(
        "rsd,df->rsf", encoder, state_weight, preferred_element_type=jnp.float32
    ).astype(jnp.bfloat16)
    scores, queries_h, keys_h, values_h = cross_scores(cross_q, cross_kv, head_count)
    attn_probs, cross_logs = soft_rows(scores)
    cross_mix = jnp.einsum(
        "shqk,kshe->qshe",
        attn_probs.astype(jnp.bfloat16),
        values_h,
        preferred_element_type=jnp.float32,
    )
    cross_attended = cross_mix.reshape(local_len, seq_count, head_width).astype(jnp.bfloat16)
    after_cross = after_self + branch_sum(cross_attended, cross_output_weight)
    normed_three = (after_cross * rms_scale(after_cross) * norm_ffn).astype(jnp.bfloat16)
    third_rows = gather_rows(normed_three)
    feedforward_weight = jnp.concatenate([w_gate, w_up], axis=1)
    gate_up_product = jnp.einsum(
        "rmh,ha->rma", third_rows, feedforward_weight, preferred_element_type=jnp.float32
    )
    gate_pre = gate_up_product[..., :feed_width]
    up_pre = gate_up_product[..., feed_width:]
    hidden_rows = (jax.nn.gelu(gate_pre, approximate=True) * up_pre).astype(jnp.bfloat16)
    result = after_cross + branch_sum(hidden_rows, down_weight)
    grad_result = cotangent.astype(jnp.float32)
    feedforward_gradient = gather_grads(grad_result.astype(jnp.bfloat16))
    feedforward_down_gradient = jnp.einsum(
        "euy,euh->yh", hidden_rows, feedforward_gradient, preferred_element_type=jnp.float32
    )
    hidden_gradient = jnp.einsum(
        "ezk,ck->ezc", feedforward_gradient, down_weight, preferred_element_type=jnp.float32
    )
    _, feed_pull = jax.vjp(
        lambda gate_in, up_in: jax.nn.gelu(gate_in, approximate=True) * up_in, gate_pre, up_pre
    )
    grad_gate, grad_up = feed_pull(hidden_gradient)
    gate_up_gradient = jnp.concatenate([grad_gate, grad_up], axis=-1).astype(jnp.bfloat16)
    feed_grads = jnp.einsum(
        "zvn,zvp->np", third_rows, gate_up_gradient, preferred_element_type=jnp.float32
    )
    ffn_gate_grad = feed_grads[:, :feed_width]
    ffn_up_grad = feed_grads[:, feed_width:]
    ffn_sums = None
    grad_back_three, gain_three = norm_back(
        after_cross, norm_ffn, input_sum(gate_up_gradient, feedforward_weight)
    )
    grad_mid = grad_result + grad_back_three
    cross_gradient = gather_grads(grad_mid.astype(jnp.bfloat16))
    cross_out_grad = jnp.einsum(
        "euy,euh->yh", cross_attended, cross_gradient, preferred_element_type=jnp.float32
    )
    grad_crossed = jnp.einsum(
        "ezk,ck->ezc", cross_gradient, cross_output_weight, preferred_element_type=jnp.float32
    ).astype(jnp.bfloat16)
    grad_heads = grad_crossed.reshape(local_len, seq_count, head_count, -1)
    cross_probs = jnp.exp(scores - cross_logs)
    grad_cvalues = jnp.einsum(
        "shqk,qshe->kshe",
        cross_probs.astype(jnp.bfloat16),
        grad_heads,
        preferred_element_type=jnp.float32,
    )
    grad_probs = jnp.einsum(
        "qshe,kshe->shqk", grad_heads, values_h, preferred_element_type=jnp.float32
    )
    grad_low = soft_back(cross_probs, grad_probs).astype(jnp.bfloat16)
    cross_query_weight_gradient = jnp.einsum(
        "shqk,kshe->qshe", grad_low, keys_h, preferred_element_type=jnp.float32
    )
    cross_query_weight_gradient = cross_query_weight_gradient.reshape(
        local_len, seq_count, head_width
    ).astype(jnp.bfloat16)
    grad_ckeys = jnp.einsum(
        "shqk,qshe->kshe", grad_low, queries_h, preferred_element_type=jnp.float32
    )
    state_len = encoder.shape[0]
    grad_ckv = jnp.concatenate(
        [
            grad_ckeys.reshape(state_len, seq_count, head_width),
            grad_cvalues.reshape(state_len, seq_count, head_width),
        ],
        axis=-1,
    )
    grad_ckv_own = lax.psum_scatter(
        grad_ckv.astype(jnp.bfloat16), CTX, scatter_dimension=0, tiled=True
    )
    state_rows = grad_ckv_own.shape[0]
    states_own = lax.dynamic_slice_in_dim(encoder, ctx_index * state_rows, state_rows, 0)
    state_grads = jnp.einsum(
        "rsd,rsf->df", states_own, grad_ckv_own, preferred_element_type=jnp.float32
    )
    cross_key_grad = state_grads[:, :head_width]
    cross_value_grad = state_grads[:, head_width:]
    state_term = jnp.einsum(
        "rsf,df->rsd", grad_ckv_own, state_weight, preferred_element_type=jnp.float32
    )
    encoder_grad = lax.psum_scatter(
        state_term.astype(jnp.bfloat16), TP, scatter_dimension=2, tiled=True
    ).astype(jnp.float32)
    cross_query_grad = jnp.einsum(
        "zvn,zvp->np", second_rows, cross_query_weight_gradient, preferred_element_type=jnp.float32
    )
    grad_back_two, gain_two = norm_back(
        after_self, norm_cross, input_sum(cross_query_weight_gradient, cross_query_weight)
    )
    grad_first = grad_mid + grad_back_two
    self_attention_gradient = gather_grads(grad_first.astype(jnp.bfloat16))
    self_out_grad = jnp.einsum(
        "euy,euh->yh", attended_rows, self_attention_gradient, preferred_element_type=jnp.float32
    )
    grad_attended = jnp.einsum(
        "ezk,ck->ezc", self_attention_gradient, output_weight, preferred_element_type=jnp.float32
    ).astype(jnp.bfloat16)
    grad_q, grad_window, grad_lines = lax.map(
        self_backward,
        (
            seq_queries,
            seq_window,
            seg_query,
            seg_window,
            self_logs,
            jnp.moveaxis(grad_attended, 1, 0),
        ),
    )
    table_grad = jnp.einsum(
        "tb,ht->bh",
        one_hot,
        jnp.sum(grad_lines, axis=0),
        precision=lax.Precision.HIGHEST,
        preferred_element_type=jnp.float32,
    )
    grad_window = jnp.moveaxis(grad_window, 0, 1)
    grad_kv = grad_window[2 * local_len :]
    for offset, grad_part in (
        (-2, grad_window[:local_len]),
        (-1, grad_window[local_len : 2 * local_len]),
    ):
        grad_kv = grad_kv + from_behind(grad_part.astype(jnp.bfloat16), CTX, offset).astype(
            grad_part.dtype
        )
    projection_gradient = jnp.concatenate([jnp.moveaxis(grad_q, 0, 1), grad_kv], axis=-1).astype(
        jnp.bfloat16
    )
    self_attention_gradients = jnp.einsum(
        "zvn,zvp->np", first_rows, projection_gradient, preferred_element_type=jnp.float32
    )
    self_query_grad = self_attention_gradients[:, :head_width]
    self_key_grad = self_attention_gradients[:, head_width : 2 * head_width]
    self_value_grad = self_attention_gradients[:, 2 * head_width :]
    grad_back_one, gain_one = norm_back(
        resid_in, norm_self, input_sum(projection_gradient, self_attention_weight)
    )
    tokens_grad = grad_first + grad_back_one
    local_grads = (
        self_query_grad,
        self_key_grad,
        self_value_grad,
        self_out_grad,
        cross_query_grad,
        cross_key_grad,
        cross_value_grad,
        cross_out_grad,
        ffn_gate_grad,
        ffn_up_grad,
        feedforward_down_gradient,
        table_grad,
    )
    return (
        result.astype(jnp.bfloat16),
        tokens_grad,
        encoder_grad,
        (gain_one, gain_two, gain_three),
        local_grads,
        ffn_sums,
    )


def body(
    tokens,
    segments,
    encoder,
    norm_self,
    norm_cross,
    norm_ffn,
    rel_table,
    self_query,
    self_key,
    self_value,
    self_out,
    cross_query,
    cross_key,
    cross_value,
    cross_out,
    ffn_gate,
    ffn_up,
    ffn_down,
    cotangent,
):
    shards = (
        self_query,
        self_key,
        self_value,
        self_out,
        cross_query,
        cross_key,
        cross_value,
        cross_out,
        ffn_gate,
        ffn_up,
        ffn_down,
    )
    per_micro = tokens.shape[1] // MICRO
    results = []
    token_grads = []
    state_grads = []
    gains = None
    totals = None
    for micro in range(MICRO):
        first = micro * per_micro
        out = micro_step(
            tokens[:, first : first + per_micro],
            segments[first : first + per_micro],
            encoder[:, first : first + per_micro],
            cotangent[:, first : first + per_micro],
            norm_self,
            norm_cross,
            norm_ffn,
            rel_table,
            shards,
        )
        results.append(out[0])
        token_grads.append(out[1])
        state_grads.append(out[2])
        gains = out[3] if gains is None else tuple((a + b for a, b in zip(gains, out[3])))
        totals = out[4] if totals is None else tuple((a + b for a, b in zip(totals, out[4])))
    gain_sums = lax.psum(gains, (SHARD, CTX, TP))
    summed = (
        lax.psum_scatter(
            totals[0].astype(jnp.bfloat16), (SHARD, CTX), scatter_dimension=0, tiled=True
        ).astype(jnp.float32),
        lax.psum_scatter(
            totals[1].astype(jnp.bfloat16), (SHARD, CTX), scatter_dimension=0, tiled=True
        ).astype(jnp.float32),
        lax.psum_scatter(
            totals[2].astype(jnp.bfloat16), (SHARD, CTX), scatter_dimension=0, tiled=True
        ).astype(jnp.float32),
        lax.psum_scatter(
            totals[3].astype(jnp.bfloat16), (SHARD, CTX), scatter_dimension=1, tiled=True
        ).astype(jnp.float32),
        lax.psum_scatter(
            totals[4].astype(jnp.bfloat16), (SHARD, CTX), scatter_dimension=0, tiled=True
        ).astype(jnp.float32),
        lax.psum_scatter(
            totals[5].astype(jnp.bfloat16), (SHARD, CTX), scatter_dimension=0, tiled=True
        ).astype(jnp.float32),
        lax.psum_scatter(
            totals[6].astype(jnp.bfloat16), (SHARD, CTX), scatter_dimension=0, tiled=True
        ).astype(jnp.float32),
        lax.psum_scatter(
            totals[7].astype(jnp.bfloat16), (SHARD, CTX), scatter_dimension=1, tiled=True
        ).astype(jnp.float32),
        lax.psum_scatter(
            totals[8].astype(jnp.bfloat16), (SHARD, CTX), scatter_dimension=0, tiled=True
        ).astype(jnp.float32),
        lax.psum_scatter(
            totals[9].astype(jnp.bfloat16), (SHARD, CTX), scatter_dimension=0, tiled=True
        ).astype(jnp.float32),
        lax.psum_scatter(
            totals[10].astype(jnp.bfloat16), (SHARD, CTX), scatter_dimension=1, tiled=True
        ).astype(jnp.float32),
        lax.psum_scatter(
            totals[11].astype(jnp.bfloat16), (SHARD, CTX), scatter_dimension=0, tiled=True
        ).astype(jnp.float32),
    )
    result = jnp.concatenate(results, axis=1)
    tokens_grad = jnp.concatenate(token_grads, axis=1)
    encoder_grad = jnp.concatenate(state_grads, axis=1)
    return (
        result,
        tokens_grad,
        encoder_grad,
        gain_sums[0],
        gain_sums[1],
        gain_sums[2],
        summed[11],
        summed[0],
        summed[1],
        summed[2],
        summed[3],
        summed[4],
        summed[5],
        summed[6],
        summed[7],
        summed[8],
        summed[9],
        summed[10],
    )


def chip_coords(index):
    return (index >> 4, (index >> 3) & 1, (index >> 2) & 1, index & 3)


def move(x, target):
    pairs = []
    for index in range(32):
        sx, core, y, z = target(*chip_coords(index))
        pairs.append((index, sx * 16 + core * 8 + y * 4 + z))
    return lax.ppermute(x, AXES, pairs)


def flip_x(v):
    return move(v, lambda sx, core, y, z: (1 - sx, core, y, z))


def flip_core(v):
    return move(v, lambda sx, core, y, z: (sx, 1 - core, y, z))


def flip_y(v):
    return move(v, lambda sx, core, y, z: (sx, core, 1 - y, z))


def from_z(v, step):
    return move(v, lambda sx, core, y, z: (sx, core, y, (z - step) % 4))


def my_coords():
    shard = lax.axis_index(SHARD)
    return (shard // 2, shard % 2, lax.axis_index(CTX), lax.axis_index(TP))


def swap_blocks(blocks, place):
    sx, core, y, _ = place
    for bit, mask in ((y, 1), (core, 2), (sx, 4)):
        taken = bit == 1
        blocks = [jnp.where(taken, blocks[at ^ mask], blocks[at]) for at in range(8)]
    return blocks


RELATIVE = (0, 1, 4, 5, 2, 3, 6, 7)


def lanes(v):
    width = v.shape[-1] // 8
    return [v[..., at * width : (at + 1) * width] for at in range(8)]


def to_relative(v, place):
    blocks = swap_blocks(lanes(v), place)
    return jnp.concatenate([blocks[at] for at in RELATIVE], axis=-1)


def from_relative(v, place):
    given = lanes(v)
    blocks = [given[RELATIVE.index(at)] for at in range(8)]
    return jnp.concatenate(swap_blocks(blocks, place), axis=-1)


def pick(stack, at):
    return lax.dynamic_index_in_dim(stack, at, 0, keepdims=False)


def send_rows(block, place):
    _, _, _, z = place
    by_seq = jnp.transpose(block, (1, 0, 2))
    return [
        move(
            pick(by_seq, (z + step) % 4),
            lambda sx, core, y, z, step=step: (sx, (z >> 1) ^ y, core, (z + step) % 4),
        )
        for step in range(4)
    ]


def send_back(slots):
    return [
        move(
            slots[step],
            lambda sx, core, y, z, step=step: (
                sx,
                y,
                core ^ (((z - step) % 4) >> 1),
                (z - step) % 4,
            ),
        )
        for step in range(4)
    ]


def place_back(got, place):
    z = place[3]
    stack = jnp.stack(got)
    return jnp.stack([pick(stack, (at - z) % 4) for at in range(4)], axis=1)


def settle(*values):
    return lax.optimization_barrier(values)


WAYS = ((flip_y, flip_x), (flip_x, flip_y))
BITS = (1, 2)


def spread(pieces):
    both = lax.all_gather(jnp.stack(pieces), TP, axis=1)
    return [both[0], both[1]]


def ordered(way, held, near, far, cores):
    if way[0] is flip_y:
        return [held, near, far[0], far[1]] + cores
    return [held, far[0], near, far[1], cores[0], cores[2], cores[1], cores[3]]


def collect(both):
    rows = both.shape[1] // 2
    both = lax.psum_scatter(both, TP, scatter_dimension=0)
    return [both[:rows], both[rows:]]


def fast_layer(
    tokens, segments, encoder, norm_self, norm_cross, norm_ffn, rel_table,
    self_query, self_key, self_value, self_out,
    cross_query, cross_key, cross_value, cross_out,
    ffn_gate, ffn_up, ffn_down, cotangent,
):
    place = my_coords()
    _, core, y, z = place
    spot = jnp.stack(place).astype(jnp.int32)
    core_id = spot[1:2]
    heads = rel_table.shape[1]
    inner = self_query.shape[1]
    feed = ffn_gate.shape[1]
    cut = feed // 4
    rows = tokens.shape[0] * 4
    half = rows // 2
    width = tokens.shape[2]

    def near_of(held):
        return [way[0](h) for way, h in zip(WAYS, held)]

    def far_of(held, near):
        return [[way[1](h), way[1](n)] for way, h, n in zip(WAYS, held, near)]

    def cores_of(values):
        return [flip_core(v) for v in values]

    def far_cores(far):
        return [cores_of(f) for f in far]

    def arrange(held, near, far, core_0, core_1, core_23):
        return [
            ordered(way, h, n, f, [a, b] + c)
            for way, h, n, f, a, b, c in zip(WAYS, held, near, far, core_0, core_1, core_23)
        ]

    pieces_s = [
        jnp.concatenate([self_key.T, self_value.T], axis=0),
        jnp.concatenate([self_query.T, self_out], axis=0),
    ]
    pieces_c = [
        jnp.concatenate([cross_key.T, cross_value.T], axis=0),
        jnp.concatenate([cross_query.T, cross_out], axis=0),
    ]
    gate_t, up_t = ffn_gate.T, ffn_up.T
    pieces_f = [
        [
            jnp.concatenate([w[at : at + cut] for w in (gate_t, up_t, ffn_down)], axis=0)
            for at in (2 * chunk * cut, (2 * chunk + 1) * cut)
        ]
        for chunk in (0, 1)
    ]
    mine = lax.dynamic_index_in_dim(encoder, z, 1, keepdims=False)
    mine_seg = lax.dynamic_index_in_dim(segments, z, 0, keepdims=True)
    pairs = []
    for index in range(32):
        ax, ac, ay, az = chip_coords(index)
        if ac == ay:
            pairs.append((index, ax * 16 + (1 - ac) * 8 + ay * 4 + az))

    held_s = spread(pieces_s)
    held_c = spread(pieces_c)
    held_f1 = spread(pieces_f[0])
    held_f2 = spread(pieces_f[1])
    held_s, rows_out, mine, mine_seg, rel_table = settle(held_s, tokens, mine, mine_seg, rel_table)
    near_s, core_s0 = near_of(held_s), cores_of(held_s)
    came_rows = send_rows(rows_out, place)
    came_enc = lax.ppermute(mine, AXES, pairs)
    came_seg = lax.ppermute(mine_seg, AXES, pairs)
    came_table = [from_z(rel_table, step) for step in (1, 2, 3)]
    near_s, core_s0 = settle(near_s, core_s0)
    far_s, core_s1 = far_of(held_s, near_s), cores_of(near_s)
    far_s, core_s1, held_c, low_cotangent = settle(far_s, core_s1, held_c, cotangent)
    core_s2 = far_cores(far_s)
    near_c, core_c0 = near_of(held_c), cores_of(held_c)
    came_grad = send_rows(low_cotangent, place)
    near_c, core_c0, held_f1 = settle(near_c, core_c0, held_f1)
    far_c, core_c1 = far_of(held_c, near_c), cores_of(near_c)
    near_f1, core_f10 = near_of(held_f1), cores_of(held_f1)
    far_c, core_c1, near_f1, core_f10, came_grad = settle(
        far_c, core_c1, near_f1, core_f10, came_grad
    )
    core_c2 = far_cores(far_c)
    far_f1, core_f11 = far_of(held_f1, near_f1), cores_of(near_f1)
    near_f2, core_f20 = near_of(held_f2), cores_of(held_f2)
    far_f1, core_f11, near_f2, core_f20 = settle(far_f1, core_f11, near_f2, core_f20)
    core_f12 = far_cores(far_f1)
    far_f2, core_f21 = far_of(held_f2, near_f2), cores_of(near_f2)
    far_f2, core_f21 = settle(far_f2, core_f21)
    core_f22 = far_cores(far_f2)

    s_kv, s_qo = arrange(held_s, near_s, far_s, core_s0, core_s1, core_s2)
    c_kv, c_qo = arrange(held_c, near_c, far_c, core_c0, core_c1, core_c2)
    f_one = arrange(held_f1, near_f1, far_f1, core_f10, core_f11, core_f12)
    f_two = arrange(held_f2, near_f2, far_f2, core_f20, core_f21, core_f22)
    w_kv, w_ckv = ([s_kv], 0, 2 * inner), ([c_kv], 0, 2 * inner)
    w_q, w_so = ([s_qo], 0, inner), ([s_qo], inner, inner)
    w_cq, w_co = ([c_qo], 0, inner), ([c_qo], inner, inner)
    w_feed = [[(blocks, at * cut, cut) for at in range(3)] for blocks in (f_one, f_two)]

    resid = gather_rows_call(spot, came_rows)
    own_seq = core == y
    states = to_relative(jnp.where(own_seq, mine, came_enc), place)
    seg = jnp.where(own_seq, mine_seg, came_seg)[0]
    tables = jnp.stack([rel_table] + came_table)
    table = jnp.concatenate([pick(tables, (at - z) % 4) for at in range(4)], axis=1)
    gains = to_relative(jnp.stack([norm_self, norm_cross, norm_ffn]), place)
    gain_self, gain_cross, gain_ffn = gains[0:1], gains[1:2], gains[2:3]

    turn = jnp.arange(2 * half, dtype=jnp.int32)
    signed = jnp.where(turn < half, turn, turn - 2 * half)
    buckets = jnp.arange(table.shape[0], dtype=jnp.int32)

    def hot(distance):
        return (bucket_index(distance)[..., None] == buckets).astype(F32)

    def bias_lines(distance):
        return jnp.dot(
            hot(distance), table, precision=lax.Precision.HIGHEST, preferred_element_type=F32
        ).T

    def kernel_lines(sign):
        near = bias_lines(sign * signed).reshape(-1, 2, 2 * half)
        after = bias_lines(half + sign * signed).reshape(-1, 2, 2 * half)
        far = jnp.broadcast_to(table[-1].reshape(-1, 2, 1), near.shape)
        blank = jnp.zeros((near.shape[0], 2, 2 * half), F32)
        return jnp.concatenate(
            [near[:, 0:1], after[:, 0:1], near[:, 1:2], after[:, 1:2], far, blank], axis=1
        )

    lines = kernel_lines(1)

    quarter = jnp.arange(half, dtype=jnp.int32)
    spots = jnp.concatenate([quarter + half * n for n in (core, 3 - core, 1 - core, 2 + core)])
    seg_spots = jnp.concatenate(
        [
            lax.dynamic_slice_in_dim(seg, half * n, half, 0)
            for n in (core, 3 - core, 1 - core, 2 + core)
        ]
    )

    def mask_of(query_at, key_at, query_seg, key_seg):
        return jnp.where((query_seg == key_seg) & (key_at <= query_at), 0.0, masked_score).astype(F32)

    mask_t = mask_of(spots[None, :rows], spots[:, None], seg_spots[None, :rows], seg_spots[:, None])

    tall = min(256, rows)
    dot = 2 * rows * width

    def full(count, dtype=BF):
        return ((rows, count), dtype)

    gain_out = ((1, width), F32)

    normed_self, kv_own = staged(
        kv_body, [w_kv], [resid], [gain_self],
        [full(width), full(2 * width)], tall, dot * 2 * width,
    )
    kv_far = flip_core(kv_own)
    (queries,) = staged(nt_body, [w_q], [normed_self], [], [full(width)], tall, dot * width)
    mixed, self_logs = self_forward(core_id, queries, kv_own, kv_far, lines, mask_t)
    (cross_kv,) = staged(
        nt_body, [w_ckv], [states], [],
        [((states.shape[0], 2 * width), BF)], states.shape[0], dot * width,
    )
    after_self, normed_cross, cross_q = staged(
        mid_body, [w_so, w_cq], [mixed, resid], [gain_cross],
        [full(width, F32), full(width), full(width)], tall, dot * 2 * width,
    )
    cross_mixed, cross_logs = cross_forward(cross_q, cross_kv)
    after_cross, normed_ffn = staged(
        mid_body, [w_co], [cross_mixed, after_self], [gain_ffn],
        [full(width, F32), full(width)], tall, dot * width,
    )
    grad_low = gather_rows_call(spot, came_grad)
    total, grad_normed = after_cross, []
    feed_sides, feed_over = [], []
    for chunk in (0, 1):
        sides, total, *grad_normed = staged(
            feed_body, w_feed[chunk], [normed_ffn, grad_low, total, *grad_normed], [],
            [((3, rows, 8 * cut), BF), full(width, BF if chunk else F32), full(width, F32)],
            tall, dot * 6 * 8 * cut,
        )
        away = weight_grads(sides, normed_ffn, grad_low, cut, BITS)
        feed_sides.append(sides)
        feed_over.append(cores_of(away))
    result_slots = scatter_rows_call(spot, total)

    def feed_jobs(chunk):
        return weight_grads(feed_sides[chunk], normed_ffn, grad_low, cut, BITS, feed_over[chunk])

    def first_stage(jobs):
        return [way[0](sent) for way, sent in zip(WAYS, jobs[0::2])]

    def second_stage(jobs, came):
        return [way[1](h) for way, h in zip(WAYS, near_sums(jobs[1::2], came))]

    def finish(jobs, came, last, earlier):
        both = far_sums(jobs[1::2], came, last)
        if earlier is not None:
            both, earlier = settle(both, earlier)
        return collect(both), earlier

    grad_mid, low_mid, grad_cross_mixed, gain_three = staged(
        turn_body, [w_co], [after_cross, *grad_normed, grad_low], [gain_ffn],
        [full(width, F32), full(width), full(width), gain_out], tall, dot * width,
    )
    grad_cq, shared = cross_backward(cross_q, cross_kv, grad_cross_mixed, cross_logs)
    own_states = states.shape[0] // 2
    sent = lax.dynamic_slice_in_dim(shared, (1 - core) * own_states, own_states, 0)
    kept = lax.dynamic_slice_in_dim(shared, core * own_states, own_states, 0)
    grad_ckv = kept + flip_core(sent)
    states_own = lax.dynamic_slice_in_dim(states, core * own_states, own_states, 0)
    grad_first, low_first, grad_mixed, gain_two = staged(
        second_turn_body, [w_cq, w_so], [grad_cq, after_self, grad_mid], [gain_cross],
        [full(width, F32), full(width), full(width), gain_out], tall, dot * 2 * width,
    )
    pair_c = (grad_cq, cross_mixed)
    away_c = weight_grads(grad_ckv[None], states_own, states_own, 2 * inner, BITS[:1])
    away_c += weight_grads(pair_c, normed_cross, low_mid, inner, BITS[1:])
    over_c = cores_of(away_c)
    (state_grad,) = staged(
        nn_body, [w_ckv], [grad_ckv], [],
        [((own_states, width), BF)], own_states, dot * width,
    )
    grad_q, kv_kept, kv_sent, sums = self_backward(
        core_id, queries, kv_own, kv_far, grad_mixed, lines, mask_t, self_logs
    )
    grad_kv = kv_kept + flip_core(kv_sent)
    pair_s = (grad_q, mixed)
    away_s = weight_grads(pair_s, normed_self, low_first, inner, BITS[1:])
    away_s = weight_grads(grad_kv[None], normed_self, normed_self, 2 * inner, BITS[:1]) + away_s
    over_s = cores_of(away_s)
    tokens_rows, gain_one = staged(
        last_body, [w_q, w_kv], [grad_q, grad_kv, resid, grad_first], [gain_self],
        [full(width), gain_out], tall, dot * 3 * width,
    )
    token_slots = scatter_rows_call(spot, tokens_rows)

    def cross_jobs():
        first = weight_grads(
            grad_ckv[None], states_own, states_own, 2 * inner, BITS[:1], over_c[:1]
        )
        return first + weight_grads(pair_c, normed_cross, low_mid, inner, BITS[1:], over_c[1:])

    def self_jobs():
        first = weight_grads(
            grad_kv[None], normed_self, normed_self, 2 * inner, BITS[:1], over_s[:1]
        )
        return first + weight_grads(pair_s, normed_self, low_first, inner, BITS[1:], over_s[1:])

    jobs_f1 = feed_jobs(0)
    n1 = first_stage(jobs_f1)
    (n1,) = settle(n1)
    jobs_f2 = feed_jobs(1)
    n2 = second_stage(jobs_f1, n1)
    done_f1, _ = finish(jobs_f1, n1, n2, None)
    n1 = first_stage(jobs_f2)
    n1, result_slots = settle(n1, result_slots)
    jobs_c = cross_jobs()
    n2 = second_stage(jobs_f2, n1)
    back_result = send_back(result_slots)
    done_f2, done_f1 = finish(jobs_f2, n1, n2, done_f1)
    n1 = first_stage(jobs_c)
    (n1,) = settle(n1)
    jobs_s = self_jobs()
    n2 = second_stage(jobs_c, n1)
    done_c, done_f2 = finish(jobs_c, n1, n2, done_f2)
    state_abs = from_relative(state_grad, place)
    state_cols = jnp.stack([state_abs[:, at * inner : (at + 1) * inner] for at in range(4)])
    got = [
        move(
            pick(state_cols, (z + step) % 4),
            lambda sx, core, y, z, step=step: (sx, y, core, (z + step) % 4),
        )
        for step in range(4)
    ]
    n1 = first_stage(jobs_s)
    (n1,) = settle(n1)
    back_tokens = send_back(token_slots)
    n2 = second_stage(jobs_s, n1)
    sum_s = far_sums(jobs_s[1::2], n1, n2)

    inside = (signed[None, :] - jnp.arange(8, dtype=jnp.int32)[:, None]) % (2 * half)
    inside = jnp.where(inside < half, inside, inside - 2 * half)
    kinds = jnp.stack(
        [inside, half + inside, (3 - 2 * core) * half + inside, jnp.full_like(inside, 2 * half)]
    )
    sums = sums.reshape(4 * heads, 4, 8, 2 * half)
    table_grad = jnp.einsum(
        "ndmb,hndm->bh",
        hot(kinds),
        sums,
        precision=lax.Precision.HIGHEST,
        preferred_element_type=F32,
    )
    by_z = table_grad.reshape(-1, 4, heads)
    gain_parts = from_relative(jnp.concatenate([gain_one, gain_two, gain_three]), place)
    small = jnp.concatenate([gain_parts.reshape(-1), by_z.reshape(-1)]).reshape(-1, 128)
    sum_s, small, done_c = settle(sum_s, small, done_c)
    done_s = collect(sum_s)
    for flip in (
        flip_core,
        flip_x,
        flip_y,
        lambda v: move(v, lambda sx, core, y, z: (sx, core, y, z ^ 1)),
        lambda v: move(v, lambda sx, core, y, z: (sx, core, y, z ^ 2)),
    ):
        small = small + flip(small)
    small = small.reshape(-1)
    gain_sums = small[: gain_parts.size].reshape(gain_parts.shape)
    table_sum = small[gain_parts.size :].reshape(by_z.shape)
    block = lax.axis_index(SHARD) * 2 + y
    own_table = lax.dynamic_slice_in_dim(
        lax.dynamic_index_in_dim(table_sum, z, 1, keepdims=False), block * 4, 4, 0
    )
    result = place_back(back_result, place)
    tokens_grad = place_back(back_tokens, place).astype(F32)
    got = jnp.stack(got)
    encoder_grad = jnp.stack([pick(got, (z - at) % 4) for at in range(4)], axis=1).astype(F32)
    done_f1, done_f2, done_c, done_s = (
        [v.astype(F32) for v in done] for done in (done_f1, done_f2, done_c, done_s)
    )
    feed_done = [*done_f1, *done_f2]
    gate_grad, up_grad, down_grad = (
        jnp.concatenate([done[at * cut : (at + 1) * cut] for done in feed_done], axis=0)
        for at in range(3)
    )
    (kv_done, qo_done), (ckv_done, cqo_done) = done_s, done_c
    return (
        result,
        tokens_grad,
        encoder_grad,
        gain_sums[0],
        gain_sums[1],
        gain_sums[2],
        own_table,
        qo_done[:inner].T,
        kv_done[:inner].T,
        kv_done[inner:].T,
        qo_done[inner:],
        cqo_done[:inner].T,
        ckv_done[:inner].T,
        ckv_done[inner:].T,
        cqo_done[inner:],
        gate_grad.T,
        up_grad.T,
        down_grad,
    )


def fast_body(*args):
    return fast_layer(*args)


def solution(mesh):
    placed = (
        P((CTX, TP), SHARD, None),
        P(SHARD, None),
        P(None, SHARD, None),
        P(),
        P(),
        P(),
        P(None, TP),
        P((SHARD, CTX), TP),
        P((SHARD, CTX), TP),
        P((SHARD, CTX), TP),
        P(TP, (SHARD, CTX)),
        P((SHARD, CTX), TP),
        P((SHARD, CTX), TP),
        P((SHARD, CTX), TP),
        P(TP, (SHARD, CTX)),
        P((SHARD, CTX), TP),
        P((SHARD, CTX), TP),
        P(TP, (SHARD, CTX)),
        P((CTX, TP), SHARD, None),
    )
    fits = tuple(mesh.shape[axis] for axis in AXES) == (4, 2, 4)
    return jax.shard_map(
        fast_body if fits else body,
        mesh=mesh,
        in_specs=placed,
        out_specs=(
            P((CTX, TP), SHARD, None),
            P((CTX, TP), SHARD, None),
            P(CTX, SHARD, TP),
            P(),
            P(),
            P(),
            P((SHARD, CTX), TP),
            P((SHARD, CTX), TP),
            P((SHARD, CTX), TP),
            P((SHARD, CTX), TP),
            P(TP, (SHARD, CTX)),
            P((SHARD, CTX), TP),
            P((SHARD, CTX), TP),
            P((SHARD, CTX), TP),
            P(TP, (SHARD, CTX)),
            P((SHARD, CTX), TP),
            P((SHARD, CTX), TP),
            P(TP, (SHARD, CTX)),
        ),
        check_vma=False,
    )
```
